256 devices in a mesh: lon: 16 (over x_lo, y, core), lat: 16 (over z, x_hi).
Axes of the slice: x: 4 (x_hi: 2, x_lo: 2; x = x_hi * 2 + x_lo), y: 4, z: 8, core: 2. Of those that a mesh axis runs over, the one named last changes fastest.
Arguments:
- state: bfloat16 [256, 256, 2048], P(None, 'lat', 'lon'), may hold values from -6 to 6
- land: int32 [256, 2048], P('lat', 'lon'), may hold values 0 or 1
- depth_kernel: bfloat16 [256, 49], replicated, may hold values from -0.875 to 0.875
- norm_gain: float32 [256], replicated, may hold values from 0.1 to 1.9
- expand_weight: bfloat16 [256, 1024], replicated, may hold values from -0.375 to 0.375
- reduce_weight: bfloat16 [1024, 256], replicated, may hold values from -0.1875 to 0.1875
- layer_scale: float32 [256], replicated, may hold values from 0.1 to 1.9
- cotangent: bfloat16 [256, 256, 2048], P(None, 'lat', 'lon'), may hold values from -6 to 6
Outputs:
- updated: bfloat16 [256, 256, 2048], P(None, 'lat', 'lon')
- state_grad: bfloat16 [256, 256, 2048], P(None, 'lat', 'lon')
- kernel_grad: float32 [256, 49], replicated
- gain_grad: float32 [256], replicated
- expand_grad: float32 [256, 1024], replicated
- reduce_grad: float32 [1024, 256], replicated
- scale_grad: float32 [256], replicated
The draws below stay inside these ranges and needn't reach their ends.
Inputs may be any that keep to these rules, and one draw needn't show every extreme that they name: 1 marks sea, 0 land.
All inputs are finite; a program needn't handle non-finite values. No bound on the sum of `land` on one device may be relied on, other than what follows from the above.
Results may differ from the reference program's by a relative error of at most 0.0062.
Values may be sent and summed in bfloat16 or wider, within the bound.
A program may use at most 128 MiB of HBM per device.

```python
import jax
import jax.numpy as jnp
from jax import lax

C = 256
FF = 1024
HL = 16
NLAT = 256
NLON = 2048


def with_ends(entries, stream_key, smallest, largest):
    place = [jax.random.randint(jax.random.fold_in(stream_key, axis), (), 0, length) for axis, length in enumerate(entries.shape)]
    main_axis = entries.shape.index(max(entries.shape))
    neighbour = place[:main_axis] + [(place[main_axis] + 1) % entries.shape[main_axis]] + place[main_axis + 1:]
    return entries.at[tuple(place)].set(smallest).at[tuple(neighbour)].set(largest)


def steps_of(stream_key, shape, pieces, low, largest):
    def one(axis_at, shards_of):
        heights = jax.random.uniform(jax.random.fold_in(jax.random.fold_in(stream_key, 6), axis_at), (shards_of,), jnp.float32, low / len(pieces), largest / len(pieces))
        return jnp.repeat(jnp.exp(heights), shape[axis_at] // shards_of).reshape((-1,) + (1,) * (len(shape) - axis_at - 1))

    loudness = one(*pieces[0])
    for cut in pieces[1:]:
        loudness = loudness * one(*cut)
    return loudness


def scatter_about(key, extent, scale, reach, shards=(), held_as=jnp.bfloat16):
    level = steps_of(key, extent, shards, -0.22, 0.18) if shards else 1.0
    drawn = jax.random.normal(key, extent, jnp.float32) * scale * level
    return jnp.minimum(jnp.maximum(drawn, -reach), reach).astype(held_as)


def setup_inputs(seed: int = 0) -> dict:
    key_list = jax.random.split(jax.random.key(seed), 9)
    return {
        "state": scatter_about(key_list[0], (C, NLAT, NLON), 1.0, 6.0, ((1, 16), (2, 16))),
        "land": with_ends((jax.random.randint(key_list[1], (NLAT, NLON), 0, 4) < 3).astype(jnp.int32), jax.random.fold_in(key_list[1], 1), 0, 1),
        "depth_kernel": scatter_about(key_list[2], (C, 49), 49 ** -0.5, 0.875),
        "norm_gain": jnp.clip(1.0 + 0.18 * jax.random.normal(key_list[3], (C,), jnp.float32), 0.1, 1.9),
        "expand_weight": scatter_about(key_list[4], (C, FF), C ** -0.5, 0.375),
        "reduce_weight": scatter_about(key_list[5], (FF, C), FF ** -0.5, 0.1875),
        "layer_scale": jnp.clip(1.0 + 0.18 * jax.random.normal(key_list[6], (C,), jnp.float32), 0.1, 1.9),
        "cotangent": scatter_about(key_list[7], (C, NLAT, NLON), 1.0, 6.0, ((1, 16), (2, 16))),
    }


epsilon = 1e-06

def extend(source):
    fold_rows = source[:, ::-1, ::-1][:, :3, :]
    south = jnp.zeros_like(source[:, :3, :])
    stacked = jnp.concatenate([south, source, fold_rows], 1)
    return jnp.concatenate([stacked[:, :, -3:], stacked, stacked[:, :, :3]], 2)

def depthwise(padded, kernel, height, breadth):
    running = jnp.zeros((padded.shape[0], height, breadth), jnp.float32)
    for tap_index in range(49):
        row_off = tap_index // 7
        col_off = tap_index % 7
        window = padded[:, row_off:row_off + height, col_off:col_off + breadth].astype(jnp.float32)
        running = running + window * kernel[:, tap_index][:, None, None]
    return running

def gelu_slope(value):
    return 0.5 * (1.0 + jax.scipy.special.erf(value * 0.7071067811865476)) + value * jnp.exp(-0.5 * value * value) * 0.3989422804014327

def reference(state, land, depth_kernel, norm_gain, expand_weight, reduce_weight, layer_scale, cotangent):
    kernel = depth_kernel.astype(jnp.float32)
    groups = C // 8

    def conv_group(member):
        return depthwise(extend(member[0]), member[1], NLAT, NLON)
    filtered = lax.map(conv_group, (state.reshape(groups, 8, NLAT, NLON), kernel.reshape(groups, 8, 49)))
    filtered = filtered.reshape(C, NLAT, NLON)
    blocks = NLAT // HL

    def to_blocks(array):
        return array.reshape(array.shape[0], blocks, HL * NLON).transpose(1, 0, 2)
    sea_blocks = land.astype(jnp.float32).reshape(blocks, 1, HL * NLON)

    def block_step(totals, member):
        filt_block, state_block, sea_mask, cot_block = member
        masked = sea_mask * filt_block
        average = lax.optimization_barrier(jnp.mean(masked, 0, keepdims=True))
        centred = masked - average
        inverse = lax.rsqrt(lax.optimization_barrier(jnp.mean(centred * centred, 0, keepdims=True)) + epsilon)
        unit = centred * inverse
        normed = (unit * norm_gain[:, None]).astype(jnp.bfloat16)
        hidden = jnp.dot(expand_weight.T, normed, preferred_element_type=jnp.float32)
        activated = jax.nn.gelu(hidden, approximate=False).astype(jnp.bfloat16)
        branch = jnp.dot(reduce_weight.T, activated, preferred_element_type=jnp.float32)
        out_block = (state_block.astype(jnp.float32) + sea_mask * layer_scale[:, None] * branch).astype(jnp.bfloat16)
        cot_f = cot_block.astype(jnp.float32)
        scaled = (sea_mask * layer_scale[:, None] * cot_f).astype(jnp.bfloat16)
        grad_scale = lax.optimization_barrier(jnp.sum(sea_mask * cot_f * branch, 1))
        grad_reduce = jnp.dot(activated, scaled.T, preferred_element_type=jnp.float32)
        grad_act = jnp.dot(reduce_weight, scaled, preferred_element_type=jnp.float32)
        grad_hidden = (grad_act * gelu_slope(hidden)).astype(jnp.bfloat16)
        grad_expand = jnp.dot(normed, grad_hidden.T, preferred_element_type=jnp.float32)
        grad_norm = jnp.dot(expand_weight, grad_hidden, preferred_element_type=jnp.float32)
        grad_gain = lax.optimization_barrier(jnp.sum(grad_norm * unit, 1))
        grad_hat = grad_norm * norm_gain[:, None]
        grad_masked = inverse * (grad_hat - lax.optimization_barrier(jnp.mean(grad_hat, 0, keepdims=True)) - unit * lax.optimization_barrier(jnp.mean(grad_hat * unit, 0, keepdims=True)))
        grad_filt = sea_mask * grad_masked
        totals = (totals[0] + grad_expand, totals[1] + grad_reduce, totals[2] + grad_gain, totals[3] + grad_scale)
        return (totals, (out_block, grad_filt))
    start = (jnp.zeros((C, FF), jnp.float32), jnp.zeros((FF, C), jnp.float32), jnp.zeros((C,), jnp.float32), jnp.zeros((C,), jnp.float32))
    totals, (out_blocks, grad_blocks) = lax.scan(block_step, start, (to_blocks(filtered), to_blocks(state), sea_blocks, to_blocks(cotangent)))

    def from_blocks(array):
        return array.transpose(1, 0, 2).reshape(array.shape[1], NLAT, NLON)
    updated = from_blocks(out_blocks)
    grad_filtered = from_blocks(grad_blocks)

    def back_group(member):
        source, gradient, kern = member
        padded = extend(source).astype(jnp.float32)
        zeroed = jnp.pad(gradient, ((0, 0), (6, 6), (6, 6)))
        grad_pad = jnp.zeros((source.shape[0], NLAT + 6, NLON + 6), jnp.float32)
        tap_sums = []
        for tap_index in range(49):
            row_off = tap_index // 7
            col_off = tap_index % 7
            tap_sums.append(lax.optimization_barrier(jnp.sum(gradient * padded[:, row_off:row_off + NLAT, col_off:col_off + NLON], (1, 2))))
            grad_pad = grad_pad + zeroed[:, 6 - row_off:12 - row_off + NLAT, 6 - col_off:12 - col_off + NLON] * kern[:, tap_index][:, None, None]
        unused, pullback = jax.vjp(extend, source.astype(jnp.float32))
        return (jnp.stack(tap_sums, 1), pullback(grad_pad)[0])
    kernel_sums, grad_source = lax.map(back_group, (state.reshape(groups, 8, NLAT, NLON), grad_filtered.reshape(groups, 8, NLAT, NLON), kernel.reshape(groups, 8, 49)))
    kernel_sums = kernel_sums.reshape(C, 49)
    grad_source = grad_source.reshape(C, NLAT, NLON)
    state_grad = (cotangent.astype(jnp.float32) + grad_source).astype(jnp.bfloat16)
    factor = float(NLAT * NLON) ** (-0.5)
    return (updated, state_grad, kernel_sums * factor, totals[2] * factor, totals[0] * factor, totals[1] * factor, totals[3] * factor)
```

```python
import functools

import jax
import jax.numpy as jnp
from jax import lax
from jax.experimental import pallas as pl
from jax.experimental.pallas import tpu as pltpu
from jax.sharding import PartitionSpec as P

epsilon = 1e-06
MESH = pl.DeviceIdType.MESH


def swapped(value, axis, stride):
    mask = 2**stride
    pairs = [(source, source ^ mask) for source in range(lax.axis_size(axis))]
    return lax.ppermute(value, axis, pairs)


def with_halo(value, sides, width, wrap):
    for axis, dim in sides:
        count, length = (lax.axis_size(axis), value.shape[dim])
        up = [(i, (i + 1) % count) for i in range(count if wrap else count - 1)]
        down = [(j, i) for i, j in up]
        last = lax.slice_in_dim(value, length - width, length, axis=dim)
        leading = lax.slice_in_dim(value, 0, width, axis=dim)
        before = lax.ppermute(last, axis, up)
        after = lax.ppermute(leading, axis, down)
        value = jnp.concatenate([before, value, after], axis=dim)
    return value


def fold_forward(top_strip):
    bit_count = lax.axis_size("lon").bit_length() - 1
    for bit_index in range(bit_count):
        top_strip = swapped(top_strip, "lon", bit_index)
    return top_strip


def fold_backward(top_strip):
    bit_count = lax.axis_size("lon").bit_length() - 1
    for bit_index in range(bit_count):
        top_strip = swapped(top_strip.astype(jnp.bfloat16), "lon", bit_index).astype(
            top_strip.dtype
        )
    return top_strip


def extend(source, at_top):
    height = source.shape[1]
    stacked = with_halo(source, (("lat", 1),), 3, False)
    top_strip = source[:, height - 3 :, :][:, ::-1, ::-1]
    folded = fold_forward(top_strip)
    upper_rows = jnp.where(at_top, folded, stacked[:, height + 3 :, :])
    stacked = jnp.concatenate([stacked[:, : height + 3, :], upper_rows], 1)
    return with_halo(stacked, (("lon", 2),), 3, True)


def retract(gradient, at_top):
    height = gradient.shape[1] - 6
    breadth = gradient.shape[2] - 6
    edge_cols = jnp.concatenate([gradient[:, :, :3], gradient[:, :, breadth + 3 :]], 2)
    arrived = with_halo(edge_cols.astype(jnp.bfloat16), (("lon", 2),), 3, True).astype(
        edge_cols.dtype
    )
    centre = gradient[:, :, 3 : breadth + 3]
    centre = (
        centre.at[:, :, :3].add(arrived[:, :, :3]).at[:, :, breadth - 3 :].add(arrived[:, :, 9:])
    )
    returned = fold_backward(centre[:, height + 3 :, :][:, ::-1, ::-1])
    centre = centre.at[:, height : height + 3, :].add(jnp.where(at_top, returned, 0.0))
    edge_rows = jnp.concatenate([centre[:, :3, :], centre[:, height + 3 :, :]], 1)
    arrived = with_halo(edge_rows.astype(jnp.bfloat16), (("lat", 1),), 3, False).astype(
        edge_rows.dtype
    )
    inner = centre[:, 3 : height + 3, :]
    return inner.at[:, :3, :].add(arrived[:, :3, :]).at[:, height - 3 :, :].add(arrived[:, 9:, :])


def gelu_slope(value):
    return (
        0.5 * (1.0 + jax.scipy.special.erf(value * 0.7071067811865476))
        + value * jnp.exp(-0.5 * value * value) * 0.3989422804014327
    )


def device_at(core, y, x, z, ny):
    return {"lon": (x % 2) * (2 * ny) + y * 2 + core, "lat": z * 2 + x // 2}


def my_place(ny):
    lon, lat = lax.axis_index("lon"), lax.axis_index("lat")
    return lon % 2, (lon // 2) % ny, (lat % 2) * 2 + lon // (2 * ny), lat // 2


def neighbours_of(place, sizes, axis):
    out = []
    for d in range(1, sizes[axis]):
        other = list(place)
        other[axis] = (place[axis] + d) % sizes[axis]
        out.append(tuple(other))
    return out


def sum_kernel(sizes, big_ref, small_ref, big_out, small_out, *scratch):
    stages = len(sizes)
    ny = sizes[1]
    place = my_place(ny)
    got, held = scratch[:stages], scratch[stages : 2 * stages]
    got_small, held_small = scratch[2 * stages : 3 * stages], scratch[3 * stages : 4 * stages]
    full = scratch[4 * stages : 5 * stages - 1]
    sems = scratch[5 * stages - 1 :]
    send, recv, send_small, recv_small, send_back, recv_back = sems

    barrier = pltpu.get_barrier_semaphore()
    partners = 0
    for axis in range(stages):
        for other in neighbours_of(place, sizes, axis):
            pl.semaphore_signal(barrier, inc=1, device_id=device_at(*other, ny), device_id_type=MESH)
            partners += 1
    pl.semaphore_wait(barrier, partners)

    current, current_small = big_ref, small_ref
    base = 0
    for axis in range(stages):
        n = sizes[axis]
        mine = place[axis]
        tiles = current.shape[0] // n
        copies = []
        for d, other in enumerate(neighbours_of(place, sizes, axis)):
            target = device_at(*other, ny)
            copies.append(
                pltpu.make_async_remote_copy(
                    src_ref=current.at[pl.ds(other[axis] * tiles, tiles)],
                    dst_ref=got[axis].at[d],
                    send_sem=send.at[base + d],
                    recv_sem=recv.at[base + d],
                    device_id=target,
                    device_id_type=MESH,
                )
            )
            copies.append(
                pltpu.make_async_remote_copy(
                    src_ref=current_small,
                    dst_ref=got_small[axis].at[d],
                    send_sem=send_small.at[base + d],
                    recv_sem=recv_small.at[base + d],
                    device_id=target,
                    device_id_type=MESH,
                )
            )
        for copy in copies:
            copy.start()
        for copy in copies:
            copy.wait()
        group = min(8, tiles)

        def add_up(i, carry, n=n, mine=mine, tiles=tiles, current=current, axis=axis, group=group):
            total = current[pl.ds(mine * tiles + i * group, group)].astype(jnp.float32)
            for d in range(n - 1):
                total = total + got[axis][d, pl.ds(i * group, group)].astype(jnp.float32)
            held[axis][pl.ds(i * group, group)] = total.astype(jnp.bfloat16)
            return carry

        lax.fori_loop(0, tiles // group, add_up, 0)
        total = current_small[...]
        for d in range(n - 1):
            total = total + got_small[axis][d]
        if axis == stages - 1:
            small_out[...] = total
        else:
            held_small[axis][...] = total
        current, current_small = held[axis], held_small[axis]
        base += n - 1
    for axis in range(stages - 1, -1, -1):
        n = sizes[axis]
        base -= n - 1
        mine = place[axis]
        tiles = current.shape[0]
        target_ref = big_out if axis == 0 else full[axis - 1]
        copies = []
        for d, other in enumerate(neighbours_of(place, sizes, axis)):
            copies.append(
                pltpu.make_async_remote_copy(
                    src_ref=current,
                    dst_ref=target_ref.at[pl.ds(mine * tiles, tiles)],
                    send_sem=send_back.at[base + d],
                    recv_sem=recv_back.at[base + d],
                    device_id=device_at(*other, ny),
                    device_id_type=MESH,
                )
            )
        for copy in copies:
            copy.start()
        group = min(8, tiles)

        def keep(i, carry, mine=mine, tiles=tiles, current=current, target_ref=target_ref, group=group):
            target_ref[pl.ds(mine * tiles + i * group, group)] = current[pl.ds(i * group, group)]
            return carry

        lax.fori_loop(0, tiles // group, keep, 0)
        for copy in copies:
            copy.wait()
        current = target_ref


def sum_over_devices(big, small):
    ny, nz = lax.axis_size("lon") // 4, lax.axis_size("lat") // 2
    sizes = (2, ny, 4, nz)
    stages = len(sizes)
    tile, lines = big.shape[1:], small.shape
    got, held, full = [], [], []
    count = big.shape[0]
    for n in sizes:
        count //= n
        got.append(pltpu.VMEM((n - 1, count) + tile, jnp.bfloat16))
        held.append(pltpu.VMEM((count,) + tile, jnp.bfloat16))
    count = big.shape[0]
    for n in sizes[:-1]:
        count //= n
        full.append(pltpu.VMEM((count,) + tile, jnp.bfloat16))
    links = sum(n - 1 for n in sizes)
    return pl.pallas_call(
        functools.partial(sum_kernel, sizes),
        out_shape=(
            jax.ShapeDtypeStruct(big.shape, jnp.bfloat16),
            jax.ShapeDtypeStruct(small.shape, jnp.float32),
        ),
        in_specs=[pl.BlockSpec(memory_space=pltpu.VMEM)] * 2,
        out_specs=[pl.BlockSpec(memory_space=pltpu.VMEM)] * 2,
        scratch_shapes=got
        + held
        + [pltpu.VMEM((n - 1,) + lines, jnp.float32) for n in sizes]
        + [pltpu.VMEM(lines, jnp.float32) for n in sizes]
        + full
        + [pltpu.SemaphoreType.DMA((links,)) for _ in range(6)],
        compiler_params=pltpu.CompilerParams(collective_id=0, has_side_effects=True),
        name="sum_over_devices",
    )(big, small)


def local(
    state, land, depth_kernel, norm_gain, expand_weight, reduce_weight, layer_scale, cotangent
):
    channels, height, breadth = state.shape
    cells = height * breadth
    at_top = lax.axis_index("lat") == lax.axis_size("lat") - 1
    kernel = depth_kernel.astype(jnp.float32)
    padded = extend(state, at_top)
    filtered = jnp.zeros((channels, height, breadth), jnp.float32)
    for tap_index in range(49):
        row_off = tap_index // 7
        col_off = tap_index % 7
        window = padded[:, row_off : row_off + height, col_off : col_off + breadth].astype(
            jnp.float32
        )
        filtered = filtered + window * kernel[:, tap_index][:, None, None]
    sea_mask = land.astype(jnp.float32).reshape(1, cells)
    masked = sea_mask * filtered.reshape(channels, cells)
    average = jnp.mean(masked, 0, keepdims=True)
    centred = masked - average
    inverse = lax.rsqrt(jnp.mean(centred * centred, 0, keepdims=True) + epsilon)
    unit = centred * inverse
    normed = (unit * norm_gain[:, None]).astype(jnp.bfloat16)
    hidden = jnp.einsum("cf,cn->fn", expand_weight, normed, preferred_element_type=jnp.float32)
    activated = jax.nn.gelu(hidden, approximate=False).astype(jnp.bfloat16)
    branch = jnp.einsum("fc,fn->cn", reduce_weight, activated, preferred_element_type=jnp.float32)
    state_flat = state.reshape(channels, cells).astype(jnp.float32)
    updated = (state_flat + sea_mask * layer_scale[:, None] * branch).astype(jnp.bfloat16)
    cot_flat = cotangent.reshape(channels, cells).astype(jnp.float32)
    scaled = (sea_mask * layer_scale[:, None] * cot_flat).astype(jnp.bfloat16)
    grad_scale = jnp.sum(sea_mask * cot_flat * branch, 1)
    grad_reduce = jnp.einsum("fn,cn->fc", activated, scaled, preferred_element_type=jnp.float32)
    grad_act = jnp.einsum("fc,cn->fn", reduce_weight, scaled, preferred_element_type=jnp.float32)
    grad_hidden = (grad_act * gelu_slope(hidden)).astype(jnp.bfloat16)
    grad_expand = jnp.einsum("cn,fn->cf", normed, grad_hidden, preferred_element_type=jnp.float32)
    grad_norm = jnp.einsum(
        "cf,fn->cn", expand_weight, grad_hidden, preferred_element_type=jnp.float32
    )
    grad_gain = jnp.sum(grad_norm * unit, 1)
    grad_hat = grad_norm * norm_gain[:, None]
    grad_masked = inverse * (
        grad_hat
        - jnp.mean(grad_hat, 0, keepdims=True)
        - unit * jnp.mean(grad_hat * unit, 0, keepdims=True)
    )
    grad_filt = (sea_mask * grad_masked).reshape(channels, height, breadth)
    zeroed = jnp.pad(grad_filt, ((0, 0), (6, 6), (6, 6)))
    grad_pad = jnp.zeros((channels, height + 6, breadth + 6), jnp.float32)
    tap_sums = []
    for tap_index in range(49):
        row_off = tap_index // 7
        col_off = tap_index % 7
        window = padded[:, row_off : row_off + height, col_off : col_off + breadth].astype(
            jnp.float32
        )
        tap_sums.append(jnp.sum(grad_filt * window, (1, 2)))
        grad_pad = (
            grad_pad
            + zeroed[:, 6 - row_off : 12 - row_off + height, 6 - col_off : 12 - col_off + breadth]
            * kernel[:, tap_index][:, None, None]
        )
    grad_kernel = jnp.stack(tap_sums, 1)
    grad_source = retract(grad_pad, at_top)
    state_grad = (cotangent.astype(jnp.float32) + grad_source).astype(jnp.bfloat16)
    big = jnp.concatenate([grad_expand.T, grad_reduce], 0).astype(jnp.bfloat16)
    rows = big.shape[0]
    big = big.reshape(rows // 16, 16, 2, 128).transpose(0, 2, 1, 3).reshape(rows // 8, 16, 128)
    small = jnp.concatenate([grad_kernel, grad_gain[:, None], grad_scale[:, None]], 1).T
    small = jnp.pad(small, ((0, 5), (0, 0)))
    big, small = sum_over_devices(big, small)
    big = big.reshape(rows // 16, 2, 16, 128).transpose(0, 2, 1, 3).reshape(rows, 256)
    big = big.astype(jnp.float32)
    summed = (small[:49].T, small[49], big[: rows // 2].T, big[rows // 2 :], small[50])
    factor = float(height * lax.axis_size("lat") * breadth * lax.axis_size("lon")) ** (-0.5)
    return (
        updated.reshape(channels, height, breadth),
        state_grad,
        summed[0] * factor,
        summed[1] * factor,
        summed[2] * factor,
        summed[3] * factor,
        summed[4] * factor,
    )


def solution(mesh):
    return jax.shard_map(
        local,
        mesh=mesh,
        in_specs=(
            P(None, "lat", "lon"),
            P("lat", "lon"),
            P(),
            P(),
            P(),
            P(),
            P(),
            P(None, "lat", "lon"),
        ),
        out_specs=(P(None, "lat", "lon"), P(None, "lat", "lon"), P(), P(), P(), P(), P()),
        check_vma=False,
    )
```

```python
import functools

import jax
import jax.numpy as jnp
import numpy as np
from jax import lax
from jax.experimental import pallas as pl
from jax.experimental.pallas import tpu as pltpu
from jax.sharding import PartitionSpec as P

epsilon = 1e-06
MESH = pl.DeviceIdType.MESH
BF16 = jnp.bfloat16
F32 = jnp.float32
C, FF, ROWS, LANES = 256, 1024, 16, 128
BLOCK_ROWS = 4
BLOCK = BLOCK_ROWS * LANES
UNROLL_PAIRS = 16
GROUPS = C // 16


def tap_tables():
    table = np.full((3, 2, ROWS, 256), -1, np.int32)
    for variant in range(3):
        for r in range(ROWS):
            for b in range(7):
                for i in range(16):
                    a = i + 3 - r
                    if 0 <= a <= 6:
                        tap = a * 7 + b
                        tap = 48 - tap if variant else tap
                        table[variant, 0, r, b * 16 + i] = tap
                        table[variant, 1, r, b * 16 + i] = tap + 64
                for h in range(2):
                    for j in range(6):
                        p = j if j < 3 else 16 + j
                        a = p - r
                        if 0 <= a <= 6:
                            tap = a * 7 + b
                            turned = variant == 1 or (variant == 2 and j < 3)
                            tap = 48 - tap if turned else tap
                            table[variant, 0, r, 128 + b * 16 + 8 * h + j] = tap + 64 * h
    return table


def edge_picker():
    pick = np.zeros((96, 256), np.float32)
    for j in range(3):
        for c in range(16):
            pick[j * 16 + c, c * 16 + j] = 1
            pick[48 + j * 16 + c, c * 16 + 13 + j] = 1
    return pick


def halo_placer():
    place = np.zeros((2, 128, 96), np.float32)
    for c in range(16):
        for j in range(3):
            row = (c // 2) * 16 + (c % 2) * 8
            place[:, row + j, j * 16 + c] = 1
            place[0, row + 3 + j, 48 + j * 16 + c] = 1
            place[1, row + 3 + j, 48 + (2 - j) * 16 + c] = 1
    return place


def column_picker():
    pick = np.zeros((8, 128), np.float32)
    for j in range(3):
        pick[j, j] = 1
        pick[3 + j, 125 + j] = 1
    return pick


def column_placer():
    place = np.zeros((16, 128), np.float32)
    for j in range(3):
        place[3 + j, 125 + j] = 1
        place[8 + j, j] = 1
    return place


def lane_orders():
    return np.stack([np.eye(128), np.eye(128)[::-1]]).astype(np.float32)


def tap_gather():
    gather = np.zeros((3, 64, 128), np.float32)
    for a in range(7):
        for b in range(7):
            gather[0, a * 7 + b, b * 16 + a + 12] = 1
            for h in range(2):
                lane = b * 16 + 8 * h + a + (15 if a < 3 else -1)
                if a != 3:
                    gather[1 + h, a * 7 + b, lane] = 1
    return gather


def valid_mask():
    mask = np.zeros((3, ROWS, 128), np.float32)
    for r in range(ROWS):
        for b in range(7):
            for i in range(16):
                if 0 <= i + 3 - r <= 6:
                    mask[0, 15 - r, b * 16 + i] = 1
            for h in range(2):
                for j in range(6):
                    p = j if j < 3 else 16 + j
                    if 0 <= p - r <= 6:
                        mask[1 + h, 15 - r, b * 16 + 8 * h + j] = 1
    return mask


def dot(a, b):
    return jnp.dot(a, b, preferred_element_type=F32)


def dot_lanes(a, b, precision=None):
    return lax.dot_general(a, b, (((1,), (1,)), ((), ())), preferred_element_type=F32, precision=precision)


def dot_first(a, b):
    return lax.dot_general(a, b, (((0,), (0,)), ((), ())), preferred_element_type=F32)


def shifted(tile, edge, lane):
    windows = []
    for b in range(7):
        if b == 3:
            windows.append(tile)
            continue
        mask = lane >= 125 + b if b < 3 else lane < b - 3
        windows.append(pltpu.roll(jnp.where(mask, edge, tile), (3 - b) % LANES, 1))
    return jnp.concatenate(windows, 0)


def halves(hidden):
    bell = jnp.exp(hidden * hidden * -0.5)
    t = pl.reciprocal(1.0 + 0.23164190 * jnp.abs(hidden), approx=False)
    poly = t * (0.127414796 + t * (-0.142248368 + t * (0.7107068705 + t * (-0.7265760135 + t * 0.5307027145))))
    tail = poly * bell
    return jnp.where(hidden >= 0.0, 1.0 - tail, tail), bell


def device_at(core, y, x, z, ny):
    return {"lon": (x % 2) * (2 * ny) + y * 2 + core, "lat": z * 2 + x // 2}


def my_place(ny):
    lon, lat = lax.axis_index("lon"), lax.axis_index("lat")
    return lon % 2, (lon // 2) % ny, (lat % 2) * 2 + lon // (2 * ny), lat // 2


def neighbours_of(place, sizes, axis):
    out = []
    for d in range(1, sizes[axis]):
        other = list(place)
        other[axis] = (place[axis] + d) % sizes[axis]
        out.append(tuple(other))
    return out


class Halo:
    def __init__(self, field, tables, packed, rows_in, cols, cols_in, corner, corner_in, edge, halo, halo_edge, sems):
        self.field, self.tables = field, tables
        self.packed, self.rows_in = packed, rows_in
        self.cols, self.cols_in, self.corner, self.corner_in = cols, cols_in, corner, corner_in
        self.edge, self.halo, self.halo_edge = edge, halo, halo_edge
        self.send, self.recv = sems
        lon, lat = lax.axis_index("lon"), lax.axis_index("lat")
        nlon, nlat = lax.axis_size("lon"), lax.axis_size("lat")
        self.at_top, self.lat = lat == nlat - 1, lat
        self.up = {"lon": jnp.where(self.at_top, nlon - 1 - lon, lon), "lat": jnp.minimum(lat + 1, nlat - 1)}
        self.down = {"lon": lon, "lat": jnp.maximum(lat - 1, 0)}
        self.left = {"lon": (lon + nlon - 1) % nlon, "lat": lat}
        self.right = {"lon": (lon + 1) % nlon, "lat": lat}

    def copy(self, src, dst, sem, to):
        return pltpu.make_async_remote_copy(
            src_ref=src, dst_ref=dst, send_sem=self.send.at[sem[0]], recv_sem=self.recv.at[sem[1]], device_id=to,
            device_id_type=MESH,
        )

    def start(self):
        pick, col_pick = self.tables["edge_picker"], self.tables["column_picker"]

        def pack(g, carry):
            rows = self.field[pl.ds(g * 16, 16)].reshape(256, LANES)
            edges = dot(pick[...], rows).astype(BF16)
            self.packed[0, g] = edges[:48]
            self.packed[1, g] = edges[48:]
            lanes = pl.ds(pl.multiple_of(g * 256, 256), 256)
            self.cols[:, lanes] = dot_lanes(col_pick[...], rows).astype(BF16)
            return carry

        lax.fori_loop(0, GROUPS, pack, 0)
        below = jnp.where(self.at_top, 1, 0)
        self.to_up = self.copy(self.packed.at[1], self.rows_in.at[below], (0, below), self.up)
        self.to_up.start()
        self.to_down = self.copy(self.packed.at[0], self.rows_in.at[1], (1, 1), self.down)

        @pl.when(self.lat > 0)
        def _():
            self.to_down.start()

        self.to_left = self.copy(self.cols, self.cols_in.at[1], (2, 2), self.left)
        self.to_right = self.copy(self.cols, self.cols_in.at[0], (3, 3), self.right)
        self.to_left.start()
        self.to_right.start()

    def columns(self):
        self.to_left.wait()
        self.to_right.wait()
        place = self.tables["column_placer"]

        def put(g, carry):
            lanes = pl.ds(pl.multiple_of(g * 256, 256), 256)
            both = jnp.concatenate([self.cols_in[0, :, lanes], self.cols_in[1, :, lanes]], 0)
            self.edge[pl.ds(g * 16, 16)] = dot_first(both, place[...]).astype(BF16).reshape(16, ROWS, LANES)
            return carry

        lax.fori_loop(0, GROUPS, put, 0)

    def rows(self):
        self.to_up.wait_send()
        order = self.tables["lane_orders"]
        col_pick = self.tables["column_picker"]
        turn = jnp.where(self.at_top, 1, 0)

        @pl.when(self.lat > 0)
        def _():
            self.to_down.wait_send()
            self.copy(self.packed.at[1], self.rows_in.at[0], (0, 0), self.up).wait_recv()

        @pl.when(self.lat == 0)
        def _():
            self.rows_in[0] = jnp.zeros_like(self.rows_in[0])

        self.copy(self.packed.at[0], self.rows_in.at[1], (1, 1), self.down).wait_recv()

        def put(g, carry):
            upper = self.rows_in[0, g]
            lower = dot(self.rows_in[1, g], order[turn]).astype(BF16)
            both = jnp.concatenate([upper, lower], 0)
            self.halo[pl.ds(g * 8, 8)] = (
                dot(self.tables["halo_placer"][turn], both).astype(BF16).reshape(8, ROWS, LANES)
            )
            tiles = self.halo[pl.ds(g * 8, 8)].reshape(128, LANES)
            lanes = pl.ds(pl.multiple_of(g * 128, 128), 128)
            self.corner[:, lanes] = dot_lanes(col_pick[...], tiles).astype(BF16)
            return carry

        lax.fori_loop(0, GROUPS, put, 0)
        self.on_left = self.copy(self.corner, self.corner_in.at[1], (4, 4), self.left)
        self.on_right = self.copy(self.corner, self.corner_in.at[0], (5, 5), self.right)
        self.on_left.start()
        self.on_right.start()

    def corners(self):
        self.on_left.wait()
        self.on_right.wait()
        place = self.tables["column_placer"]

        def put(g, carry):
            lanes = pl.ds(pl.multiple_of(g * 128, 128), 128)
            both = jnp.concatenate([self.corner_in[0, :, lanes], self.corner_in[1, :, lanes]], 0)
            self.halo_edge[pl.ds(g * 8, 8)] = dot_first(both, place[...]).astype(BF16).reshape(8, ROWS, LANES)
            return carry

        lax.fori_loop(0, GROUPS, put, 0)


def halo_scratch():
    return [
        pltpu.VMEM((2, GROUPS, 48, LANES), BF16),
        pltpu.VMEM((2, GROUPS, 48, LANES), BF16),
        pltpu.VMEM((8, C * ROWS), BF16),
        pltpu.VMEM((2, 8, C * ROWS), BF16),
        pltpu.VMEM((8, C * 8), BF16),
        pltpu.VMEM((2, 8, C * 8), BF16),
        pltpu.VMEM((C, ROWS, LANES), BF16),
        pltpu.VMEM((C // 2, ROWS, LANES), BF16),
        pltpu.VMEM((C // 2, ROWS, LANES), BF16),
    ]


def build_row_matrices(variant, taps, table, wide, out):
    tap_index = lax.broadcasted_iota(jnp.int32, (LANES, 256), 0)

    def per_row(r, carry):
        first = table[variant, 0, pl.ds(r, 1), :]
        second = table[variant, 1, pl.ds(r, 1), :]
        chosen = jnp.where((tap_index == first) | (tap_index == second), 1.0, 0.0).astype(BF16)
        both = dot(taps[...], chosen)
        wide[0, pl.ds(r, C, stride=ROWS), :] = both[:, :LANES]
        wide[1, pl.ds(r, C, stride=ROWS), :] = both[:, LANES:]
        return carry

    lax.fori_loop(0, ROWS, per_row, 0)

    def per_group(g, carry):
        rows = pl.ds(pl.multiple_of(g * 256, 256), 256)
        for h in range(2):
            half = wide[h, rows, :].astype(BF16).reshape(16, ROWS, LANES)
            out[pl.ds(g * 16, 16), :, h * LANES : (h + 1) * LANES] = half
        return carry

    lax.fori_loop(0, GROUPS, per_group, 0)


def convolve(part, field, edge, halo, halo_edge, matrices, emit):
    lane = lax.broadcasted_iota(jnp.int32, (ROWS, LANES), 1)

    def step(i, carry):
        for u in range(UNROLL_PAIRS):
            q = i * UNROLL_PAIRS + u
            beyond = shifted(halo[q], halo_edge[q], lane)
            both = matrices[pl.ds(2 * q, 2)].reshape(2 * ROWS, 256)
            outer = dot(both[:, 128:240], beyond)
            for k in range(2):
                c = 2 * q + k
                own = shifted(field[c], edge[c], lane)
                inner = dot(both[k * ROWS : (k + 1) * ROWS, :112], own)
                emit(c, inner + outer[k * ROWS : (k + 1) * ROWS])
        return carry

    steps = C // 2 // UNROLL_PAIRS // 4
    lax.fori_loop(part * steps, (part + 1) * steps, step, 0)


def kernel_sums(part, grad, field, edge, halo, halo_edge, mask, inner_sums, outer_sums):
    lane = lax.broadcasted_iota(jnp.int32, (ROWS, LANES), 1)
    pad = jnp.zeros((LANES - 112, LANES), BF16)

    def in_line(product, which):
        kept = jnp.where(mask[which] > 0.0, product, 0.0)
        upper = pltpu.roll(kept[:8], 0, 1, stride=1, stride_axis=0)
        lower = pltpu.roll(kept[8:], 8, 1, stride=1, stride_axis=0)
        return jnp.sum(upper + lower, 0, keepdims=True)

    def step(i, carry):
        for u in range(UNROLL_PAIRS):
            q = i * UNROLL_PAIRS + u
            beyond = jnp.concatenate([shifted(halo[q], halo_edge[q], lane), pad], 0)
            both = grad[pl.ds(2 * q, 2)].reshape(2 * ROWS, LANES)
            outer = dot_lanes(both, beyond)
            for k in range(2):
                c = 2 * q + k
                own = jnp.concatenate([shifted(field[c], edge[c], lane), pad], 0)
                inner = dot_lanes(both[k * ROWS : (k + 1) * ROWS], own)
                inner_sums[pl.ds(c, 1), :] = in_line(inner, 0)
                outer_sums[k, pl.ds(q, 1), :] = in_line(outer[k * ROWS : (k + 1) * ROWS], 1 + k)
        return carry

    steps = C // 2 // UNROLL_PAIRS // 4
    lax.fori_loop(part * steps, (part + 1) * steps, step, 0)


class Sum:
    def __init__(self, sizes, stages, first, last, got, held, full, sems):
        self.sizes, self.ny, self.stages = sizes, sizes[1], stages
        self.place = my_place(self.ny)
        self.first, self.last, self.got, self.held, self.full = first, last, got, held, full
        self.send, self.recv, self.send_back, self.recv_back = sems
        self.base = [sum(sizes[axis] - 1 for axis, _ in stages[:i]) for i in range(len(stages))]
        self.backs = [i for i, (_, shared) in enumerate(stages) if shared]

    def others(self, axis):
        return enumerate(neighbours_of(self.place, self.sizes, axis))

    def source(self, stage):
        return self.first if stage == 0 else self.held[stage - 1]

    def start(self, stage):
        axis, shared = self.stages[stage]
        source = self.source(stage)
        tiles = self.held[stage].shape[0]
        self.copies = []
        for d, other in self.others(axis):
            self.copies.append(
                pltpu.make_async_remote_copy(
                    src_ref=source.at[pl.ds(other[axis] * tiles, tiles)] if shared else source,
                    dst_ref=self.got[stage].at[d],
                    send_sem=self.send.at[self.base[stage] + d],
                    recv_sem=self.recv.at[self.base[stage] + d],
                    device_id=device_at(*other, self.ny),
                    device_id_type=MESH,
                )
            )
        for copy in self.copies:
            copy.start()

    def finish(self, stage):
        for copy in self.copies:
            copy.wait()
        axis, shared = self.stages[stage]
        source, got, held = self.source(stage), self.got[stage], self.held[stage]
        tiles = held.shape[0]
        mine = self.place[axis] * tiles if shared else 0
        group = min(8, tiles)

        def add_up(i, carry):
            total = source[pl.ds(mine + i * group, group)].astype(F32)
            for d in range(self.sizes[axis] - 1):
                total = total + got[d, pl.ds(i * group, group)].astype(F32)
            held[pl.ds(i * group, group)] = total.astype(held.dtype)
            return carry

        lax.fori_loop(0, tiles // group, add_up, 0)

    def start_back(self, i):
        stage = self.backs[i]
        axis, _ = self.stages[stage]
        source = self.held[-1] if i == len(self.backs) - 1 else self.full[i]
        target = self.last if i == 0 else self.full[i - 1]
        tiles = source.shape[0]
        mine = self.place[axis] * tiles
        self.copies = []
        for d, other in self.others(axis):
            self.copies.append(
                pltpu.make_async_remote_copy(
                    src_ref=source,
                    dst_ref=target.at[pl.ds(mine, tiles)],
                    send_sem=self.send_back.at[self.base[stage] + d],
                    recv_sem=self.recv_back.at[self.base[stage] + d],
                    device_id=device_at(*other, self.ny),
                    device_id_type=MESH,
                )
            )
        for copy in self.copies:
            copy.start()
        group = min(8, tiles)

        def keep(i, carry):
            target[pl.ds(mine + i * group, group)] = source[pl.ds(i * group, group)]
            return carry

        lax.fori_loop(0, tiles // group, keep, 0)

    def finish_back(self, i):
        for copy in self.copies:
            copy.wait()


BIG_STAGES = ((0, True), (1, True), (2, True), (3, True))
SMALL_STAGES = ((0, True), (3, True), (1, False), (2, False))


def sum_scratch(sizes, stages, count, tile, dtype):
    got, held, full = [], [], []
    rest = count
    for axis, shared in stages:
        rest = rest // sizes[axis] if shared else rest
        got.append(pltpu.VMEM((sizes[axis] - 1, rest) + tile, dtype))
        held.append(pltpu.VMEM((rest,) + tile, dtype))
        if shared:
            full.append(pltpu.VMEM((rest,) + tile, dtype))
    return [pltpu.VMEM((count,) + tile, dtype), pltpu.VMEM((count,) + tile, dtype)] + got + held + full[:-1]


def sum_sems(sizes):
    return [pltpu.SemaphoreType.DMA((sum(n - 1 for n in sizes),)) for _ in range(4)]


TABLES = ("tap_table", "edge_picker", "halo_placer", "column_picker", "column_placer", "lane_orders", "tap_gather", "valid_mask")


def make_tables():
    return (
        jnp.asarray(tap_tables()),
        jnp.asarray(edge_picker(), BF16),
        jnp.asarray(halo_placer(), BF16),
        jnp.asarray(column_picker(), BF16),
        jnp.asarray(column_placer(), BF16),
        jnp.asarray(lane_orders(), BF16),
        jnp.asarray(tap_gather(), F32),
        jnp.asarray(valid_mask(), F32),
    )


def mlp_block(rb, land, gain, scale, w1, w1t, w2, w2t, filt, cot, s):
    first = rb * BLOCK_ROWS
    for j in range(BLOCK_ROWS):
        rows = pl.ds(pl.multiple_of((first + j) * C, C), C)
        sea = land[pl.ds(first + j, 1), :]
        lanes = slice(j * LANES, (j + 1) * LANES)
        masked = sea * filt[rows, :]
        average = jnp.sum(masked, 0, keepdims=True) * (1.0 / C)
        centred = masked - average
        inverse = lax.rsqrt(jnp.sum(centred * centred, 0, keepdims=True) * (1.0 / C) + epsilon)
        unit = centred * inverse
        s["inverse"][pl.ds(j, 1), :] = inverse
        s["unit"][j] = unit
        s["normed"][:, lanes] = (unit * gain[...]).astype(BF16)
        s["scaled"][:, lanes] = (sea * scale[...] * cot[rows, :]).astype(BF16)
    for f in range(4):
        part = slice(f * 256, (f + 1) * 256)
        s["hidden"][f % 2] = dot(w1t[part, :], s["normed"][...])
        s["grad_act"][f % 2] = dot(w2[part, :], s["scaled"][...])
        for t in range(16):
            hidden = s["hidden"][f % 2, t * 16 : (t + 1) * 16, :]
            grad_act = s["grad_act"][f % 2, t * 16 : (t + 1) * 16, :]
            lower, bell = halves(hidden)
            rows = slice(f * 256 + t * 16, f * 256 + (t + 1) * 16)
            s["activated"][rows, :] = (hidden * lower).astype(BF16)
            s["grad_hidden"][rows, :] = (grad_act * (lower + hidden * bell * 0.3989422804014327)).astype(BF16)
    s["branch"][...] = dot(w2t[...], s["activated"][...])
    s["grad_norm"][...] = dot(w1[...], s["grad_hidden"][...])
    s["reduce_sum"][...] += dot_lanes(s["activated"][...], s["scaled"][...])
    s["expand_sum"][...] += dot_lanes(s["normed"][...], s["grad_hidden"][...])
    for j in range(BLOCK_ROWS):
        rows = pl.ds(pl.multiple_of((first + j) * C, C), C)
        sea = land[pl.ds(first + j, 1), :]
        lanes = slice(j * LANES, (j + 1) * LANES)
        branch = sea * s["branch"][:, lanes]
        grad_norm = s["grad_norm"][:, lanes]
        unit = s["unit"][j]
        s["added"][pl.ds(first + j, C, stride=ROWS), :] = scale[...] * branch
        s["scale_sum"][...] += cot[rows, :] * branch
        s["gain_sum"][...] += grad_norm * unit
        grad_hat = grad_norm * gain[...]
        mean = jnp.sum(grad_hat, 0, keepdims=True) * (1.0 / C)
        mean_unit = jnp.sum(grad_hat * unit, 0, keepdims=True) * (1.0 / C)
        grad = (sea * s["inverse"][pl.ds(j, 1), :]) * (grad_hat - mean - unit * mean_unit)
        s["grad_wide"][0, pl.ds(first + j, C, stride=ROWS), :] = grad
        s["grad_wide"][1, pl.ds(ROWS - 1 - first - j, C, stride=ROWS), :] = grad


COMPUTE = {
    "wide": ((2, C * ROWS, LANES), F32),
    "matrices": ((C, ROWS, 256), BF16),
    "back_matrices": ((C, ROWS, 256), BF16),
    "filt": ((C * ROWS, LANES), F32),
    "cot": ((C * ROWS, LANES), F32),
    "inverse": ((8, LANES), F32),
    "unit": ((BLOCK_ROWS, C, LANES), F32),
    "normed": ((C, BLOCK), BF16),
    "scaled": ((C, BLOCK), BF16),
    "hidden": ((2, 256, BLOCK), F32),
    "grad_act": ((2, 256, BLOCK), F32),
    "activated": ((FF, BLOCK), BF16),
    "grad_hidden": ((FF, BLOCK), BF16),
    "branch": ((C, BLOCK), F32),
    "grad_norm": ((C, BLOCK), F32),
    "reduce_sum": ((FF, C), F32),
    "expand_sum": ((C, FF), F32),
    "added": ((C * ROWS, LANES), F32),
    "grad_wide": ((2, C * ROWS, LANES), F32),
    "grad": ((C, ROWS, LANES), BF16),
    "turned_grad": ((C, ROWS, LANES), BF16),
    "scale_sum": ((C, LANES), F32),
    "gain_sum": ((C, LANES), F32),
    "inner_sums": ((C, LANES), F32),
    "outer_sums": ((2, C // 2, LANES), F32),
}


def block_kernel(
    sizes, state, land, taps, gain, scale, w1, w1t, w2, w2t, cotangent, *rest
):
    tables = dict(zip(TABLES, rest[: len(TABLES)]))
    rest = list(rest[len(TABLES) :])
    updated, state_grad, expand_out, reduce_out, small_out = rest[:5]
    rest = rest[5:]

    def take(n):
        out = rest[:n]
        del rest[:n]
        return out

    s = dict(zip(COMPUTE, take(len(COMPUTE))))
    ahead_refs = take(len(halo_scratch()))
    back_refs = take(len(halo_scratch()))
    ahead = Halo(state, tables, *ahead_refs, sems=take(2))
    back = Halo(s["grad"], tables, *back_refs, sems=take(2))
    stages = len(sizes)
    big_first, big_last = take(2)
    big = Sum(sizes, BIG_STAGES, big_first, big_last, take(stages), take(stages), take(3), take(4))
    small_first, small_last = take(2)
    small = Sum(sizes, SMALL_STAGES, small_first, small_last, take(stages), take(stages), take(1), take(4))

    barrier = pltpu.get_barrier_semaphore()
    greeted = [ahead.up, ahead.left, ahead.right]
    for axis in range(stages):
        greeted += [device_at(*other, sizes[1]) for _, other in big.others(axis)]
    for device in greeted:
        pl.semaphore_signal(barrier, inc=1, device_id=device, device_id_type=MESH)

    @pl.when(ahead.lat > 0)
    def _():
        pl.semaphore_signal(barrier, inc=1, device_id=ahead.down, device_id_type=MESH)

    pl.semaphore_wait(barrier, len(greeted) + jnp.where(ahead.lat > 0, 1, 0))

    ahead.start()
    build_row_matrices(0, taps, tables["tap_table"], s["wide"], s["matrices"])
    build_row_matrices(
        jnp.where(ahead.at_top, 2, 1), taps, tables["tap_table"], s["wide"], s["back_matrices"]
    )

    def turn(i, carry):
        for u in range(16):
            c = i * 16 + u
            s["cot"][pl.ds(c, ROWS, stride=C), :] = cotangent[c].astype(F32)
        return carry

    lax.fori_loop(0, C // 16, turn, 0)
    s["reduce_sum"][...] = jnp.zeros_like(s["reduce_sum"])
    s["expand_sum"][...] = jnp.zeros_like(s["expand_sum"])
    s["scale_sum"][...] = jnp.zeros_like(s["scale_sum"])
    s["gain_sum"][...] = jnp.zeros_like(s["gain_sum"])
    ahead.columns()
    ahead.rows()
    ahead.corners()

    def put_filtered(c, value):
        s["filt"][pl.ds(c, ROWS, stride=C), :] = value

    for part in range(4):
        convolve(part, state, ahead.edge, ahead.halo, ahead.halo_edge, s["matrices"], put_filtered)

    def block(rb, carry):
        mlp_block(rb, land, gain, scale, w1, w1t, w2, w2t, s["filt"], s["cot"], s)
        return carry

    lax.fori_loop(0, ROWS // BLOCK_ROWS, block, 0)

    def settle(g, carry):
        rows = pl.ds(pl.multiple_of(g * 128, 128), 128)
        channels = pl.ds(g * 8, 8)
        s["grad"][channels] = s["grad_wide"][0, rows, :].astype(BF16).reshape(8, ROWS, LANES)
        s["turned_grad"][channels] = s["grad_wide"][1, rows, :].astype(BF16).reshape(8, ROWS, LANES)
        updated[channels] = (
            (state[channels].reshape(128, LANES).astype(F32) + s["added"][rows, :]).astype(BF16).reshape(8, ROWS, LANES)
        )
        return carry

    lax.fori_loop(0, C // 8, settle, 0)
    back.start()

    def cut_expand(g, carry):
        rows = pl.ds(pl.multiple_of(g * 16, 16), 16)
        for h in range(8):
            big_first[g * 8 + h] = s["expand_sum"][rows, h * LANES : (h + 1) * LANES].astype(BF16)
        return carry

    lax.fori_loop(0, C // 16, cut_expand, 0)

    def cut_reduce(g, carry):
        rows = pl.ds(pl.multiple_of(g * 16, 16), 16)
        for h in range(2):
            big_first[128 + g * 2 + h] = s["reduce_sum"][rows, h * LANES : (h + 1) * LANES].astype(BF16)
        return carry

    lax.fori_loop(0, FF // 16, cut_reduce, 0)
    big.start(0)

    def sums(part):
        kernel_sums(
            part, s["turned_grad"], state, ahead.edge, ahead.halo, ahead.halo_edge, tables["valid_mask"], s["inner_sums"],
            s["outer_sums"],
        )

    def put_grad(c, value):
        state_grad[c] = (cotangent[c].astype(F32) + value).astype(BF16)

    def convolve_back(part):
        convolve(part, s["grad"], back.edge, back.halo, back.halo_edge, s["back_matrices"], put_grad)

    sums(0)
    big.finish(0)
    big.start(1)
    sums(1)
    sums(2)
    back.columns()
    back.rows()
    sums(3)
    big.finish(1)
    big.start(2)

    exact = lax.Precision.HIGHEST
    gather = tables["tap_gather"]
    even_odd = lax.broadcasted_iota(jnp.int32, (C // 2, C), 0)
    channel = lax.broadcasted_iota(jnp.int32, (C // 2, C), 1)
    total = dot_lanes(gather[0], s["inner_sums"][...], exact)
    for h in range(2):
        part = dot_lanes(gather[1 + h], s["outer_sums"][h], exact)
        spread = jnp.where(channel == 2 * even_odd + h, 1.0, 0.0)
        total = total + jnp.dot(part, spread, preferred_element_type=F32, precision=exact)
    row = lax.broadcasted_iota(jnp.int32, (64, LANES), 0)
    total = total + dot_lanes(jnp.where(row == 49, 1.0, 0.0), s["gain_sum"][...], exact)
    total = total + dot_lanes(jnp.where(row == 50, 1.0, 0.0), s["scale_sum"][...], exact)
    for g in range(8):
        for h in range(2):
            small_first[g * 2 + h] = total[g * 8 : (g + 1) * 8, h * LANES : (h + 1) * LANES]
    small.start(0)
    back.corners()
    convolve_back(0)
    small.finish(0)
    small.start(1)
    big.finish(2)
    big.start(3)
    convolve_back(1)
    small.finish(1)
    small.start(2)
    convolve_back(2)
    big.finish(3)
    big.start_back(3)
    small.finish(2)
    small.start(3)
    convolve_back(3)
    big.finish_back(3)
    big.start_back(2)
    small.finish(3)
    small.start_back(1)
    big.finish_back(2)
    big.start_back(1)
    small.finish_back(1)
    small.start_back(0)
    big.finish_back(1)
    big.start_back(0)
    small.finish_back(0)
    big.finish_back(0)

    def paste_expand(g, carry):
        rows = pl.ds(pl.multiple_of(g * 16, 16), 16)
        for h in range(8):
            expand_out[rows, h * LANES : (h + 1) * LANES] = big_last[g * 8 + h].astype(F32)
        return carry

    lax.fori_loop(0, C // 16, paste_expand, 0)

    def paste_reduce(g, carry):
        rows = pl.ds(pl.multiple_of(g * 16, 16), 16)
        for h in range(2):
            reduce_out[rows, h * LANES : (h + 1) * LANES] = big_last[128 + g * 2 + h].astype(F32)
        return carry

    lax.fori_loop(0, FF // 16, paste_reduce, 0)
    for g in range(8):
        for h in range(2):
            small_out[g * 8 : (g + 1) * 8, h * LANES : (h + 1) * LANES] = small_last[g * 2 + h]


def local(state, land, depth_kernel, norm_gain, expand_weight, reduce_weight, layer_scale, cotangent):
    ny, nz = lax.axis_size("lon") // 4, lax.axis_size("lat") // 2
    sizes = (2, ny, 4, nz)
    parity = (jnp.arange(C) % 2 == 1)[:, None]
    low = jnp.pad(depth_kernel, ((0, 0), (0, LANES - 49)))
    high = jnp.pad(depth_kernel, ((0, 0), (64, LANES - 64 - 49)))
    taps = jnp.where(parity, high, low)
    wide = lambda vector: jnp.broadcast_to(vector[:, None], (C, LANES))
    operands = (
        state, land.astype(F32), taps, wide(norm_gain), wide(layer_scale), expand_weight, expand_weight.T, reduce_weight,
        reduce_weight.T, cotangent, *make_tables(),
    )
    vmem = pl.BlockSpec(memory_space=pltpu.VMEM)
    out_shape = (
        jax.ShapeDtypeStruct((C, ROWS, LANES), BF16),
        jax.ShapeDtypeStruct((C, ROWS, LANES), BF16),
        jax.ShapeDtypeStruct((C, FF), F32),
        jax.ShapeDtypeStruct((FF, C), F32),
        jax.ShapeDtypeStruct((64, C), F32),
    )
    halo_sems = [pltpu.SemaphoreType.DMA((6,)) for _ in range(4)]
    updated, state_grad, expand_grad, reduce_grad, small = pl.pallas_call(
        functools.partial(block_kernel, sizes),
        out_shape=out_shape,
        in_specs=[vmem] * len(operands),
        out_specs=[vmem] * len(out_shape),
        scratch_shapes=[pltpu.VMEM(shape, dtype) for shape, dtype in COMPUTE.values()]
        + halo_scratch()
        + halo_scratch()
        + halo_sems
        + sum_scratch(sizes, BIG_STAGES, 256, (16, LANES), BF16)
        + sum_sems(sizes)
        + sum_scratch(sizes, SMALL_STAGES, 16, (8, LANES), F32)
        + sum_sems(sizes),
        compiler_params=pltpu.CompilerParams(
            collective_id=0, has_side_effects=True, vmem_limit_bytes=63 * 2**20
        ),
        name="convnext_block",
    )(*operands)
    factor = float(ROWS * lax.axis_size("lat") * LANES * lax.axis_size("lon")) ** (-0.5)
    return (
        updated,
        state_grad,
        small[:49].T * factor,
        small[49] * factor,
        expand_grad * factor,
        reduce_grad * factor,
        small[50] * factor,
    )


def solution(mesh):
    grid = P(None, "lat", "lon")
    return jax.shard_map(
        local,
        mesh=mesh,
        in_specs=(grid, P("lat", "lon"), P(), P(), P(), P(), P(), grid),
        out_specs=(grid, grid, P(), P(), P(), P(), P()),
        check_vma=False,
    )
```

```python
import functools

import jax
import jax.numpy as jnp
import numpy as np
from jax import lax
from jax.experimental import pallas as pl
from jax.experimental.pallas import tpu as pltpu
from jax.sharding import PartitionSpec as P

epsilon = 1e-06
MESH = pl.DeviceIdType.MESH
BF16 = jnp.bfloat16
F32 = jnp.float32
C, FF, ROWS, LANES = 256, 1024, 16, 128
BLOCK_ROWS = 4
BLOCK = BLOCK_ROWS * LANES
UNROLL_PAIRS = 16
GROUPS = C // 16


def tap_tables():
    table = np.full((3, 2, ROWS, 256), -1, np.int32)
    for variant in range(3):
        for r in range(ROWS):
            for b in range(7):
                for i in range(16):
                    a = i + 3 - r
                    if 0 <= a <= 6:
                        tap = a * 7 + b
                        tap = 48 - tap if variant else tap
                        table[variant, 0, r, b * 16 + i] = tap
                        table[variant, 1, r, b * 16 + i] = tap + 64
                for h in range(2):
                    for j in range(6):
                        p = j if j < 3 else 16 + j
                        a = p - r
                        if 0 <= a <= 6:
                            tap = a * 7 + b
                            turned = variant == 1 or (variant == 2 and j < 3)
                            tap = 48 - tap if turned else tap
                            table[variant, 0, r, 128 + b * 16 + 8 * h + j] = tap + 64 * h
    return table


def edge_picker():
    pick = np.zeros((LANES, 256), np.float32)
    for j in range(3):
        for c in range(16):
            pick[j * 16 + c, c * 16 + j] = 1
            pick[64 + j * 16 + c, c * 16 + 13 + j] = 1
    return pick


def halo_placer():
    place = np.zeros((2, 128, 96), np.float32)
    for c in range(16):
        for j in range(3):
            row = (c // 2) * 16 + (c % 2) * 8
            place[:, row + j, j * 16 + c] = 1
            place[0, row + 3 + j, 48 + j * 16 + c] = 1
            place[1, row + 3 + j, 48 + (2 - j) * 16 + c] = 1
    return place


def column_picker():
    pick = np.zeros((8, 128), np.float32)
    for j in range(3):
        pick[j, j] = 1
        pick[3 + j, 125 + j] = 1
    return pick


def column_placer():
    place = np.zeros((16, 128), np.float32)
    for j in range(3):
        place[3 + j, 125 + j] = 1
        place[8 + j, j] = 1
    return place


def lane_orders():
    return np.stack([np.eye(128), np.eye(128)[::-1]]).astype(np.float32)


def tap_gather():
    gather = np.zeros((3, 64, 128), np.float32)
    for a in range(7):
        for b in range(7):
            gather[0, a * 7 + b, b * 16 + a + 12] = 1
            for h in range(2):
                lane = b * 16 + 8 * h + a + (15 if a < 3 else -1)
                if a != 3:
                    gather[1 + h, a * 7 + b, lane] = 1
    return gather


def valid_mask():
    mask = np.zeros((3, ROWS, 128), np.float32)
    for r in range(ROWS):
        for b in range(7):
            for i in range(16):
                if 0 <= i + 3 - r <= 6:
                    mask[0, 15 - r, b * 16 + i] = 1
            for h in range(2):
                for j in range(6):
                    p = j if j < 3 else 16 + j
                    if 0 <= p - r <= 6:
                        mask[1 + h, 15 - r, b * 16 + 8 * h + j] = 1
    return mask


def dot(a, b):
    return jnp.dot(a, b, preferred_element_type=F32)


def dot_lanes(a, b, precision=None):
    return lax.dot_general(a, b, (((1,), (1,)), ((), ())), preferred_element_type=F32, precision=precision)


def dot_first(a, b):
    return lax.dot_general(a, b, (((0,), (0,)), ((), ())), preferred_element_type=F32)


def shifted(tile, edge, lane):
    windows = []
    for b in range(7):
        if b == 3:
            windows.append(tile)
            continue
        mask = lane >= 125 + b if b < 3 else lane < b - 3
        windows.append(pltpu.roll(jnp.where(mask, edge, tile), (3 - b) % LANES, 1))
    return jnp.concatenate(windows, 0)


def halves(hidden):
    bell = jnp.exp(hidden * hidden * -0.5)
    t = pl.reciprocal(1.0 + 0.23164190 * jnp.abs(hidden), approx=False)
    poly = t * (0.127414796 + t * (-0.142248368 + t * (0.7107068705 + t * (-0.7265760135 + t * 0.5307027145))))
    tail = poly * bell
    return jnp.where(hidden >= 0.0, 1.0 - tail, tail), bell


def device_at(core, y, x, z, ny):
    return {"lon": (x % 2) * (2 * ny) + y * 2 + core, "lat": z * 2 + x // 2}


def my_place(ny):
    lon, lat = lax.axis_index("lon"), lax.axis_index("lat")
    return lon % 2, (lon // 2) % ny, (lat % 2) * 2 + lon // (2 * ny), lat // 2


def group_size(sizes, axes):
    return int(np.prod([sizes[axis] for axis in axes]))


def neighbours_of(place, sizes, axes):
    out = []
    for steps in np.ndindex(*(sizes[axis] for axis in axes)):
        if any(steps):
            other = list(place)
            for axis, step in zip(axes, steps):
                other[axis] = (place[axis] + step) % sizes[axis]
            out.append(tuple(other))
    return out


class Halo:
    def __init__(self, field, rows_out, tables, rows_in, cols, cols_in, corner, corner_in, edge, halo, halo_edge, sems):
        self.field, self.rows_out, self.tables, self.rows_in = field, rows_out, tables, rows_in
        self.cols, self.cols_in, self.corner, self.corner_in = cols, cols_in, corner, corner_in
        self.edge, self.halo, self.halo_edge = edge, halo, halo_edge
        self.send, self.recv = sems
        lon, lat = lax.axis_index("lon"), lax.axis_index("lat")
        nlon, nlat = lax.axis_size("lon"), lax.axis_size("lat")
        self.at_top, self.lat = lat == nlat - 1, lat
        self.below = jnp.where(self.at_top, 1, 0)
        self.up = {"lon": jnp.where(self.at_top, nlon - 1 - lon, lon), "lat": jnp.minimum(lat + 1, nlat - 1)}
        self.down = {"lon": lon, "lat": jnp.maximum(lat - 1, 0)}
        self.left = {"lon": (lon + nlon - 1) % nlon, "lat": lat}
        self.right = {"lon": (lon + 1) % nlon, "lat": lat}

    def copy(self, src, dst, sem, to):
        return pltpu.make_async_remote_copy(
            src_ref=src, dst_ref=dst, send_sem=self.send.at[sem[0]], recv_sem=self.recv.at[sem[1]], device_id=to,
            device_id_type=MESH,
        )

    def row_copies(self):
        low, high = self.rows_out
        return (
            self.copy(high, self.rows_in.at[self.below], (0, self.below), self.up),
            self.copy(low, self.rows_in.at[1], (1, 1), self.down),
            self.copy(high, self.rows_in.at[0], (0, 0), self.up),
        )

    def corner_copies(self):
        return (
            self.copy(self.corner, self.corner_in.at[self.below], (4, 4 + self.below), self.up),
            self.copy(self.corner, self.corner_in.at[1], (5, 5), self.down),
            self.copy(self.corner, self.corner_in.at[0], (4, 4), self.up),
        )

    def column_copies(self):
        return (
            self.copy(self.cols, self.cols_in.at[1], (2, 2), self.left),
            self.copy(self.cols, self.cols_in.at[0], (3, 3), self.right),
        )

    def send_pair(self, copies):
        copies[0].start()

        @pl.when(self.lat > 0)
        def _():
            copies[1].start()

    def await_pair(self, copies):
        copies[0].wait_send()
        copies[1].wait_recv()

        @pl.when(self.lat > 0)
        def _():
            copies[1].wait_send()
            copies[2].wait_recv()

    def pack_rows(self):
        pick = self.tables["edge_picker"]
        low, high = self.rows_out

        def pack(g, carry):
            rows = self.field[pl.ds(g * 16, 16)].reshape(256, LANES)
            edges = dot(pick[...], rows).astype(BF16)
            channels = pl.ds(pl.multiple_of(g * 16, 16), 16)
            for j in range(3):
                low[j, channels, :] = edges[j * 16 : (j + 1) * 16]
                high[j, channels, :] = edges[64 + j * 16 : 64 + (j + 1) * 16]
            return carry

        lax.fori_loop(0, GROUPS, pack, 0)

    def pack_columns(self):
        col_pick = self.tables["column_picker"]

        def pack(g, carry):
            rows = self.field[pl.ds(g * 16, 16)].reshape(256, LANES)
            lanes = pl.ds(pl.multiple_of(g * 256, 256), 256)
            self.cols[:, lanes] = dot_lanes(col_pick[...], rows).astype(BF16)
            return carry

        lax.fori_loop(0, GROUPS, pack, 0)

    def send_rows(self):
        self.send_pair(self.row_copies())

    def send_columns(self):
        for copy in self.column_copies():
            copy.start()

    def columns(self):
        for copy in self.column_copies():
            copy.wait()
        place, pick, col_pick = (self.tables[k] for k in ("column_placer", "edge_picker", "column_picker"))

        def put(g, carry):
            lanes = pl.ds(pl.multiple_of(g * 256, 256), 256)
            both = jnp.concatenate([self.cols_in[0, :, lanes], self.cols_in[1, :, lanes]], 0)
            tiles = dot_first(both, place[...]).astype(BF16)
            self.edge[pl.ds(g * 16, 16)] = tiles.reshape(16, ROWS, LANES)
            edges = dot(pick[...], tiles).astype(BF16)
            lanes = pl.ds(pl.multiple_of(g * LANES, LANES), LANES)
            self.corner[:, lanes] = dot_lanes(col_pick[...], edges).astype(BF16)
            return carry

        lax.fori_loop(0, GROUPS, put, 0)
        self.send_pair(self.corner_copies())

    def rows(self):
        self.await_pair(self.row_copies())
        self.await_pair(self.corner_copies())

        @pl.when(self.lat == 0)
        def _():
            self.rows_in[0] = jnp.zeros_like(self.rows_in[0])
            self.corner_in[0] = jnp.zeros_like(self.corner_in[0])

        order, placer, col_pick = (self.tables[k] for k in ("lane_orders", "halo_placer", "column_picker"))
        turn = self.below

        def settle(upper, lower):
            both = jnp.concatenate([upper, dot(lower, order[turn]).astype(BF16)], 0)
            return dot(placer[turn], both).astype(BF16).reshape(8, ROWS, LANES)

        def put(g, carry):
            channels = pl.ds(pl.multiple_of(g * 16, 16), 16)
            upper = jnp.concatenate([self.rows_in[0, j, channels, :] for j in range(3)], 0)
            lower = jnp.concatenate([self.rows_in[1, j, channels, :] for j in range(3)], 0)
            self.halo[pl.ds(g * 8, 8)] = settle(upper, lower)
            lanes = pl.ds(pl.multiple_of(g * LANES, LANES), LANES)
            above = dot_first(self.corner_in[0, :, lanes], col_pick[...]).astype(BF16)
            below = dot_first(self.corner_in[1, :, lanes], col_pick[...]).astype(BF16)
            below = jnp.where(self.at_top, below[64:112], below[:48])
            self.halo_edge[pl.ds(g * 8, 8)] = settle(above[64:112], below)
            return carry

        lax.fori_loop(0, GROUPS, put, 0)


def halo_scratch():
    return [
        pltpu.VMEM((2, 3, C, LANES), BF16),
        pltpu.VMEM((8, C * ROWS), BF16),
        pltpu.VMEM((2, 8, C * ROWS), BF16),
        pltpu.VMEM((8, C * 8), BF16),
        pltpu.VMEM((2, 8, C * 8), BF16),
        pltpu.VMEM((C, ROWS, LANES), BF16),
        pltpu.VMEM((C // 2, ROWS, LANES), BF16),
        pltpu.VMEM((C // 2, ROWS, LANES), BF16),
    ]


def build_row_matrices(variant, taps, table, wide, out):
    tap_index = lax.broadcasted_iota(jnp.int32, (LANES, 256), 0)

    def per_row(r, carry):
        first = table[variant, 0, pl.ds(r, 1), :]
        second = table[variant, 1, pl.ds(r, 1), :]
        chosen = jnp.where((tap_index == first) | (tap_index == second), 1.0, 0.0).astype(BF16)
        both = dot(taps[...].astype(BF16), chosen)
        wide[0, pl.ds(r, C, stride=ROWS), :] = both[:, :LANES]
        wide[1, pl.ds(r, C, stride=ROWS), :] = both[:, LANES:]
        return carry

    lax.fori_loop(0, ROWS, per_row, 0)

    def per_group(g, carry):
        rows = pl.ds(pl.multiple_of(g * 256, 256), 256)
        for h in range(2):
            half = wide[h, rows, :].astype(BF16).reshape(16, ROWS, LANES)
            out[pl.ds(g * 16, 16), :, h * LANES : (h + 1) * LANES] = half
        return carry

    lax.fori_loop(0, GROUPS, per_group, 0)


def convolve_own(start, stop, field, edge, matrices, emit):
    lane = lax.broadcasted_iota(jnp.int32, (ROWS, LANES), 1)
    count = 2 * UNROLL_PAIRS

    def step(i, carry):
        for u in range(count):
            c = i * count + u
            emit(c, dot(matrices[c][:, :112], shifted(field[c], edge[c], lane)))
        return carry

    lax.fori_loop(start, stop, step, 0)


def convolve_beyond(halo, halo_edge, matrices, emit):
    lane = lax.broadcasted_iota(jnp.int32, (ROWS, LANES), 1)

    def step(i, carry):
        for u in range(UNROLL_PAIRS):
            q = i * UNROLL_PAIRS + u
            both = matrices[pl.ds(2 * q, 2)].reshape(2 * ROWS, 256)
            emit(q, dot(both[:, 128:240], shifted(halo[q], halo_edge[q], lane)))
        return carry

    lax.fori_loop(0, C // 2 // UNROLL_PAIRS, step, 0)


def kernel_sums(part, grad, field, edge, halo, halo_edge, mask, inner_sums, outer_sums):
    lane = lax.broadcasted_iota(jnp.int32, (ROWS, LANES), 1)
    pad = jnp.zeros((LANES - 112, LANES), BF16)

    def in_line(product, which):
        kept = jnp.where(mask[which] > 0.0, product, 0.0)
        upper = pltpu.roll(kept[:8], 0, 1, stride=1, stride_axis=0)
        lower = pltpu.roll(kept[8:], 8, 1, stride=1, stride_axis=0)
        return jnp.sum(upper + lower, 0, keepdims=True)

    def step(i, carry):
        for u in range(UNROLL_PAIRS):
            q = i * UNROLL_PAIRS + u
            beyond = jnp.concatenate([shifted(halo[q], halo_edge[q], lane), pad], 0)
            both = grad[pl.ds(2 * q, 2)].reshape(2 * ROWS, LANES)
            outer = dot_lanes(both, beyond)
            for k in range(2):
                c = 2 * q + k
                own = jnp.concatenate([shifted(field[c], edge[c], lane), pad], 0)
                inner = dot_lanes(both[k * ROWS : (k + 1) * ROWS], own)
                inner_sums[pl.ds(c, 1), :] = in_line(inner, 0)
                outer_sums[k, pl.ds(q, 1), :] = in_line(outer[k * ROWS : (k + 1) * ROWS], 1 + k)
        return carry

    steps = C // 2 // UNROLL_PAIRS // 4
    lax.fori_loop(part * steps, (part + 1) * steps, step, 0)


class Sum:
    def __init__(self, sizes, stages, first, last, got, held, full, sems):
        self.sizes, self.ny, self.stages = sizes, sizes[1], stages
        self.place = my_place(self.ny)
        self.first, self.last, self.got, self.held, self.full = first, last, got, held, full
        self.send, self.recv, self.send_back, self.recv_back = sems
        self.base = [sum(group_size(sizes, axes) - 1 for axes, _ in stages[:i]) for i in range(len(stages))]
        self.backs = [i for i, (_, shared) in enumerate(stages) if shared]

    def others(self, axes):
        return enumerate(neighbours_of(self.place, self.sizes, axes))

    def index(self, place, axes):
        found = 0
        for axis in axes:
            found = found * self.sizes[axis] + place[axis]
        return found

    def source(self, stage):
        return self.first if stage == 0 else self.held[stage - 1]

    def start(self, stage):
        axes, shared = self.stages[stage]
        source = self.source(stage)
        tiles = self.held[stage].shape[0]
        self.copies = []
        for d, other in self.others(axes):
            self.copies.append(
                pltpu.make_async_remote_copy(
                    src_ref=source.at[pl.ds(self.index(other, axes) * tiles, tiles)] if shared else source,
                    dst_ref=self.got[stage].at[d],
                    send_sem=self.send.at[self.base[stage] + d],
                    recv_sem=self.recv.at[self.base[stage] + d],
                    device_id=device_at(*other, self.ny),
                    device_id_type=MESH,
                )
            )
        for copy in self.copies:
            copy.start()

    def finish(self, stage):
        for copy in self.copies:
            copy.wait()
        axes, shared = self.stages[stage]
        source, got, held = self.source(stage), self.got[stage], self.held[stage]
        tiles = held.shape[0]
        mine = self.index(self.place, axes) * tiles if shared else 0
        group = min(8, tiles)

        def add_up(i, carry):
            total = source[pl.ds(mine + i * group, group)].astype(F32)
            for d in range(group_size(self.sizes, axes) - 1):
                total = total + got[d, pl.ds(i * group, group)].astype(F32)
            held[pl.ds(i * group, group)] = total.astype(held.dtype)
            return carry

        lax.fori_loop(0, tiles // group, add_up, 0)

    def start_back(self, i):
        stage = self.backs[i]
        axes, _ = self.stages[stage]
        source = self.held[-1] if i == len(self.backs) - 1 else self.full[i]
        target = self.last if i == 0 else self.full[i - 1]
        tiles = source.shape[0]
        mine = self.index(self.place, axes) * tiles
        self.copies = []
        for d, other in self.others(axes):
            self.copies.append(
                pltpu.make_async_remote_copy(
                    src_ref=source,
                    dst_ref=target.at[pl.ds(mine, tiles)],
                    send_sem=self.send_back.at[self.base[stage] + d],
                    recv_sem=self.recv_back.at[self.base[stage] + d],
                    device_id=device_at(*other, self.ny),
                    device_id_type=MESH,
                )
            )
        for copy in self.copies:
            copy.start()
        group = min(8, tiles)

        def keep(i, carry):
            target[pl.ds(mine + i * group, group)] = source[pl.ds(i * group, group)]
            return carry

        lax.fori_loop(0, tiles // group, keep, 0)

    def finish_back(self, i):
        for copy in self.copies:
            copy.wait()


BIG_STAGES = (((0,), True), ((1, 2), True), ((3,), True))
SMALL_STAGES = (((0,), True), ((3,), True), ((1, 2), False))


def sum_scratch(sizes, stages, count, tile, dtype):
    got, held, full = [], [], []
    rest = count
    for axes, shared in stages:
        members = group_size(sizes, axes)
        rest = rest // members if shared else rest
        got.append(pltpu.VMEM((members - 1, rest) + tile, dtype))
        held.append(pltpu.VMEM((rest,) + tile, dtype))
        if shared:
            full.append(pltpu.VMEM((rest,) + tile, dtype))
    return [pltpu.VMEM((count,) + tile, dtype), pltpu.VMEM((count,) + tile, dtype)] + got + held + full[:-1]


def sum_sems(sizes):
    links = sum(group_size(sizes, axes) - 1 for axes, _ in BIG_STAGES)
    return [pltpu.SemaphoreType.DMA((links,)) for _ in range(4)]


TABLES = ("tap_table", "edge_picker", "halo_placer", "column_picker", "column_placer", "lane_orders", "tap_gather", "valid_mask")


def make_tables():
    return (
        jnp.asarray(tap_tables()),
        jnp.asarray(edge_picker(), BF16),
        jnp.asarray(halo_placer(), BF16),
        jnp.asarray(column_picker(), BF16),
        jnp.asarray(column_placer(), BF16),
        jnp.asarray(lane_orders(), BF16),
        jnp.asarray(tap_gather(), F32),
        jnp.asarray(valid_mask(), F32),
    )


def forward_block(rb, w1t, w2, s):
    first = rb * BLOCK_ROWS
    for j in range(BLOCK_ROWS):
        rows = pl.ds(first + j, C, stride=ROWS)
        sea = s["land"][pl.ds(first + j, 1), :]
        lanes = slice(j * LANES, (j + 1) * LANES)
        masked = sea * s["filt"][rows, :]
        average = jnp.sum(masked, 0, keepdims=True) * (1.0 / C)
        centred = masked - average
        inverse = lax.rsqrt(jnp.sum(centred * centred, 0, keepdims=True) * (1.0 / C) + epsilon)
        unit = centred * inverse
        s["inverse"][pl.ds(first + j, 1), :] = inverse
        s["unit"][first + j] = unit
        s["normed"][:, lanes] = (unit * s["gain"][...]).astype(BF16)
        s["scaled"][:, lanes] = (sea * s["scale"][...] * s["cot"][rows, :]).astype(BF16)
    for f in range(4):
        part = slice(f * 256, (f + 1) * 256)
        s["hidden"][f % 2] = dot(w1t[part, :], s["normed"][...])
        s["grad_act"][f % 2] = dot(w2[part, :], s["scaled"][...])
        for t in range(16):
            hidden = s["hidden"][f % 2, t * 16 : (t + 1) * 16, :]
            grad_act = s["grad_act"][f % 2, t * 16 : (t + 1) * 16, :]
            lower, bell = halves(hidden)
            rows = slice(f * 256 + t * 16, f * 256 + (t + 1) * 16)
            s["activated"][rb, rows, :] = (hidden * lower).astype(BF16)
            s["grad_hidden"][rb, rows, :] = (grad_act * (lower + hidden * bell * 0.3989422804014327)).astype(BF16)
    s["reduce_sum"][...] += dot_lanes(s["activated"][rb], s["scaled"][...])
    s["expand_sum"][...] += dot_lanes(s["normed"][...], s["grad_hidden"][rb])


def backward_block(rb, w1, w2t, s):
    first = rb * BLOCK_ROWS
    s["branch"][...] = dot(w2t[...], s["activated"][rb])
    s["grad_norm"][...] = dot(w1[...], s["grad_hidden"][rb])
    for j in range(BLOCK_ROWS):
        rows = pl.ds(first + j, C, stride=ROWS)
        sea = s["land"][pl.ds(first + j, 1), :]
        lanes = slice(j * LANES, (j + 1) * LANES)
        branch = sea * s["branch"][:, lanes]
        grad_norm = s["grad_norm"][:, lanes]
        unit = s["unit"][first + j]
        s["scale_sum"][...] += s["cot"][rows, :] * branch
        s["added"][rows, :] = s["scale"][...] * branch
        s["gain_sum"][...] += grad_norm * unit
        grad_hat = grad_norm * s["gain"][...]
        mean = jnp.sum(grad_hat, 0, keepdims=True) * (1.0 / C)
        mean_unit = jnp.sum(grad_hat * unit, 0, keepdims=True) * (1.0 / C)
        grad = (sea * s["inverse"][pl.ds(first + j, 1), :]) * (grad_hat - mean - unit * mean_unit)
        s["grad_wide"][0, rows, :] = grad
        s["grad_wide"][1, pl.ds(ROWS - 1 - first - j, C, stride=ROWS), :] = grad
        s["grad_rows"][first + j] = grad.astype(BF16)


COMPUTE = {
    "land": ((ROWS, LANES), F32),
    "gain": ((C, LANES), F32),
    "scale": ((C, LANES), F32),
    "taps": ((C, LANES), F32),
    "w1t": ((FF, C), BF16),
    "w2t": ((C, FF), BF16),
    "matrices": ((C, ROWS, 256), BF16),
    "back_matrices": ((C, ROWS, 256), BF16),
    "filt": ((C * ROWS, LANES), F32),
    "cot": ((C * ROWS, LANES), F32),
    "inverse": ((ROWS, LANES), F32),
    "unit": ((ROWS, C, LANES), F32),
    "normed": ((C, BLOCK), BF16),
    "scaled": ((C, BLOCK), BF16),
    "hidden": ((2, 256, BLOCK), F32),
    "grad_act": ((2, 256, BLOCK), F32),
    "activated": ((ROWS // BLOCK_ROWS, FF, BLOCK), BF16),
    "grad_hidden": ((ROWS // BLOCK_ROWS, FF, BLOCK), BF16),
    "branch": ((C, BLOCK), F32),
    "grad_norm": ((C, BLOCK), F32),
    "reduce_sum": ((FF, C), F32),
    "expand_sum": ((C, FF), F32),
    "added": ((C * ROWS, LANES), F32),
    "grad_wide": ((2, C * ROWS, LANES), F32),
    "grad": ((C, ROWS, LANES), BF16),
    "grad_rows": ((ROWS, C, LANES), BF16),
    "edge_rows": ((2, 3, C, LANES), BF16),
    "turned_grad": ((C, ROWS, LANES), BF16),
    "scale_sum": ((C, LANES), F32),
    "gain_sum": ((C, LANES), F32),
    "inner_sums": ((C, LANES), F32),
    "outer_sums": ((2, C // 2, LANES), F32),
}


def prepare(land, depth_kernel, gain, scale, w1, w2, cotangent, s):
    s["land"][...] = land[...].astype(F32)
    for vector, name in ((gain, "gain"), (scale, "scale")):
        for h in range(2):
            row = vector[pl.ds(h, 1), :]
            s[name][h * LANES : (h + 1) * LANES, :] = jnp.broadcast_to(row, (LANES, LANES)).T
    for f in range(4):
        part = slice(f * 256, (f + 1) * 256)
        s["w1t"][part, :] = w1[:, part].T
        s["w2t"][:, part] = w2[part, :].T

    def widen(g, carry):
        rows = pl.ds(pl.multiple_of(g * 256, 256), 256)
        s["cot"][rows, :] = cotangent[pl.ds(g * 16, 16)].reshape(256, LANES).astype(F32)
        return carry

    lax.fori_loop(0, GROUPS, widen, 0)
    for name in ("reduce_sum", "expand_sum", "scale_sum", "gain_sum"):
        s[name][...] = jnp.zeros_like(s[name])


def place_taps(depth_kernel, s):
    taps = depth_kernel[...].astype(F32)
    even = lax.broadcasted_iota(jnp.int32, taps.shape, 0) % 2 == 0
    s["taps"][...] = jnp.zeros_like(s["taps"])
    s["taps"][:, :49] = jnp.where(even, taps, 0.0)
    s["taps"][:, 64 : 64 + 49] = jnp.where(even, 0.0, taps)


def block_kernel(sizes, state, land, depth_kernel, gain, scale, w1, w2, cotangent, *rest):
    tables = dict(zip(TABLES, rest[: len(TABLES)]))
    rest = list(rest[len(TABLES) :])
    updated, state_grad, big_last, small_out = rest[:4]
    rest = rest[4:]

    def take(n):
        out = rest[:n]
        del rest[:n]
        return out

    s = dict(zip(COMPUTE, take(len(COMPUTE))))
    ahead_refs = take(len(halo_scratch()))
    back_refs = take(len(halo_scratch()))
    edge_rows, grad_rows = s["edge_rows"], s["grad_rows"]
    ahead = Halo(state, (edge_rows.at[0], edge_rows.at[1]), tables, *ahead_refs, sems=take(2))
    back = Halo(
        s["grad"], (grad_rows.at[pl.ds(0, 3)], grad_rows.at[pl.ds(ROWS - 3, 3)]), tables, *back_refs, sems=take(2)
    )
    stages = len(BIG_STAGES)
    (big_first,) = take(1)
    big = Sum(sizes, BIG_STAGES, big_first, big_last, take(stages), take(stages), take(2), take(4))
    small_first, small_last = take(2)
    small = Sum(sizes, SMALL_STAGES, small_first, small_last, take(stages), take(stages), take(1), take(4))

    barrier = pltpu.get_barrier_semaphore()
    greeted = [ahead.up, ahead.left, ahead.right]
    for axes, _ in BIG_STAGES:
        greeted += [device_at(*other, sizes[1]) for _, other in big.others(axes)]
    for device in greeted:
        pl.semaphore_signal(barrier, inc=1, device_id=device, device_id_type=MESH)

    @pl.when(ahead.lat > 0)
    def _():
        pl.semaphore_signal(barrier, inc=1, device_id=ahead.down, device_id_type=MESH)

    ahead.pack_rows()
    pl.semaphore_wait(barrier, len(greeted) + jnp.where(ahead.lat > 0, 1, 0))
    ahead.send_rows()
    ahead.pack_columns()
    ahead.send_columns()
    place_taps(depth_kernel, s)
    build_row_matrices(0, s["taps"], tables["tap_table"], s["grad_wide"], s["matrices"])
    ahead.columns()

    def put_filtered(c, value):
        s["filt"][pl.ds(pl.multiple_of(c * ROWS, ROWS), ROWS), :] = value

    own_steps = C // 2 // UNROLL_PAIRS
    convolve_own(0, own_steps, state, ahead.edge, s["matrices"], put_filtered)
    prepare(land, depth_kernel, gain, scale, w1, w2, cotangent, s)

    def add_filtered(q, value):
        rows = pl.ds(pl.multiple_of(q * 2 * ROWS, 2 * ROWS), 2 * ROWS)
        s["filt"][rows, :] += value

    def ahead_step(step, carry):
        @pl.when(step == 1)
        def _():
            ahead.rows()
            convolve_beyond(ahead.halo, ahead.halo_edge, s["matrices"], add_filtered)

        forward_block(step + 1 - 2 * (step % 2), s["w1t"], w2, s)
        return carry

    lax.fori_loop(0, ROWS // BLOCK_ROWS, ahead_step, 0)

    def cut_expand(g, carry):
        rows = pl.ds(pl.multiple_of(g * 16, 16), 16)
        for h in range(8):
            big_first[g * 8 + h] = s["expand_sum"][rows, h * LANES : (h + 1) * LANES].astype(BF16)
        return carry

    lax.fori_loop(0, C // 16, cut_expand, 0)

    def cut_reduce(g, carry):
        rows = pl.ds(pl.multiple_of(g * 16, 16), 16)
        for h in range(2):
            big_first[128 + g * 2 + h] = s["reduce_sum"][rows, h * LANES : (h + 1) * LANES].astype(BF16)
        return carry

    lax.fori_loop(0, FF // 16, cut_reduce, 0)
    big.start(0)
    build_row_matrices(back.below + 1, s["taps"], tables["tap_table"], s["grad_wide"], s["back_matrices"])
    big.finish(0)
    big.start(1)

    def back_step(step, carry):
        @pl.when(step == 2)
        def _():
            back.send_rows()

        backward_block(jnp.where(step < 2, 3 * step, step - 1), w1, s["w2t"], s)
        return carry

    lax.fori_loop(0, ROWS // BLOCK_ROWS, back_step, 0)

    def settle(g, carry):
        rows = pl.ds(pl.multiple_of(g * 128, 128), 128)
        channels = pl.ds(g * 8, 8)
        s["grad"][channels] = s["grad_wide"][0, rows, :].astype(BF16).reshape(8, ROWS, LANES)
        s["turned_grad"][channels] = s["grad_wide"][1, rows, :].astype(BF16).reshape(8, ROWS, LANES)
        updated[channels] = (
            (state[channels].reshape(128, LANES).astype(F32) + s["added"][rows, :]).astype(BF16).reshape(8, ROWS, LANES)
        )
        return carry

    lax.fori_loop(0, C // 8, settle, 0)
    back.pack_columns()
    back.send_columns()

    def sums(part):
        kernel_sums(
            part, s["turned_grad"], state, ahead.edge, ahead.halo, ahead.halo_edge, tables["valid_mask"],
            s["inner_sums"], s["outer_sums"],
        )

    sums(0)
    big.finish(1)
    big.start(2)
    back.columns()
    sums(1)
    sums(2)
    big.finish(2)
    big.start_back(2)
    sums(3)

    exact = lax.Precision.HIGHEST
    gather = tables["tap_gather"]
    pair = lax.broadcasted_iota(jnp.int32, (C // 2, C), 0)
    channel = lax.broadcasted_iota(jnp.int32, (C // 2, C), 1)
    total = dot_lanes(gather[0], s["inner_sums"][...], exact)
    for h in range(2):
        part = dot_lanes(gather[1 + h], s["outer_sums"][h], exact)
        spread = jnp.where(channel == 2 * pair + h, 1.0, 0.0)
        total = total + jnp.dot(part, spread, preferred_element_type=F32, precision=exact)
    row = lax.broadcasted_iota(jnp.int32, (64, LANES), 0)
    total = total + dot_lanes(jnp.where(row == 49, 1.0, 0.0), s["gain_sum"][...], exact)
    total = total + dot_lanes(jnp.where(row == 50, 1.0, 0.0), s["scale_sum"][...], exact)
    for g in range(8):
        for h in range(2):
            small_first[g * 2 + h] = total[g * 8 : (g + 1) * 8, h * LANES : (h + 1) * LANES]
    small.start(0)
    big.finish_back(2)
    big.start_back(1)

    def put_part(c, value):
        s["added"][pl.ds(pl.multiple_of(c * ROWS, ROWS), ROWS), :] = value

    def put_grad(q, value):
        rows = pl.ds(pl.multiple_of(q * 2 * ROWS, 2 * ROWS), 2 * ROWS)
        total = s["cot"][rows, :] + s["added"][rows, :] + value
        state_grad[pl.ds(q * 2, 2)] = total.astype(BF16).reshape(2, ROWS, LANES)

    half = own_steps // 2
    convolve_own(0, half, s["grad"], back.edge, s["back_matrices"], put_part)
    small.finish(0)
    small.start(1)
    convolve_own(half, own_steps, s["grad"], back.edge, s["back_matrices"], put_part)
    back.rows()
    small.finish(1)
    small.start(2)
    convolve_beyond(back.halo, back.halo_edge, s["back_matrices"], put_grad)
    small.finish(2)
    small.start_back(1)
    big.finish_back(1)
    big.start_back(0)
    small.finish_back(1)
    small.start_back(0)
    small.finish_back(0)
    for g in range(8):
        for h in range(2):
            small_out[g * 8 : (g + 1) * 8, h * LANES : (h + 1) * LANES] = small_last[g * 2 + h]
    big.finish_back(0)


def hand_over(factor, updated, state_grad, big, small, *outs):
    updated_out, state_out, kernel_out, gain_out, expand_out, reduce_out, scale_out = outs
    updated_out[...] = updated[...]
    state_out[...] = state_grad[...]

    def paste_expand(g, carry):
        rows = pl.ds(pl.multiple_of(g * 16, 16), 16)
        for h in range(8):
            expand_out[rows, h * LANES : (h + 1) * LANES] = big[g * 8 + h].astype(F32) * factor
        return carry

    lax.fori_loop(0, C // 16, paste_expand, 0)

    def paste_reduce(g, carry):
        rows = pl.ds(pl.multiple_of(g * 16, 16), 16)
        for h in range(2):
            reduce_out[rows, h * LANES : (h + 1) * LANES] = big[128 + g * 2 + h].astype(F32) * factor
        return carry

    lax.fori_loop(0, FF // 16, paste_reduce, 0)
    kernel_out[...] = small[...].T[:, :49] * factor
    gain_out[...] = small[49:50, :] * factor
    scale_out[...] = small[50:51, :] * factor


def local(state, land, depth_kernel, norm_gain, expand_weight, reduce_weight, layer_scale, cotangent):
    ny, nz = lax.axis_size("lon") // 4, lax.axis_size("lat") // 2
    sizes = (2, ny, 4, nz)
    operands = (
        state, land, depth_kernel, norm_gain.reshape(2, LANES), layer_scale.reshape(2, LANES), expand_weight,
        reduce_weight, cotangent, *make_tables(),
    )
    vmem = pl.BlockSpec(memory_space=pltpu.VMEM)
    field = jax.ShapeDtypeStruct((C, ROWS, LANES), BF16)
    out_shape = (
        field,
        field,
        jax.ShapeDtypeStruct((256, 16, LANES), BF16),
        jax.ShapeDtypeStruct((64, C), F32),
    )
    halo_sems = [pltpu.SemaphoreType.DMA((6,)) for _ in range(4)]
    parts = pl.pallas_call(
        functools.partial(block_kernel, sizes),
        out_shape=out_shape,
        in_specs=[vmem] * len(operands),
        out_specs=[vmem] * len(out_shape),
        scratch_shapes=[pltpu.VMEM(shape, dtype) for shape, dtype in COMPUTE.values()]
        + halo_scratch()
        + halo_scratch()
        + halo_sems
        + sum_scratch(sizes, BIG_STAGES, 256, (16, LANES), BF16)[1:]
        + sum_sems(sizes)
        + sum_scratch(sizes, SMALL_STAGES, 16, (8, LANES), F32)
        + sum_sems(sizes),
        compiler_params=pltpu.CompilerParams(
            collective_id=0, has_side_effects=True, vmem_limit_bytes=63 * 2**20
        ),
        name="convnext_block",
    )(*operands)
    factor = float(ROWS * lax.axis_size("lat") * LANES * lax.axis_size("lon")) ** (-0.5)
    vector = jax.ShapeDtypeStruct((1, C), F32)
    updated, state_grad, kernel_grad, gain_grad, expand_grad, reduce_grad, scale_grad = pl.pallas_call(
        functools.partial(hand_over, factor),
        out_shape=(
            field, field, jax.ShapeDtypeStruct((C, 49), F32), vector, jax.ShapeDtypeStruct((C, FF), F32),
            jax.ShapeDtypeStruct((FF, C), F32), vector,
        ),
        in_specs=[vmem] * 4,
        out_specs=[vmem] * 7,
        compiler_params=pltpu.CompilerParams(vmem_limit_bytes=24 * 2**20),
        name="hand_over",
    )(*parts)
    return updated, state_grad, kernel_grad, gain_grad.reshape(C), expand_grad, reduce_grad, scale_grad.reshape(C)


def solution(mesh):
    grid = P(None, "lat", "lon")
    return jax.shard_map(
        local,
        mesh=mesh,
        in_specs=(grid, P("lat", "lon"), P(), P(), P(), P(), P(), grid),
        out_specs=(grid, grid, P(), P(), P(), P(), P()),
        check_vma=False,
    )
```

```python
import functools

import jax
import jax.numpy as jnp
import numpy as np
from jax import lax
from jax.experimental import pallas as pl
from jax.experimental.pallas import tpu as pltpu
from jax.sharding import PartitionSpec as P

epsilon = 1e-06
MESH = pl.DeviceIdType.MESH
BF16 = jnp.bfloat16
F32 = jnp.float32
C, FF, ROWS, LANES = 256, 1024, 16, 128
BLOCK_ROWS = 4
BLOCK = BLOCK_ROWS * LANES
UNROLL_PAIRS = 16
GROUPS = C // 16


def tap_spreads():
    spread = np.zeros((3, LANES, 256), np.float32)
    for variant in range(3):
        for a in range(7):
            for b in range(7):
                tap = a * 7 + b
                turned = 48 - tap if variant else tap
                spread[variant, turned, (b * 16 + a - 3) % LANES] = 1
                spread[variant, turned + 64, (b * 16 + a - 3) % LANES] = 1
                if a == 3:
                    continue
                beyond = tap if variant == 2 and a > 3 else turned
                for h in range(2):
                    lane = b * 16 + 8 * h + (a if a < 3 else a - 16)
                    spread[variant, beyond + 64 * h, LANES + lane % LANES] = 1
    return spread


def edge_picker():
    pick = np.zeros((LANES, 256), np.float32)
    for j in range(3):
        for c in range(16):
            pick[j * 16 + c, c * 16 + j] = 1
            pick[64 + j * 16 + c, c * 16 + 13 + j] = 1
    return pick


def halo_placer():
    place = np.zeros((2, 128, 96), np.float32)
    for c in range(16):
        for j in range(3):
            row = (c // 2) * 16 + (c % 2) * 8
            place[:, row + j, j * 16 + c] = 1
            place[0, row + 3 + j, 48 + j * 16 + c] = 1
            place[1, row + 3 + j, 48 + (2 - j) * 16 + c] = 1
    return place


def lane_orders():
    return np.stack([np.eye(128), np.eye(128)[::-1]]).astype(np.float32)


def tap_gather():
    gather = np.zeros((3, 64, 128), np.float32)
    for a in range(7):
        for b in range(7):
            gather[0, a * 7 + b, b * 16 + a + 12] = 1
            for h in range(2):
                lane = b * 16 + 8 * h + a + (15 if a < 3 else -1)
                if a != 3:
                    gather[1 + h, a * 7 + b, lane] = 1
    return gather


def valid_mask():
    mask = np.zeros((6, ROWS, 128), np.float32)
    for r in range(ROWS):
        for b in range(7):
            for i in range(16):
                if 0 <= i + 3 - r <= 6:
                    mask[0, r, b * 16 + i] = 1
            for h in range(2):
                for j in range(6):
                    p = j if j < 3 else 16 + j
                    if 0 <= p - r <= 6:
                        mask[1 + h, r, b * 16 + 8 * h + j] = 1
    mask[3:] = mask[:3, ::-1]
    return mask


def dot(a, b):
    return jnp.dot(a, b, preferred_element_type=F32)


def dot_lanes(a, b, precision=None):
    return lax.dot_general(a, b, (((1,), (1,)), ((), ())), preferred_element_type=F32, precision=precision)


def dot_first(a, b):
    return lax.dot_general(a, b, (((0,), (0,)), ((), ())), preferred_element_type=F32)


def shifted(tile, edge, lane):
    windows = []
    for b in range(7):
        if b == 3:
            windows.append(tile)
            continue
        mask = lane >= 125 + b if b < 3 else lane < b - 3
        windows.append(pltpu.roll(jnp.where(mask, edge, tile), (3 - b) % LANES, 1))
    return jnp.concatenate(windows, 0)


def gather_columns(g):
    source = lax.broadcasted_iota(jnp.int32, (LANES, LANES), 0)
    target = lax.broadcasted_iota(jnp.int32, (LANES, LANES), 1) - 8 * g
    first = (source < 3) & (target == source)
    last = (source >= 125) & (target == source - 122)
    return jnp.where(first | last, 1.0, 0.0).astype(BF16)


def spread_columns(g):
    source = lax.broadcasted_iota(jnp.int32, (LANES, LANES), 0) - 8 * g
    target = lax.broadcasted_iota(jnp.int32, (LANES, LANES), 1)
    first = (target < 3) & (source == target)
    last = (target >= 125) & (source == target - 122)
    return jnp.where(first | last, 1.0, 0.0).astype(BF16)


def join_columns(g):
    source = lax.broadcasted_iota(jnp.int32, (2 * LANES, LANES), 0) - 8 * g
    target = lax.broadcasted_iota(jnp.int32, (2 * LANES, LANES), 1)
    last = (target >= 125) & (source == target - 122)
    first = (target < 3) & (source == target + LANES)
    return jnp.where(first | last, 1.0, 0.0).astype(BF16)


def halves(hidden):
    bell = jnp.exp(hidden * hidden * -0.5)
    t = pl.reciprocal(1.0 + 0.23164190 * jnp.abs(hidden), approx=False)
    poly = t * (0.127414796 + t * (-0.142248368 + t * (0.7107068705 + t * (-0.7265760135 + t * 0.5307027145))))
    tail = poly * bell
    return jnp.where(hidden >= 0.0, 1.0 - tail, tail), bell


def device_at(core, y, x, z, ny):
    return {"lon": (x % 2) * (2 * ny) + y * 2 + core, "lat": z * 2 + x // 2}


def my_place(ny):
    lon, lat = lax.axis_index("lon"), lax.axis_index("lat")
    return lon % 2, (lon // 2) % ny, (lat % 2) * 2 + lon // (2 * ny), lat // 2


def group_size(sizes, axes):
    return int(np.prod([sizes[axis] for axis in axes]))


def neighbours_of(place, sizes, axes):
    out = []
    for steps in np.ndindex(*(sizes[axis] for axis in axes)):
        if any(steps):
            other = list(place)
            for axis, step in zip(axes, steps):
                other[axis] = (place[axis] + step) % sizes[axis]
            out.append(tuple(other))
    return out


class Halo:
    def __init__(self, field, rows_out, tables, rows_in, cols, cols_in, corner, corner_in, edge, halo, halo_edge, sems):
        self.field, self.rows_out, self.tables, self.rows_in = field, rows_out, tables, rows_in
        self.cols, self.cols_in, self.corner, self.corner_in = cols, cols_in, corner, corner_in
        self.edge, self.halo, self.halo_edge = edge, halo, halo_edge
        self.send, self.recv = sems
        lon, lat = lax.axis_index("lon"), lax.axis_index("lat")
        nlon, nlat = lax.axis_size("lon"), lax.axis_size("lat")
        self.at_top, self.lat = lat == nlat - 1, lat
        self.below = jnp.where(self.at_top, 1, 0)
        self.up = {"lon": jnp.where(self.at_top, nlon - 1 - lon, lon), "lat": jnp.minimum(lat + 1, nlat - 1)}
        self.down = {"lon": lon, "lat": jnp.maximum(lat - 1, 0)}
        self.left = {"lon": (lon + nlon - 1) % nlon, "lat": lat}
        self.right = {"lon": (lon + 1) % nlon, "lat": lat}

    def copy(self, src, dst, sem, to):
        return pltpu.make_async_remote_copy(
            src_ref=src, dst_ref=dst, send_sem=self.send.at[sem[0]], recv_sem=self.recv.at[sem[1]], device_id=to,
            device_id_type=MESH,
        )

    def row_copies(self):
        low, high = self.rows_out
        return (
            self.copy(high, self.rows_in.at[self.below], (0, self.below), self.up),
            self.copy(low, self.rows_in.at[1], (1, 1), self.down),
            self.copy(high, self.rows_in.at[0], (0, 0), self.up),
        )

    def corner_copies(self):
        return (
            self.copy(self.corner, self.corner_in.at[self.below], (4, 4 + self.below), self.up),
            self.copy(self.corner, self.corner_in.at[1], (5, 5), self.down),
            self.copy(self.corner, self.corner_in.at[0], (4, 4), self.up),
        )

    def column_copies(self):
        return (
            self.copy(self.cols, self.cols_in.at[1], (2, 2), self.left),
            self.copy(self.cols, self.cols_in.at[0], (3, 3), self.right),
        )

    def send_pair(self, copies):
        copies[0].start()

        @pl.when(self.lat > 0)
        def _():
            copies[1].start()

    def await_pair(self, copies):
        copies[0].wait_send()
        copies[1].wait_recv()

        @pl.when(self.lat > 0)
        def _():
            copies[1].wait_send()
            copies[2].wait_recv()

    def pack_rows(self):
        pick = self.tables["edge_picker"]
        low, high = self.rows_out

        def pack(i, carry):
            for u in range(4):
                g = i * 4 + u
                edges = dot(pick[...], self.field[pl.ds(g * 16, 16)].reshape(256, LANES)).astype(BF16)
                channels = pl.ds(pl.multiple_of(g * 16, 16), 16)
                for j in range(3):
                    low[j, channels, :] = edges[j * 16 : (j + 1) * 16]
                    high[j, channels, :] = edges[64 + j * 16 : 64 + (j + 1) * 16]
            return carry

        lax.fori_loop(0, GROUPS // 4, pack, 0)

    def pack_columns(self):
        def pack(i, total):
            for u in range(4):
                g = i * 4 + u
                total = total + dot(self.field[pl.ds(g * 16, 16)].reshape(256, LANES), gather_columns(g))
            return total

        self.cols[...] = lax.fori_loop(0, GROUPS // 4, pack, jnp.zeros((256, LANES), F32)).astype(BF16)

    def send_rows(self):
        self.send_pair(self.row_copies())

    def send_columns(self):
        for copy in self.column_copies():
            copy.start()

    def columns(self):
        for copy in self.column_copies():
            copy.wait()
        pick = self.tables["edge_picker"]

        def put(i, total):
            both = jnp.concatenate([self.cols_in[0], self.cols_in[1]], 1)
            for u in range(4):
                g = i * 4 + u
                tiles = dot(both, join_columns(g)).astype(BF16)
                self.edge[pl.ds(g * 16, 16)] = tiles.reshape(16, ROWS, LANES)
                total = total + dot(dot(pick[...], tiles).astype(BF16), gather_columns(g))
            return total

        self.corner[...] = lax.fori_loop(0, GROUPS // 4, put, jnp.zeros((LANES, LANES), F32)).astype(BF16)
        self.send_pair(self.corner_copies())

    def rows(self):
        self.await_pair(self.row_copies())
        self.await_pair(self.corner_copies())

        @pl.when(self.lat == 0)
        def _():
            self.rows_in[0] = jnp.zeros_like(self.rows_in[0])
            self.corner_in[0] = jnp.zeros_like(self.corner_in[0])

        order, placer = self.tables["lane_orders"], self.tables["halo_placer"]
        turn = self.below

        def settle(upper, lower):
            both = jnp.concatenate([upper, dot(lower, order[turn]).astype(BF16)], 0)
            return dot(placer[turn], both).astype(BF16).reshape(8, ROWS, LANES)

        def put(i, carry):
            corner = jnp.concatenate(
                [self.corner_in[0, 64:112, :], self.corner_in[1, 64:112, :], self.corner_in[1, :48, :]], 0
            )
            for u in range(4):
                g = i * 4 + u
                channels = pl.ds(pl.multiple_of(g * 16, 16), 16)
                upper = jnp.concatenate([self.rows_in[0, j, channels, :] for j in range(3)], 0)
                lower = jnp.concatenate([self.rows_in[1, j, channels, :] for j in range(3)], 0)
                self.halo[pl.ds(g * 8, 8)] = settle(upper, lower)
                spread = dot(corner, spread_columns(g))
                below = jnp.where(self.at_top, spread[48:96], spread[96:]).astype(BF16)
                self.halo_edge[pl.ds(g * 8, 8)] = settle(spread[:48].astype(BF16), below)
            return carry

        lax.fori_loop(0, GROUPS // 4, put, 0)


def halo_scratch():
    return [
        pltpu.VMEM((2, 3, C, LANES), BF16),
        pltpu.VMEM((256, LANES), BF16),
        pltpu.VMEM((2, 256, LANES), BF16),
        pltpu.VMEM((LANES, LANES), BF16),
        pltpu.VMEM((2, LANES, LANES), BF16),
        pltpu.VMEM((C, ROWS, LANES), BF16),
        pltpu.VMEM((C // 2, ROWS, LANES), BF16),
        pltpu.VMEM((C // 2, ROWS, LANES), BF16),
    ]


def build_row_matrices(variant, taps, spread, mask, lines, out):
    both = dot(taps[...].astype(BF16), spread[variant])
    lines[0] = both[:, :LANES]
    lines[1] = both[:, LANES:]

    def per_group(g, carry):
        for u in range(16):
            c = g * 16 + u
            for h in range(2):
                line = jnp.broadcast_to(lines[h, pl.ds(c, 1), :], (8, LANES))
                upper = pltpu.roll(line, 0, 1, stride=1, stride_axis=0)
                lower = pltpu.roll(line, 8, 1, stride=1, stride_axis=0)
                kept = jnp.where(mask[h * (1 + u % 2)] > 0.0, jnp.concatenate([upper, lower], 0), 0.0)
                out[c, :, h * LANES : (h + 1) * LANES] = kept.astype(BF16)
        return carry

    lax.fori_loop(0, GROUPS, per_group, 0)


def convolve_own(start, stop, field, edge, matrices, emit):
    lane = lax.broadcasted_iota(jnp.int32, (ROWS, LANES), 1)
    count = 2 * UNROLL_PAIRS

    def step(i, carry):
        for u in range(count):
            c = i * count + u
            emit(c, dot(matrices[c][:, :112], shifted(field[c], edge[c], lane)))
        return carry

    lax.fori_loop(start, stop, step, 0)


def convolve_beyond(halo, halo_edge, matrices, emit):
    lane = lax.broadcasted_iota(jnp.int32, (ROWS, LANES), 1)

    def step(i, carry):
        for u in range(UNROLL_PAIRS):
            q = i * UNROLL_PAIRS + u
            both = matrices[pl.ds(2 * q, 2)].reshape(2 * ROWS, 256)
            emit(q, dot(both[:, 128:240], shifted(halo[q], halo_edge[q], lane)))
        return carry

    lax.fori_loop(0, C // 2 // UNROLL_PAIRS, step, 0)


def kernel_sums(part, grad, field, edge, halo, halo_edge, mask, inner_sums, outer_sums):
    lane = lax.broadcasted_iota(jnp.int32, (ROWS, LANES), 1)
    pad = jnp.zeros((LANES - 112, LANES), BF16)

    def in_line(product, which):
        kept = jnp.where(mask[3 + which] > 0.0, product, 0.0)
        upper = pltpu.roll(kept[:8], 0, 1, stride=1, stride_axis=0)
        lower = pltpu.roll(kept[8:], 8, 1, stride=1, stride_axis=0)
        return jnp.sum(upper + lower, 0, keepdims=True)

    def step(i, carry):
        for u in range(UNROLL_PAIRS):
            q = i * UNROLL_PAIRS + u
            beyond = jnp.concatenate([shifted(halo[q], halo_edge[q], lane), pad], 0)
            both = grad[pl.ds(2 * q, 2)].reshape(2 * ROWS, LANES)
            outer = dot_lanes(both, beyond)
            for k in range(2):
                c = 2 * q + k
                own = jnp.concatenate([shifted(field[c], edge[c], lane), pad], 0)
                inner = dot_lanes(both[k * ROWS : (k + 1) * ROWS], own)
                inner_sums[pl.ds(c, 1), :] = in_line(inner, 0)
                outer_sums[k, pl.ds(q, 1), :] = in_line(outer[k * ROWS : (k + 1) * ROWS], 1 + k)
        return carry

    steps = C // 2 // UNROLL_PAIRS // 4
    lax.fori_loop(part * steps, (part + 1) * steps, step, 0)


class Sum:
    def __init__(self, sizes, stages, first, last, got, held, full, sems):
        self.sizes, self.ny, self.stages = sizes, sizes[1], stages
        self.place = my_place(self.ny)
        self.first, self.last, self.got, self.held, self.full = first, last, got, held, full
        self.send, self.recv, self.send_back, self.recv_back = sems
        self.base = [sum(group_size(sizes, axes) - 1 for axes, _ in stages[:i]) for i in range(len(stages))]
        self.backs = [i for i, (_, shared) in enumerate(stages) if shared]

    def others(self, axes):
        return enumerate(neighbours_of(self.place, self.sizes, axes))

    def index(self, place, axes):
        found = 0
        for axis in axes:
            found = found * self.sizes[axis] + place[axis]
        return found

    def source(self, stage):
        return self.first if stage == 0 else self.held[stage - 1]

    def start(self, stage):
        axes, shared = self.stages[stage]
        source = self.source(stage)
        tiles = self.held[stage].shape[0]
        self.copies = []
        for d, other in self.others(axes):
            self.copies.append(
                pltpu.make_async_remote_copy(
                    src_ref=source.at[pl.ds(self.index(other, axes) * tiles, tiles)] if shared else source,
                    dst_ref=self.got[stage].at[d],
                    send_sem=self.send.at[self.base[stage] + d],
                    recv_sem=self.recv.at[self.base[stage] + d],
                    device_id=device_at(*other, self.ny),
                    device_id_type=MESH,
                )
            )
        for copy in self.copies:
            copy.start()

    def finish(self, stage):
        for copy in self.copies:
            copy.wait()
        axes, shared = self.stages[stage]
        source, got, held = self.source(stage), self.got[stage], self.held[stage]
        tiles = held.shape[0]
        mine = self.index(self.place, axes) * tiles if shared else 0
        group = min(8, tiles)

        def add_up(i, carry):
            total = source[pl.ds(mine + i * group, group)].astype(F32)
            for d in range(group_size(self.sizes, axes) - 1):
                total = total + got[d, pl.ds(i * group, group)].astype(F32)
            held[pl.ds(i * group, group)] = total.astype(held.dtype)
            return carry

        lax.fori_loop(0, tiles // group, add_up, 0)

    def start_back(self, i):
        stage = self.backs[i]
        axes, _ = self.stages[stage]
        source = self.held[-1] if i == len(self.backs) - 1 else self.full[i]
        target = self.last if i == 0 else self.full[i - 1]
        tiles = source.shape[0]
        mine = self.index(self.place, axes) * tiles
        self.copies = []
        for d, other in self.others(axes):
            self.copies.append(
                pltpu.make_async_remote_copy(
                    src_ref=source,
                    dst_ref=target.at[pl.ds(mine, tiles)],
                    send_sem=self.send_back.at[self.base[stage] + d],
                    recv_sem=self.recv_back.at[self.base[stage] + d],
                    device_id=device_at(*other, self.ny),
                    device_id_type=MESH,
                )
            )
        for copy in self.copies:
            copy.start()
        group = min(8, tiles)

        def keep(i, carry):
            target[pl.ds(mine + i * group, group)] = source[pl.ds(i * group, group)]
            return carry

        lax.fori_loop(0, tiles // group, keep, 0)

    def finish_back(self, i):
        for copy in self.copies:
            copy.wait()


BIG_STAGES = (((0,), True), ((1, 2), True), ((3,), True))
SMALL_STAGES = (((0,), True), ((3,), True), ((1, 2), False))


def sum_scratch(sizes, stages, count, tile, dtype):
    got, held, full = [], [], []
    rest = count
    for axes, shared in stages:
        members = group_size(sizes, axes)
        rest = rest // members if shared else rest
        got.append(pltpu.VMEM((members - 1, rest) + tile, dtype))
        held.append(pltpu.VMEM((rest,) + tile, dtype))
        if shared:
            full.append(pltpu.VMEM((rest,) + tile, dtype))
    return [pltpu.VMEM((count,) + tile, dtype), pltpu.VMEM((count,) + tile, dtype)] + got + held + full[:-1]


def sum_sems(sizes):
    links = sum(group_size(sizes, axes) - 1 for axes, _ in BIG_STAGES)
    return [pltpu.SemaphoreType.DMA((links,)) for _ in range(4)]


TABLES = ("tap_spread", "edge_picker", "halo_placer", "lane_orders", "tap_gather", "valid_mask")


def make_tables():
    return (
        jnp.asarray(tap_spreads(), BF16),
        jnp.asarray(edge_picker(), BF16),
        jnp.asarray(halo_placer(), BF16),
        jnp.asarray(lane_orders(), BF16),
        jnp.asarray(tap_gather(), F32),
        jnp.asarray(valid_mask(), F32),
    )


def forward_block(rb, w1t, w2, s):
    first = rb * BLOCK_ROWS
    for j in range(BLOCK_ROWS):
        rows = pl.ds(first + j, C, stride=ROWS)
        sea = s["land"][pl.ds(first + j, 1), :]
        lanes = slice(j * LANES, (j + 1) * LANES)
        masked = sea * s["filt"][rows, :]
        average = jnp.sum(masked, 0, keepdims=True) * (1.0 / C)
        centred = masked - average
        inverse = lax.rsqrt(jnp.sum(centred * centred, 0, keepdims=True) * (1.0 / C) + epsilon)
        unit = centred * inverse
        s["inverse"][pl.ds(first + j, 1), :] = inverse
        s["unit"][first + j] = unit
        s["normed"][:, lanes] = (unit * s["gain"][...]).astype(BF16)
        s["scaled"][:, lanes] = (sea * s["scale"][...] * s["cot"][rows, :]).astype(BF16)
    for f in range(4):
        part = slice(f * 256, (f + 1) * 256)
        s["hidden"][f % 2] = dot(w1t[part, :], s["normed"][...])
        s["grad_act"][f % 2] = dot(w2[part, :], s["scaled"][...])
        for t in range(16):
            hidden = s["hidden"][f % 2, t * 16 : (t + 1) * 16, :]
            grad_act = s["grad_act"][f % 2, t * 16 : (t + 1) * 16, :]
            lower, bell = halves(hidden)
            rows = slice(f * 256 + t * 16, f * 256 + (t + 1) * 16)
            s["activated"][rb, rows, :] = (hidden * lower).astype(BF16)
            s["grad_hidden"][rb, rows, :] = (grad_act * (lower + hidden * bell * 0.3989422804014327)).astype(BF16)
    s["reduce_sum"][...] += dot_lanes(s["activated"][rb], s["scaled"][...])
    s["expand_sum"][...] += dot_lanes(s["normed"][...], s["grad_hidden"][rb])


def backward_block(rb, w1, w2t, s):
    first = rb * BLOCK_ROWS
    s["branch"][...] = dot(w2t[...], s["activated"][rb])
    s["grad_norm"][...] = dot(w1[...], s["grad_hidden"][rb])
    for j in range(BLOCK_ROWS):
        rows = pl.ds(first + j, C, stride=ROWS)
        sea = s["land"][pl.ds(first + j, 1), :]
        lanes = slice(j * LANES, (j + 1) * LANES)
        branch = sea * s["branch"][:, lanes]
        grad_norm = s["grad_norm"][:, lanes]
        unit = s["unit"][first + j]
        s["scale_sum"][...] += s["cot"][rows, :] * branch
        s["added"][rows, :] = s["scale"][...] * branch
        s["gain_sum"][...] += grad_norm * unit
        grad_hat = grad_norm * s["gain"][...]
        mean = jnp.sum(grad_hat, 0, keepdims=True) * (1.0 / C)
        mean_unit = jnp.sum(grad_hat * unit, 0, keepdims=True) * (1.0 / C)
        grad = (sea * s["inverse"][pl.ds(first + j, 1), :]) * (grad_hat - mean - unit * mean_unit)
        s["grad_wide"][0, rows, :] = grad
        s["grad_wide"][1, pl.ds(ROWS - 1 - first - j, C, stride=ROWS), :] = grad
        s["grad_rows"][first + j] = grad.astype(BF16)


COMPUTE = {
    "land": ((ROWS, LANES), F32),
    "gain": ((C, LANES), F32),
    "scale": ((C, LANES), F32),
    "taps": ((C, LANES), F32),
    "lines": ((2, C, LANES), F32),
    "w1t": ((FF, C), BF16),
    "w2t": ((C, FF), BF16),
    "matrices": ((C, ROWS, 256), BF16),
    "back_matrices": ((C, ROWS, 256), BF16),
    "filt": ((C * ROWS, LANES), F32),
    "cot": ((C * ROWS, LANES), F32),
    "inverse": ((ROWS, LANES), F32),
    "unit": ((ROWS, C, LANES), F32),
    "normed": ((C, BLOCK), BF16),
    "scaled": ((C, BLOCK), BF16),
    "hidden": ((2, 256, BLOCK), F32),
    "grad_act": ((2, 256, BLOCK), F32),
    "activated": ((ROWS // BLOCK_ROWS, FF, BLOCK), BF16),
    "grad_hidden": ((ROWS // BLOCK_ROWS, FF, BLOCK), BF16),
    "branch": ((C, BLOCK), F32),
    "grad_norm": ((C, BLOCK), F32),
    "reduce_sum": ((FF, C), F32),
    "expand_sum": ((C, FF), F32),
    "added": ((C * ROWS, LANES), F32),
    "grad_wide": ((2, C * ROWS, LANES), F32),
    "grad": ((C, ROWS, LANES), BF16),
    "grad_rows": ((ROWS, C, LANES), BF16),
    "edge_rows": ((2, 3, C, LANES), BF16),
    "turned_grad": ((C, ROWS, LANES), BF16),
    "scale_sum": ((C, LANES), F32),
    "gain_sum": ((C, LANES), F32),
    "inner_sums": ((C, LANES), F32),
    "outer_sums": ((2, C // 2, LANES), F32),
}


def prepare(land, depth_kernel, gain, scale, w1, w2, cotangent, s):
    s["land"][...] = land[...].astype(F32)
    for vector, name in ((gain, "gain"), (scale, "scale")):
        for h in range(2):
            row = vector[pl.ds(h, 1), :]
            s[name][h * LANES : (h + 1) * LANES, :] = jnp.broadcast_to(row, (LANES, LANES)).T
    for f in range(4):
        part = slice(f * 256, (f + 1) * 256)
        s["w1t"][part, :] = w1[:, part].T
        s["w2t"][:, part] = w2[part, :].T

    def widen(g, carry):
        rows = pl.ds(pl.multiple_of(g * 256, 256), 256)
        s["cot"][rows, :] = cotangent[pl.ds(g * 16, 16)].reshape(256, LANES).astype(F32)
        return carry

    lax.fori_loop(0, GROUPS, widen, 0)
    for name in ("reduce_sum", "expand_sum", "scale_sum", "gain_sum"):
        s[name][...] = jnp.zeros_like(s[name])


def place_taps(depth_kernel, s):
    taps = depth_kernel[...].astype(F32)
    even = lax.broadcasted_iota(jnp.int32, taps.shape, 0) % 2 == 0
    s["taps"][...] = jnp.zeros_like(s["taps"])
    s["taps"][:, :49] = jnp.where(even, taps, 0.0)
    s["taps"][:, 64 : 64 + 49] = jnp.where(even, 0.0, taps)


def block_kernel(sizes, state, land, depth_kernel, gain, scale, w1, w2, cotangent, *rest):
    tables = dict(zip(TABLES, rest[: len(TABLES)]))
    rest = list(rest[len(TABLES) :])
    updated, state_grad, big_last, small_out = rest[:4]
    rest = rest[4:]

    def take(n):
        out = rest[:n]
        del rest[:n]
        return out

    s = dict(zip(COMPUTE, take(len(COMPUTE))))
    ahead_refs = take(len(halo_scratch()))
    back_refs = take(len(halo_scratch()))
    edge_rows, grad_rows = s["edge_rows"], s["grad_rows"]
    ahead = Halo(state, (edge_rows.at[0], edge_rows.at[1]), tables, *ahead_refs, sems=take(2))
    back = Halo(
        s["grad"], (grad_rows.at[pl.ds(0, 3)], grad_rows.at[pl.ds(ROWS - 3, 3)]), tables, *back_refs, sems=take(2)
    )
    stages = len(BIG_STAGES)
    (big_first,) = take(1)
    big = Sum(sizes, BIG_STAGES, big_first, big_last, take(stages), take(stages), take(2), take(4))
    small_first, small_last = take(2)
    small = Sum(sizes, SMALL_STAGES, small_first, small_last, take(stages), take(stages), take(1), take(4))

    barrier = pltpu.get_barrier_semaphore()
    greeted = [ahead.up, ahead.left, ahead.right]
    for axes, _ in BIG_STAGES:
        greeted += [device_at(*other, sizes[1]) for _, other in big.others(axes)]
    for device in greeted:
        pl.semaphore_signal(barrier, inc=1, device_id=device, device_id_type=MESH)

    @pl.when(ahead.lat > 0)
    def _():
        pl.semaphore_signal(barrier, inc=1, device_id=ahead.down, device_id_type=MESH)

    ahead.pack_rows()
    pl.semaphore_wait(barrier, len(greeted) + jnp.where(ahead.lat > 0, 1, 0))
    ahead.send_rows()
    ahead.pack_columns()
    ahead.send_columns()
    place_taps(depth_kernel, s)
    build_row_matrices(0, s["taps"], tables["tap_spread"], tables["valid_mask"], s["lines"], s["matrices"])
    ahead.columns()

    def put_filtered(c, value):
        s["filt"][pl.ds(pl.multiple_of(c * ROWS, ROWS), ROWS), :] = value

    own_steps = C // 2 // UNROLL_PAIRS
    convolve_own(0, own_steps, state, ahead.edge, s["matrices"], put_filtered)
    prepare(land, depth_kernel, gain, scale, w1, w2, cotangent, s)

    def add_filtered(q, value):
        rows = pl.ds(pl.multiple_of(q * 2 * ROWS, 2 * ROWS), 2 * ROWS)
        s["filt"][rows, :] += value

    def ahead_step(step, carry):
        @pl.when(step == 1)
        def _():
            ahead.rows()
            convolve_beyond(ahead.halo, ahead.halo_edge, s["matrices"], add_filtered)

        forward_block(step + 1 - 2 * (step % 2), s["w1t"], w2, s)
        return carry

    lax.fori_loop(0, ROWS // BLOCK_ROWS, ahead_step, 0)

    def cut_expand(g, carry):
        rows = pl.ds(pl.multiple_of(g * 16, 16), 16)
        for h in range(8):
            big_first[g * 8 + h] = s["expand_sum"][rows, h * LANES : (h + 1) * LANES].astype(BF16)
        return carry

    lax.fori_loop(0, C // 16, cut_expand, 0)

    def cut_reduce(g, carry):
        rows = pl.ds(pl.multiple_of(g * 16, 16), 16)
        for h in range(2):
            big_first[128 + g * 2 + h] = s["reduce_sum"][rows, h * LANES : (h + 1) * LANES].astype(BF16)
        return carry

    lax.fori_loop(0, FF // 16, cut_reduce, 0)
    big.start(0)
    build_row_matrices(
        back.below + 1, s["taps"], tables["tap_spread"], tables["valid_mask"], s["lines"], s["back_matrices"]
    )
    big.finish(0)
    big.start(1)

    def back_step(step, carry):
        @pl.when(step == 2)
        def _():
            back.send_rows()

        backward_block(jnp.where(step < 2, 3 * step, step - 1), w1, s["w2t"], s)
        return carry

    lax.fori_loop(0, ROWS // BLOCK_ROWS, back_step, 0)

    def settle(g, carry):
        rows = pl.ds(pl.multiple_of(g * 128, 128), 128)
        channels = pl.ds(g * 8, 8)
        s["grad"][channels] = s["grad_wide"][0, rows, :].astype(BF16).reshape(8, ROWS, LANES)
        s["turned_grad"][channels] = s["grad_wide"][1, rows, :].astype(BF16).reshape(8, ROWS, LANES)
        updated[channels] = (
            (state[channels].reshape(128, LANES).astype(F32) + s["added"][rows, :]).astype(BF16).reshape(8, ROWS, LANES)
        )
        return carry

    lax.fori_loop(0, C // 8, settle, 0)
    back.pack_columns()
    back.send_columns()

    def sums(part):
        kernel_sums(
            part, s["turned_grad"], state, ahead.edge, ahead.halo, ahead.halo_edge, tables["valid_mask"],
            s["inner_sums"], s["outer_sums"],
        )

    sums(0)
    big.finish(1)
    big.start(2)
    back.columns()
    sums(1)
    sums(2)
    big.finish(2)
    big.start_back(2)
    sums(3)

    exact = lax.Precision.HIGHEST
    gather = tables["tap_gather"]
    pair = lax.broadcasted_iota(jnp.int32, (C // 2, C), 0)
    channel = lax.broadcasted_iota(jnp.int32, (C // 2, C), 1)
    total = dot_lanes(gather[0], s["inner_sums"][...], exact)
    for h in range(2):
        part = dot_lanes(gather[1 + h], s["outer_sums"][h], exact)
        spread = jnp.where(channel == 2 * pair + h, 1.0, 0.0)
        total = total + jnp.dot(part, spread, preferred_element_type=F32, precision=exact)
    row = lax.broadcasted_iota(jnp.int32, (64, LANES), 0)
    total = total + dot_lanes(jnp.where(row == 49, 1.0, 0.0), s["gain_sum"][...], exact)
    total = total + dot_lanes(jnp.where(row == 50, 1.0, 0.0), s["scale_sum"][...], exact)
    for g in range(8):
        for h in range(2):
            small_first[g * 2 + h] = total[g * 8 : (g + 1) * 8, h * LANES : (h + 1) * LANES]
    small.start(0)
    big.finish_back(2)
    big.start_back(1)

    def put_part(c, value):
        s["added"][pl.ds(pl.multiple_of(c * ROWS, ROWS), ROWS), :] = value

    def put_grad(q, value):
        rows = pl.ds(pl.multiple_of(q * 2 * ROWS, 2 * ROWS), 2 * ROWS)
        total = s["cot"][rows, :] + s["added"][rows, :] + value
        state_grad[pl.ds(q * 2, 2)] = total.astype(BF16).reshape(2, ROWS, LANES)

    half = own_steps // 2
    convolve_own(0, half, s["grad"], back.edge, s["back_matrices"], put_part)
    small.finish(0)
    small.start(1)
    convolve_own(half, own_steps, s["grad"], back.edge, s["back_matrices"], put_part)
    back.rows()
    small.finish(1)
    small.start(2)
    convolve_beyond(back.halo, back.halo_edge, s["back_matrices"], put_grad)
    small.finish(2)
    small.start_back(1)
    big.finish_back(1)
    big.start_back(0)
    small.finish_back(1)
    small.start_back(0)
    small.finish_back(0)
    for g in range(8):
        for h in range(2):
            small_out[g * 8 : (g + 1) * 8, h * LANES : (h + 1) * LANES] = small_last[g * 2 + h]
    big.finish_back(0)


def hand_over(factor, updated, state_grad, big, small, *outs):
    updated_out, state_out, kernel_out, gain_out, expand_out, reduce_out, scale_out = outs
    updated_out[...] = updated[...]
    state_out[...] = state_grad[...]

    def paste_expand(g, carry):
        rows = pl.ds(pl.multiple_of(g * 16, 16), 16)
        for h in range(8):
            expand_out[rows, h * LANES : (h + 1) * LANES] = big[g * 8 + h].astype(F32) * factor
        return carry

    lax.fori_loop(0, C // 16, paste_expand, 0)

    def paste_reduce(g, carry):
        rows = pl.ds(pl.multiple_of(g * 16, 16), 16)
        for h in range(2):
            reduce_out[rows, h * LANES : (h + 1) * LANES] = big[128 + g * 2 + h].astype(F32) * factor
        return carry

    lax.fori_loop(0, FF // 16, paste_reduce, 0)
    kernel_out[...] = small[...].T[:, :49] * factor
    gain_out[...] = small[49:50, :] * factor
    scale_out[...] = small[50:51, :] * factor


def local(state, land, depth_kernel, norm_gain, expand_weight, reduce_weight, layer_scale, cotangent):
    ny, nz = lax.axis_size("lon") // 4, lax.axis_size("lat") // 2
    sizes = (2, ny, 4, nz)
    operands = (
        state, land, depth_kernel, norm_gain.reshape(2, LANES), layer_scale.reshape(2, LANES), expand_weight,
        reduce_weight, cotangent, *make_tables(),
    )
    vmem = pl.BlockSpec(memory_space=pltpu.VMEM)
    field = jax.ShapeDtypeStruct((C, ROWS, LANES), BF16)
    out_shape = (
        field,
        field,
        jax.ShapeDtypeStruct((256, 16, LANES), BF16),
        jax.ShapeDtypeStruct((64, C), F32),
    )
    halo_sems = [pltpu.SemaphoreType.DMA((6,)) for _ in range(4)]
    parts = pl.pallas_call(
        functools.partial(block_kernel, sizes),
        out_shape=out_shape,
        in_specs=[vmem] * len(operands),
        out_specs=[vmem] * len(out_shape),
        scratch_shapes=[pltpu.VMEM(shape, dtype) for shape, dtype in COMPUTE.values()]
        + halo_scratch()
        + halo_scratch()
        + halo_sems
        + sum_scratch(sizes, BIG_STAGES, 256, (16, LANES), BF16)[1:]
        + sum_sems(sizes)
        + sum_scratch(sizes, SMALL_STAGES, 16, (8, LANES), F32)
        + sum_sems(sizes),
        compiler_params=pltpu.CompilerParams(
            collective_id=0, has_side_effects=True, vmem_limit_bytes=63 * 2**20
        ),
        name="convnext_block",
    )(*operands)
    factor = float(ROWS * lax.axis_size("lat") * LANES * lax.axis_size("lon")) ** (-0.5)
    vector = jax.ShapeDtypeStruct((1, C), F32)
    updated, state_grad, kernel_grad, gain_grad, expand_grad, reduce_grad, scale_grad = pl.pallas_call(
        functools.partial(hand_over, factor),
        out_shape=(
            field, field, jax.ShapeDtypeStruct((C, 49), F32), vector, jax.ShapeDtypeStruct((C, FF), F32),
            jax.ShapeDtypeStruct((FF, C), F32), vector,
        ),
        in_specs=[vmem] * 4,
        out_specs=[vmem] * 7,
        compiler_params=pltpu.CompilerParams(vmem_limit_bytes=24 * 2**20),
        name="hand_over",
    )(*parts)
    return updated, state_grad, kernel_grad, gain_grad.reshape(C), expand_grad, reduce_grad, scale_grad.reshape(C)


def solution(mesh):
    grid = P(None, "lat", "lon")
    return jax.shard_map(
        local,
        mesh=mesh,
        in_specs=(grid, P("lat", "lon"), P(), P(), P(), P(), P(), grid),
        out_specs=(grid, grid, P(), P(), P(), P(), P()),
        check_vma=False,
    )
```

```python
import functools

import jax
import jax.numpy as jnp
import numpy as np
from jax import lax
from jax.experimental import pallas as pl
from jax.experimental.pallas import tpu as pltpu
from jax.sharding import PartitionSpec as P

epsilon = 1e-06
MESH = pl.DeviceIdType.MESH
BF16 = jnp.bfloat16
F32 = jnp.float32
C, FF, ROWS, LANES = 256, 1024, 16, 128
BLOCK_ROWS = 4
BLOCK = BLOCK_ROWS * LANES
UNROLL_PAIRS = 16
GROUPS = C // 16


def tap_spreads():
    spread = np.zeros((3, LANES, 256), np.float32)
    for variant in range(3):
        for a in range(7):
            for b in range(7):
                tap = a * 7 + b
                turned = 48 - tap if variant else tap
                spread[variant, turned, (b * 16 + a - 3) % LANES] = 1
                spread[variant, turned + 64, (b * 16 + a - 3) % LANES] = 1
                if a == 3:
                    continue
                beyond = tap if variant == 2 and a > 3 else turned
                for h in range(2):
                    lane = b * 16 + 8 * h + (a if a < 3 else a - 16)
                    spread[variant, beyond + 64 * h, LANES + lane % LANES] = 1
    return spread


def edge_picker():
    pick = np.zeros((LANES, 256), np.float32)
    for j in range(3):
        for c in range(16):
            pick[j * 16 + c, c * 16 + j] = 1
            pick[64 + j * 16 + c, c * 16 + 13 + j] = 1
    return pick


def halo_placer():
    place = np.zeros((2, 128, 96), np.float32)
    for c in range(16):
        for j in range(3):
            row = (c // 2) * 16 + (c % 2) * 8
            place[:, row + j, j * 16 + c] = 1
            place[0, row + 3 + j, 48 + j * 16 + c] = 1
            place[1, row + 3 + j, 48 + (2 - j) * 16 + c] = 1
    return place


def lane_orders():
    return np.stack([np.eye(128), np.eye(128)[::-1]]).astype(np.float32)


def tap_gather():
    gather = np.zeros((3, 64, 128), np.float32)
    for a in range(7):
        for b in range(7):
            gather[0, a * 7 + b, b * 16 + a + 12] = 1
            for h in range(2):
                lane = b * 16 + 8 * h + a + (15 if a < 3 else -1)
                if a != 3:
                    gather[1 + h, a * 7 + b, lane] = 1
    return gather


def valid_mask():
    mask = np.zeros((6, ROWS, 128), np.float32)
    for r in range(ROWS):
        for b in range(7):
            for i in range(16):
                if 0 <= i + 3 - r <= 6:
                    mask[0, r, b * 16 + i] = 1
            for h in range(2):
                for j in range(6):
                    p = j if j < 3 else 16 + j
                    if 0 <= p - r <= 6:
                        mask[1 + h, r, b * 16 + 8 * h + j] = 1
    mask[3:] = mask[:3, ::-1]
    return mask


def dot(a, b):
    return jnp.dot(a, b, preferred_element_type=F32)


def dot_lanes(a, b, precision=None):
    return lax.dot_general(a, b, (((1,), (1,)), ((), ())), preferred_element_type=F32, precision=precision)


def dot_first(a, b):
    return lax.dot_general(a, b, (((0,), (0,)), ((), ())), preferred_element_type=F32)


def shifted(tile, edge, lane):
    windows = []
    for b in range(7):
        if b == 3:
            windows.append(tile)
            continue
        mask = lane >= 125 + b if b < 3 else lane < b - 3
        windows.append(pltpu.roll(jnp.where(mask, edge, tile), (3 - b) % LANES, 1))
    return jnp.concatenate(windows, 0)


def gather_columns(g):
    source = lax.broadcasted_iota(jnp.int32, (LANES, LANES), 0)
    target = lax.broadcasted_iota(jnp.int32, (LANES, LANES), 1) - 8 * g
    first = (source < 3) & (target == source)
    last = (source >= 125) & (target == source - 122)
    return jnp.where(first | last, 1.0, 0.0).astype(BF16)


def spread_columns(g, turned):
    source = lax.broadcasted_iota(jnp.int32, (LANES, LANES), 0) - 8 * g
    target = lax.broadcasted_iota(jnp.int32, (LANES, LANES), 1)
    target = jnp.where(turned, LANES - 1 - target, target)
    first = (target < 3) & (source == target)
    last = (target >= 125) & (source == target - 122)
    return jnp.where(first | last, 1.0, 0.0).astype(BF16)


def join_columns(g):
    source = lax.broadcasted_iota(jnp.int32, (2 * LANES, LANES), 0) - 8 * g
    target = lax.broadcasted_iota(jnp.int32, (2 * LANES, LANES), 1)
    last = (target >= 125) & (source == target - 122)
    first = (target < 3) & (source == target + LANES)
    return jnp.where(first | last, 1.0, 0.0).astype(BF16)


def halves(hidden):
    bell = jnp.exp(hidden * hidden * -0.5)
    t = pl.reciprocal(1.0 + 0.23164190 * jnp.abs(hidden), approx=False)
    poly = t * (0.127414796 + t * (-0.142248368 + t * (0.7107068705 + t * (-0.7265760135 + t * 0.5307027145))))
    tail = poly * bell
    return jnp.where(hidden >= 0.0, 1.0 - tail, tail), bell


def device_at(core, y, x, z, ny):
    return {"lon": (x % 2) * (2 * ny) + y * 2 + core, "lat": z * 2 + x // 2}


def my_place(ny):
    lon, lat = lax.axis_index("lon"), lax.axis_index("lat")
    return lon % 2, (lon // 2) % ny, (lat % 2) * 2 + lon // (2 * ny), lat // 2


def group_size(sizes, axes):
    return int(np.prod([sizes[axis] for axis in axes]))


def neighbours_of(place, sizes, axes):
    out = []
    for steps in np.ndindex(*(sizes[axis] for axis in axes)):
        if any(steps):
            other = list(place)
            for axis, step in zip(axes, steps):
                other[axis] = (place[axis] + step) % sizes[axis]
            out.append(tuple(other))
    return out


class Halo:
    def __init__(self, field, rows_out, tables, rows_in, cols, cols_in, corner, corner_in, edge, halo, halo_edge, sems):
        self.field, self.rows_out, self.tables, self.rows_in = field, rows_out, tables, rows_in
        self.cols, self.cols_in, self.corner, self.corner_in = cols, cols_in, corner, corner_in
        self.edge, self.halo, self.halo_edge = edge, halo, halo_edge
        self.send, self.recv = sems
        lon, lat = lax.axis_index("lon"), lax.axis_index("lat")
        nlon, nlat = lax.axis_size("lon"), lax.axis_size("lat")
        self.at_top, self.lat = lat == nlat - 1, lat
        self.below = jnp.where(self.at_top, 1, 0)
        self.up = {"lon": jnp.where(self.at_top, nlon - 1 - lon, lon), "lat": jnp.minimum(lat + 1, nlat - 1)}
        self.down = {"lon": lon, "lat": jnp.maximum(lat - 1, 0)}
        self.left = {"lon": (lon + nlon - 1) % nlon, "lat": lat}
        self.right = {"lon": (lon + 1) % nlon, "lat": lat}

    def copy(self, src, dst, sem, to):
        return pltpu.make_async_remote_copy(
            src_ref=src, dst_ref=dst, send_sem=self.send.at[sem[0]], recv_sem=self.recv.at[sem[1]], device_id=to,
            device_id_type=MESH,
        )

    def row_copies(self):
        low, high = self.rows_out
        return (
            self.copy(high, self.rows_in.at[self.below], (0, self.below), self.up),
            self.copy(low, self.rows_in.at[1], (1, 1), self.down),
            self.copy(high, self.rows_in.at[0], (0, 0), self.up),
        )

    def corner_copies(self):
        return (
            self.copy(self.corner, self.corner_in.at[self.below], (4, 4 + self.below), self.up),
            self.copy(self.corner, self.corner_in.at[1], (5, 5), self.down),
            self.copy(self.corner, self.corner_in.at[0], (4, 4), self.up),
        )

    def column_copies(self):
        return (
            self.copy(self.cols, self.cols_in.at[1], (2, 2), self.left),
            self.copy(self.cols, self.cols_in.at[0], (3, 3), self.right),
        )

    def send_pair(self, copies):
        copies[0].start()

        @pl.when(self.lat > 0)
        def _():
            copies[1].start()

    def await_pair(self, copies):
        copies[0].wait_send()
        copies[1].wait_recv()

        @pl.when(self.lat > 0)
        def _():
            copies[1].wait_send()
            copies[2].wait_recv()

    def pack_rows(self):
        pick = self.tables["edge_picker"]
        low, high = self.rows_out

        def pack(i, carry):
            for u in range(8):
                g = i * 8 + u
                edges = dot(pick[...], self.field[pl.ds(g * 16, 16)].reshape(256, LANES)).astype(BF16)
                channels = pl.ds(pl.multiple_of(g * 16, 16), 16)
                for j in range(3):
                    low[j, channels, :] = edges[j * 16 : (j + 1) * 16]
                    high[j, channels, :] = edges[64 + j * 16 : 64 + (j + 1) * 16]
            return carry

        lax.fori_loop(0, GROUPS // 8, pack, 0)

    def pack_columns(self):
        def pack(i, total):
            for u in range(8):
                g = i * 8 + u
                total = total + dot(self.field[pl.ds(g * 16, 16)].reshape(256, LANES), gather_columns(g))
            return total

        self.cols[...] = lax.fori_loop(0, GROUPS // 8, pack, jnp.zeros((256, LANES), F32)).astype(BF16)

    def send_rows(self):
        self.send_pair(self.row_copies())

    def send_columns(self):
        for copy in self.column_copies():
            copy.start()

    def columns(self):
        for copy in self.column_copies():
            copy.wait()
        pick = self.tables["edge_picker"]

        def put(i, total):
            both = jnp.concatenate([self.cols_in[0], self.cols_in[1]], 1)
            for u in range(8):
                g = i * 8 + u
                tiles = dot(both, join_columns(g)).astype(BF16)
                self.edge[pl.ds(g * 16, 16)] = tiles.reshape(16, ROWS, LANES)
                total = total + dot(dot(pick[...], tiles).astype(BF16), gather_columns(g))
            return total

        self.corner[...] = lax.fori_loop(0, GROUPS // 8, put, jnp.zeros((LANES, LANES), F32)).astype(BF16)
        self.send_pair(self.corner_copies())

    def rows(self):
        self.await_pair(self.row_copies())
        self.await_pair(self.corner_copies())

        @pl.when(self.lat == 0)
        def _():
            self.rows_in[0] = jnp.zeros_like(self.rows_in[0])
            self.corner_in[0] = jnp.zeros_like(self.corner_in[0])

        @pl.when(self.at_top)
        def _():
            turned = dot(self.rows_in[1].reshape(3 * C, LANES), self.tables["lane_orders"][1])
            self.rows_in[1] = turned.astype(BF16).reshape(3, C, LANES)

        placer = self.tables["halo_placer"]

        def put(i, carry):
            place = placer[self.below]
            above = self.corner_in[0, 64:112, :]
            under = jnp.where(self.at_top, self.corner_in[1, 64:112, :], self.corner_in[1, :48, :])
            for u in range(8):
                g = i * 8 + u
                channels = pl.ds(pl.multiple_of(g * 16, 16), 16)
                both = jnp.concatenate([self.rows_in[h, j, channels, :] for h in range(2) for j in range(3)], 0)
                self.halo[pl.ds(g * 8, 8)] = dot(place, both).astype(BF16).reshape(8, ROWS, LANES)
                both = jnp.concatenate(
                    [dot(above, spread_columns(g, False)), dot(under, spread_columns(g, self.at_top))], 0
                ).astype(BF16)
                self.halo_edge[pl.ds(g * 8, 8)] = dot(place, both).astype(BF16).reshape(8, ROWS, LANES)
            return carry

        lax.fori_loop(0, GROUPS // 8, put, 0)


def halo_scratch():
    return [
        pltpu.VMEM((2, 3, C, LANES), BF16),
        pltpu.VMEM((256, LANES), BF16),
        pltpu.VMEM((2, 256, LANES), BF16),
        pltpu.VMEM((LANES, LANES), BF16),
        pltpu.VMEM((2, LANES, LANES), BF16),
        pltpu.VMEM((C, ROWS, LANES), BF16),
        pltpu.VMEM((C // 2, ROWS, LANES), BF16),
        pltpu.VMEM((C // 2, ROWS, LANES), BF16),
    ]


def build_row_matrices(variant, taps, spread, mask, lines, out):
    both = dot(taps[...].astype(BF16), spread[variant])
    lines[0] = both[:, :LANES]
    lines[1] = both[:, LANES:]

    def per_group(g, carry):
        for u in range(16):
            c = g * 16 + u
            for h in range(2):
                line = jnp.broadcast_to(lines[h, pl.ds(c, 1), :], (8, LANES))
                upper = pltpu.roll(line, 0, 1, stride=1, stride_axis=0)
                lower = pltpu.roll(line, 8, 1, stride=1, stride_axis=0)
                kept = jnp.where(mask[h * (1 + u % 2)] > 0.0, jnp.concatenate([upper, lower], 0), 0.0)
                out[c, :, h * LANES : (h + 1) * LANES] = kept.astype(BF16)
        return carry

    lax.fori_loop(0, GROUPS, per_group, 0)


def convolve_own(start, stop, field, edge, matrices, emit):
    lane = lax.broadcasted_iota(jnp.int32, (ROWS, LANES), 1)
    count = 2 * UNROLL_PAIRS

    def step(i, carry):
        for u in range(count):
            c = i * count + u
            emit(c, dot(matrices[c][:, :112], shifted(field[c], edge[c], lane)))
        return carry

    lax.fori_loop(start, stop, step, 0)


def convolve_beyond(halo, halo_edge, matrices, emit):
    lane = lax.broadcasted_iota(jnp.int32, (ROWS, LANES), 1)

    def step(i, carry):
        for u in range(UNROLL_PAIRS):
            q = i * UNROLL_PAIRS + u
            both = matrices[pl.ds(2 * q, 2)].reshape(2 * ROWS, 256)
            emit(q, dot(both[:, 128:240], shifted(halo[q], halo_edge[q], lane)))
        return carry

    lax.fori_loop(0, C // 2 // UNROLL_PAIRS, step, 0)


def kernel_sums(part, grad, field, edge, halo, halo_edge, mask, inner_sums, outer_sums):
    lane = lax.broadcasted_iota(jnp.int32, (ROWS, LANES), 1)
    pad = jnp.zeros((LANES - 112, LANES), BF16)

    def in_line(product, which):
        kept = jnp.where(mask[3 + which] > 0.0, product, 0.0)
        upper = pltpu.roll(kept[:8], 0, 1, stride=1, stride_axis=0)
        lower = pltpu.roll(kept[8:], 8, 1, stride=1, stride_axis=0)
        return jnp.sum(upper + lower, 0, keepdims=True)

    def step(i, carry):
        for u in range(UNROLL_PAIRS):
            q = i * UNROLL_PAIRS + u
            beyond = jnp.concatenate([shifted(halo[q], halo_edge[q], lane), pad], 0)
            both = grad[pl.ds(2 * q, 2)].reshape(2 * ROWS, LANES)
            outer = dot_lanes(both, beyond)
            for k in range(2):
                c = 2 * q + k
                own = jnp.concatenate([shifted(field[c], edge[c], lane), pad], 0)
                inner = dot_lanes(both[k * ROWS : (k + 1) * ROWS], own)
                inner_sums[pl.ds(c, 1), :] = in_line(inner, 0)
                outer_sums[k, pl.ds(q, 1), :] = in_line(outer[k * ROWS : (k + 1) * ROWS], 1 + k)
        return carry

    steps = C // 2 // UNROLL_PAIRS // 4
    lax.fori_loop(part * steps, (part + 1) * steps, step, 0)


class Sum:
    def __init__(self, sizes, stages, first, last, got, held, full, sems):
        self.sizes, self.ny, self.stages = sizes, sizes[1], stages
        self.place = my_place(self.ny)
        self.first, self.last, self.got, self.held, self.full = first, last, got, held, full
        self.send, self.recv, self.send_back, self.recv_back = sems
        self.base = [sum(group_size(sizes, axes) - 1 for axes, _ in stages[:i]) for i in range(len(stages))]
        self.backs = [i for i, (_, shared) in enumerate(stages) if shared]

    def others(self, axes):
        return enumerate(neighbours_of(self.place, self.sizes, axes))

    def index(self, place, axes):
        found = 0
        for axis in axes:
            found = found * self.sizes[axis] + place[axis]
        return found

    def source(self, stage):
        return self.first if stage == 0 else self.held[stage - 1]

    def start(self, stage):
        axes, shared = self.stages[stage]
        source = self.source(stage)
        tiles = self.held[stage].shape[0]
        self.copies = []
        for d, other in self.others(axes):
            self.copies.append(
                pltpu.make_async_remote_copy(
                    src_ref=source.at[pl.ds(self.index(other, axes) * tiles, tiles)] if shared else source,
                    dst_ref=self.got[stage].at[d],
                    send_sem=self.send.at[self.base[stage] + d],
                    recv_sem=self.recv.at[self.base[stage] + d],
                    device_id=device_at(*other, self.ny),
                    device_id_type=MESH,
                )
            )
        for copy in self.copies:
            copy.start()

    def finish(self, stage):
        for copy in self.copies:
            copy.wait()
        axes, shared = self.stages[stage]
        source, got, held = self.source(stage), self.got[stage], self.held[stage]
        tiles = held.shape[0]
        mine = self.index(self.place, axes) * tiles if shared else 0
        group = min(8, tiles)

        def add_up(i, carry):
            total = source[pl.ds(mine + i * group, group)].astype(F32)
            for d in range(group_size(self.sizes, axes) - 1):
                total = total + got[d, pl.ds(i * group, group)].astype(F32)
            held[pl.ds(i * group, group)] = total.astype(held.dtype)
            return carry

        lax.fori_loop(0, tiles // group, add_up, 0)

    def start_back(self, i):
        stage = self.backs[i]
        axes, _ = self.stages[stage]
        source = self.held[-1] if i == len(self.backs) - 1 else self.full[i]
        target = self.last if i == 0 else self.full[i - 1]
        tiles = source.shape[0]
        mine = self.index(self.place, axes) * tiles
        self.copies = []
        for d, other in self.others(axes):
            self.copies.append(
                pltpu.make_async_remote_copy(
                    src_ref=source,
                    dst_ref=target.at[pl.ds(mine, tiles)],
                    send_sem=self.send_back.at[self.base[stage] + d],
                    recv_sem=self.recv_back.at[self.base[stage] + d],
                    device_id=device_at(*other, self.ny),
                    device_id_type=MESH,
                )
            )
        for copy in self.copies:
            copy.start()
        group = min(8, tiles)

        def keep(i, carry):
            target[pl.ds(mine + i * group, group)] = source[pl.ds(i * group, group)]
            return carry

        lax.fori_loop(0, tiles // group, keep, 0)

    def finish_back(self, i):
        for copy in self.copies:
            copy.wait()


BIG_STAGES = (((0,), True), ((1, 2), True), ((3,), True))
SMALL_STAGES = (((0,), True), ((3,), True), ((1, 2), False))


def sum_scratch(sizes, stages, count, tile, dtype):
    got, held, full = [], [], []
    rest = count
    for axes, shared in stages:
        members = group_size(sizes, axes)
        rest = rest // members if shared else rest
        got.append(pltpu.VMEM((members - 1, rest) + tile, dtype))
        held.append(pltpu.VMEM((rest,) + tile, dtype))
        if shared:
            full.append(pltpu.VMEM((rest,) + tile, dtype))
    return [pltpu.VMEM((count,) + tile, dtype), pltpu.VMEM((count,) + tile, dtype)] + got + held + full[:-1]


def sum_sems(sizes):
    links = sum(group_size(sizes, axes) - 1 for axes, _ in BIG_STAGES)
    return [pltpu.SemaphoreType.DMA((links,)) for _ in range(4)]


TABLES = ("tap_spread", "edge_picker", "halo_placer", "lane_orders", "tap_gather", "valid_mask")


def make_tables():
    return (
        jnp.asarray(tap_spreads(), BF16),
        jnp.asarray(edge_picker(), BF16),
        jnp.asarray(halo_placer(), BF16),
        jnp.asarray(lane_orders(), BF16),
        jnp.asarray(tap_gather(), F32),
        jnp.asarray(valid_mask(), F32),
    )


def forward_block(rb, w1t, w2, s):
    first = rb * BLOCK_ROWS
    for j in range(BLOCK_ROWS):
        rows = pl.ds(first + j, C, stride=ROWS)
        sea = s["land"][pl.ds(first + j, 1), :]
        lanes = slice(j * LANES, (j + 1) * LANES)
        masked = sea * s["filt"][rows, :]
        average = jnp.sum(masked, 0, keepdims=True) * (1.0 / C)
        centred = masked - average
        inverse = lax.rsqrt(jnp.sum(centred * centred, 0, keepdims=True) * (1.0 / C) + epsilon)
        unit = centred * inverse
        s["inverse"][pl.ds(first + j, 1), :] = inverse
        s["unit"][first + j] = unit
        s["normed"][:, lanes] = (unit * s["gain"][...]).astype(BF16)
        s["scaled"][:, lanes] = (sea * s["scale"][...] * s["cot"][rows, :]).astype(BF16)
    for f in range(4):
        part = slice(f * 256, (f + 1) * 256)
        s["hidden"][f % 2] = dot(w1t[part, :], s["normed"][...])
        s["grad_act"][f % 2] = dot(w2[part, :], s["scaled"][...])
        for t in range(16):
            hidden = s["hidden"][f % 2, t * 16 : (t + 1) * 16, :]
            grad_act = s["grad_act"][f % 2, t * 16 : (t + 1) * 16, :]
            lower, bell = halves(hidden)
            rows = slice(f * 256 + t * 16, f * 256 + (t + 1) * 16)
            s["activated"][rb, rows, :] = (hidden * lower).astype(BF16)
            s["grad_hidden"][rb, rows, :] = (grad_act * (lower + hidden * bell * 0.3989422804014327)).astype(BF16)
    s["reduce_sum"][...] += dot_lanes(s["activated"][rb], s["scaled"][...])
    s["expand_sum"][...] += dot_lanes(s["normed"][...], s["grad_hidden"][rb])


def backward_block(rb, w1, w2t, s):
    first = rb * BLOCK_ROWS
    s["branch"][...] = dot(w2t[...], s["activated"][rb])
    s["grad_norm"][...] = dot(w1[...], s["grad_hidden"][rb])
    for j in range(BLOCK_ROWS):
        rows = pl.ds(first + j, C, stride=ROWS)
        sea = s["land"][pl.ds(first + j, 1), :]
        lanes = slice(j * LANES, (j + 1) * LANES)
        branch = sea * s["branch"][:, lanes]
        grad_norm = s["grad_norm"][:, lanes]
        unit = s["unit"][first + j]
        s["scale_sum"][...] += s["cot"][rows, :] * branch
        s["added"][rows, :] = s["scale"][...] * branch
        s["gain_sum"][...] += grad_norm * unit
        grad_hat = grad_norm * s["gain"][...]
        mean = jnp.sum(grad_hat, 0, keepdims=True) * (1.0 / C)
        mean_unit = jnp.sum(grad_hat * unit, 0, keepdims=True) * (1.0 / C)
        grad = (sea * s["inverse"][pl.ds(first + j, 1), :]) * (grad_hat - mean - unit * mean_unit)
        s["grad_wide"][0, rows, :] = grad
        s["grad_wide"][1, pl.ds(ROWS - 1 - first - j, C, stride=ROWS), :] = grad
        s["grad_rows"][first + j] = grad.astype(BF16)


COMPUTE = {
    "land": ((ROWS, LANES), F32),
    "gain": ((C, LANES), F32),
    "scale": ((C, LANES), F32),
    "taps": ((C, LANES), F32),
    "lines": ((2, C, LANES), F32),
    "tap_rows": ((LANES, C), F32),
    "w1t": ((FF, C), BF16),
    "w2t": ((C, FF), BF16),
    "matrices": ((C, ROWS, 256), BF16),
    "back_matrices": ((C, ROWS, 256), BF16),
    "filt": ((C * ROWS, LANES), F32),
    "cot": ((C * ROWS, LANES), F32),
    "inverse": ((ROWS, LANES), F32),
    "unit": ((ROWS, C, LANES), F32),
    "normed": ((C, BLOCK), BF16),
    "scaled": ((C, BLOCK), BF16),
    "hidden": ((2, 256, BLOCK), F32),
    "grad_act": ((2, 256, BLOCK), F32),
    "activated": ((ROWS // BLOCK_ROWS, FF, BLOCK), BF16),
    "grad_hidden": ((ROWS // BLOCK_ROWS, FF, BLOCK), BF16),
    "branch": ((C, BLOCK), F32),
    "grad_norm": ((C, BLOCK), F32),
    "reduce_sum": ((FF, C), F32),
    "expand_sum": ((C, FF), F32),
    "added": ((C * ROWS, LANES), F32),
    "grad_wide": ((2, C * ROWS, LANES), F32),
    "grad": ((C, ROWS, LANES), BF16),
    "grad_rows": ((ROWS, C, LANES), BF16),
    "edge_rows": ((2, 3, C, LANES), BF16),
    "turned_grad": ((C, ROWS, LANES), BF16),
    "scale_sum": ((C, LANES), F32),
    "gain_sum": ((C, LANES), F32),
    "inner_sums": ((C, LANES), F32),
    "outer_sums": ((2, C // 2, LANES), F32),
}


def prepare(land, depth_kernel, gain, scale, w1, w2, cotangent, s):
    s["land"][...] = land[...].astype(F32)
    for vector, name in ((gain, "gain"), (scale, "scale")):
        for h in range(2):
            row = vector[pl.ds(h, 1), :]
            s[name][h * LANES : (h + 1) * LANES, :] = jnp.broadcast_to(row, (LANES, LANES)).T
    for f in range(4):
        part = slice(f * 256, (f + 1) * 256)
        s["w1t"][part, :] = w1[:, part].T
        s["w2t"][:, part] = w2[part, :].T

    def widen(g, carry):
        rows = pl.ds(pl.multiple_of(g * 256, 256), 256)
        s["cot"][rows, :] = cotangent[pl.ds(g * 16, 16)].reshape(256, LANES).astype(F32)
        return carry

    lax.fori_loop(0, GROUPS, widen, 0)
    for name in ("reduce_sum", "expand_sum", "scale_sum", "gain_sum"):
        s[name][...] = jnp.zeros_like(s[name])


def place_taps(depth_kernel, s):
    taps = depth_kernel[...].astype(F32)
    even = lax.broadcasted_iota(jnp.int32, taps.shape, 1) % 2 == 0
    s["tap_rows"][...] = jnp.zeros_like(s["tap_rows"])
    s["tap_rows"][:49, :] = jnp.where(even, taps, 0.0)
    s["tap_rows"][64 : 64 + 49, :] = jnp.where(even, 0.0, taps)
    s["taps"][...] = s["tap_rows"][...].T


def block_kernel(sizes, state, land, depth_kernel, gain, scale, w1, w2, cotangent, *rest):
    tables = dict(zip(TABLES, rest[: len(TABLES)]))
    rest = list(rest[len(TABLES) :])
    updated, state_grad, big_last, small_out = rest[:4]
    rest = rest[4:]

    def take(n):
        out = rest[:n]
        del rest[:n]
        return out

    s = dict(zip(COMPUTE, take(len(COMPUTE))))
    ahead_refs = take(len(halo_scratch()))
    back_refs = take(len(halo_scratch()))
    edge_rows, grad_rows = s["edge_rows"], s["grad_rows"]
    ahead = Halo(state, (edge_rows.at[0], edge_rows.at[1]), tables, *ahead_refs, sems=take(2))
    back = Halo(
        s["grad"], (grad_rows.at[pl.ds(0, 3)], grad_rows.at[pl.ds(ROWS - 3, 3)]), tables, *back_refs, sems=take(2)
    )
    stages = len(BIG_STAGES)
    (big_first,) = take(1)
    big = Sum(sizes, BIG_STAGES, big_first, big_last, take(stages), take(stages), take(2), take(4))
    small_first, small_last = take(2)
    small = Sum(sizes, SMALL_STAGES, small_first, small_last, take(stages), take(stages), take(1), take(4))

    barrier = pltpu.get_barrier_semaphore()
    greeted = [ahead.up, ahead.left, ahead.right]
    for axes, _ in BIG_STAGES:
        greeted += [device_at(*other, sizes[1]) for _, other in big.others(axes)]
    for device in greeted:
        pl.semaphore_signal(barrier, inc=1, device_id=device, device_id_type=MESH)

    @pl.when(ahead.lat > 0)
    def _():
        pl.semaphore_signal(barrier, inc=1, device_id=ahead.down, device_id_type=MESH)

    ahead.pack_rows()
    pl.semaphore_wait(barrier, len(greeted) + jnp.where(ahead.lat > 0, 1, 0))
    ahead.send_rows()
    ahead.pack_columns()
    ahead.send_columns()
    place_taps(depth_kernel, s)
    build_row_matrices(0, s["taps"], tables["tap_spread"], tables["valid_mask"], s["lines"], s["matrices"])
    ahead.columns()

    def put_filtered(c, value):
        s["filt"][pl.ds(pl.multiple_of(c * ROWS, ROWS), ROWS), :] = value

    own_steps = C // 2 // UNROLL_PAIRS
    convolve_own(0, own_steps, state, ahead.edge, s["matrices"], put_filtered)
    prepare(land, depth_kernel, gain, scale, w1, w2, cotangent, s)

    def add_filtered(q, value):
        rows = pl.ds(pl.multiple_of(q * 2 * ROWS, 2 * ROWS), 2 * ROWS)
        s["filt"][rows, :] += value

    def ahead_step(step, carry):
        @pl.when(step == 1)
        def _():
            ahead.rows()
            convolve_beyond(ahead.halo, ahead.halo_edge, s["matrices"], add_filtered)

        forward_block(step + 1 - 2 * (step % 2), s["w1t"], w2, s)
        return carry

    lax.fori_loop(0, ROWS // BLOCK_ROWS, ahead_step, 0)

    def cut_expand(g, carry):
        rows = pl.ds(pl.multiple_of(g * 16, 16), 16)
        for h in range(8):
            big_first[g * 8 + h] = s["expand_sum"][rows, h * LANES : (h + 1) * LANES].astype(BF16)
        return carry

    lax.fori_loop(0, C // 16, cut_expand, 0)

    def cut_reduce(g, carry):
        rows = pl.ds(pl.multiple_of(g * 16, 16), 16)
        for h in range(2):
            big_first[128 + g * 2 + h] = s["reduce_sum"][rows, h * LANES : (h + 1) * LANES].astype(BF16)
        return carry

    lax.fori_loop(0, FF // 16, cut_reduce, 0)
    big.start(0)
    build_row_matrices(
        back.below + 1, s["taps"], tables["tap_spread"], tables["valid_mask"], s["lines"], s["back_matrices"]
    )
    big.finish(0)
    big.start(1)

    def back_step(step, carry):
        @pl.when(step == 2)
        def _():
            back.send_rows()

        backward_block(jnp.where(step < 2, 3 * step, step - 1), w1, s["w2t"], s)
        return carry

    lax.fori_loop(0, ROWS // BLOCK_ROWS, back_step, 0)

    def settle(g, carry):
        rows = pl.ds(pl.multiple_of(g * 128, 128), 128)
        channels = pl.ds(g * 8, 8)
        s["grad"][channels] = s["grad_wide"][0, rows, :].astype(BF16).reshape(8, ROWS, LANES)
        s["turned_grad"][channels] = s["grad_wide"][1, rows, :].astype(BF16).reshape(8, ROWS, LANES)
        updated[channels] = (
            (state[channels].reshape(128, LANES).astype(F32) + s["added"][rows, :]).astype(BF16).reshape(8, ROWS, LANES)
        )
        return carry

    lax.fori_loop(0, C // 8, settle, 0)
    back.pack_columns()
    back.send_columns()

    def sums(part):
        kernel_sums(
            part, s["turned_grad"], state, ahead.edge, ahead.halo, ahead.halo_edge, tables["valid_mask"],
            s["inner_sums"], s["outer_sums"],
        )

    sums(0)
    big.finish(1)
    big.start(2)
    back.columns()
    sums(1)
    sums(2)
    big.finish(2)
    big.start_back(2)
    sums(3)

    exact = lax.Precision.HIGHEST
    gather = tables["tap_gather"]
    pair = lax.broadcasted_iota(jnp.int32, (C // 2, C), 0)
    channel = lax.broadcasted_iota(jnp.int32, (C // 2, C), 1)
    total = dot_lanes(gather[0], s["inner_sums"][...], exact)
    for h in range(2):
        part = dot_lanes(gather[1 + h], s["outer_sums"][h], exact)
        spread = jnp.where(channel == 2 * pair + h, 1.0, 0.0)
        total = total + jnp.dot(part, spread, preferred_element_type=F32, precision=exact)
    row = lax.broadcasted_iota(jnp.int32, (64, LANES), 0)
    total = total + dot_lanes(jnp.where(row == 49, 1.0, 0.0), s["gain_sum"][...], exact)
    total = total + dot_lanes(jnp.where(row == 50, 1.0, 0.0), s["scale_sum"][...], exact)
    for g in range(8):
        for h in range(2):
            small_first[g * 2 + h] = total[g * 8 : (g + 1) * 8, h * LANES : (h + 1) * LANES]
    small.start(0)
    big.finish_back(2)
    big.start_back(1)

    def put_part(c, value):
        s["added"][pl.ds(pl.multiple_of(c * ROWS, ROWS), ROWS), :] = value

    def put_grad(q, value):
        rows = pl.ds(pl.multiple_of(q * 2 * ROWS, 2 * ROWS), 2 * ROWS)
        total = s["cot"][rows, :] + s["added"][rows, :] + value
        state_grad[pl.ds(q * 2, 2)] = total.astype(BF16).reshape(2, ROWS, LANES)

    half = own_steps // 2
    convolve_own(0, half, s["grad"], back.edge, s["back_matrices"], put_part)
    small.finish(0)
    small.start(1)
    convolve_own(half, own_steps, s["grad"], back.edge, s["back_matrices"], put_part)
    back.rows()
    small.finish(1)
    small.start(2)
    convolve_beyond(back.halo, back.halo_edge, s["back_matrices"], put_grad)
    small.finish(2)
    small.start_back(1)
    big.finish_back(1)
    big.start_back(0)
    small.finish_back(1)
    small.start_back(0)
    small.finish_back(0)
    for g in range(8):
        for h in range(2):
            small_out[g * 8 : (g + 1) * 8, h * LANES : (h + 1) * LANES] = small_last[g * 2 + h]
    big.finish_back(0)


def hand_over(factor, big, small, *outs):
    kernel_out, gain_out, expand_out, reduce_out, scale_out = outs

    def paste_expand(g, carry):
        rows = pl.ds(pl.multiple_of(g * 16, 16), 16)
        for h in range(8):
            expand_out[rows, h * LANES : (h + 1) * LANES] = big[g * 8 + h].astype(F32) * factor
        return carry

    lax.fori_loop(0, C // 16, paste_expand, 0)

    def paste_reduce(g, carry):
        rows = pl.ds(pl.multiple_of(g * 16, 16), 16)
        for h in range(2):
            reduce_out[rows, h * LANES : (h + 1) * LANES] = big[128 + g * 2 + h].astype(F32) * factor
        return carry

    lax.fori_loop(0, FF // 16, paste_reduce, 0)
    kernel_out[...] = small[:49, :] * factor
    gain_out[...] = small[49:50, :] * factor
    scale_out[...] = small[50:51, :] * factor


def local(state, land, depth_kernel, norm_gain, expand_weight, reduce_weight, layer_scale, cotangent):
    ny, nz = lax.axis_size("lon") // 4, lax.axis_size("lat") // 2
    sizes = (2, ny, 4, nz)
    operands = (
        state, land, depth_kernel.T, norm_gain.reshape(2, LANES), layer_scale.reshape(2, LANES), expand_weight,
        reduce_weight, cotangent, *make_tables(),
    )
    vmem = pl.BlockSpec(memory_space=pltpu.VMEM)
    field = jax.ShapeDtypeStruct((C, ROWS, LANES), BF16)
    out_shape = (
        field,
        field,
        jax.ShapeDtypeStruct((256, 16, LANES), BF16),
        jax.ShapeDtypeStruct((64, C), F32),
    )
    halo_sems = [pltpu.SemaphoreType.DMA((6,)) for _ in range(4)]
    updated, state_grad, *parts = pl.pallas_call(
        functools.partial(block_kernel, sizes),
        out_shape=out_shape,
        in_specs=[vmem] * len(operands),
        out_specs=[vmem] * len(out_shape),
        scratch_shapes=[pltpu.VMEM(shape, dtype) for shape, dtype in COMPUTE.values()]
        + halo_scratch()
        + halo_scratch()
        + halo_sems
        + sum_scratch(sizes, BIG_STAGES, 256, (16, LANES), BF16)[1:]
        + sum_sems(sizes)
        + sum_scratch(sizes, SMALL_STAGES, 16, (8, LANES), F32)
        + sum_sems(sizes),
        compiler_params=pltpu.CompilerParams(
            collective_id=0, has_side_effects=True, vmem_limit_bytes=63 * 2**20
        ),
        name="convnext_block",
    )(*operands)
    factor = float(ROWS * lax.axis_size("lat") * LANES * lax.axis_size("lon")) ** (-0.5)
    vector = jax.ShapeDtypeStruct((1, C), F32)
    kernel_grad, gain_grad, expand_grad, reduce_grad, scale_grad = pl.pallas_call(
        functools.partial(hand_over, factor),
        out_shape=(
            jax.ShapeDtypeStruct((49, C), F32), vector, jax.ShapeDtypeStruct((C, FF), F32),
            jax.ShapeDtypeStruct((FF, C), F32), vector,
        ),
        in_specs=[vmem] * 2,
        out_specs=[vmem] * 5,
        compiler_params=pltpu.CompilerParams(vmem_limit_bytes=24 * 2**20),
        name="hand_over",
    )(*parts)
    return updated, state_grad, kernel_grad.T, gain_grad.reshape(C), expand_grad, reduce_grad, scale_grad.reshape(C)


def solution(mesh):
    grid = P(None, "lat", "lon")
    return jax.shard_map(
        local,
        mesh=mesh,
        in_specs=(grid, P("lat", "lon"), P(), P(), P(), P(), P(), grid),
        out_specs=(grid, grid, P(), P(), P(), P(), P()),
        check_vma=False,
    )
```

```python
import functools

import jax
import jax.numpy as jnp
import numpy as np
from jax import lax
from jax.experimental import pallas as pl
from jax.experimental.pallas import tpu as pltpu
from jax.sharding import PartitionSpec as P

epsilon = 1e-06
MESH = pl.DeviceIdType.MESH
BF16 = jnp.bfloat16
F32 = jnp.float32
C, FF, ROWS, LANES = 256, 1024, 16, 128
BLOCK_ROWS = 4
BLOCK = BLOCK_ROWS * LANES
UNROLL_PAIRS = 16
GROUPS = C // 16


def tap_spreads():
    spread = np.zeros((3, LANES, 256), np.float32)
    for variant in range(3):
        for a in range(7):
            for b in range(7):
                tap = a * 7 + b
                turned = 48 - tap if variant else tap
                spread[variant, turned, (b * 16 + a - 3) % LANES] = 1
                spread[variant, turned + 64, (b * 16 + a - 3) % LANES] = 1
                if a == 3:
                    continue
                beyond = tap if variant == 2 and a > 3 else turned
                for h in range(2):
                    lane = b * 16 + 8 * h + (a if a < 3 else a - 16)
                    spread[variant, beyond + 64 * h, LANES + lane % LANES] = 1
    return spread


def edge_picker():
    pick = np.zeros((LANES, 256), np.float32)
    for j in range(3):
        for c in range(16):
            pick[j * 16 + c, c * 16 + j] = 1
            pick[64 + j * 16 + c, c * 16 + 13 + j] = 1
    return pick


def halo_placer():
    place = np.zeros((2, 128, 96), np.float32)
    for c in range(16):
        for j in range(3):
            row = (c // 2) * 16 + (c % 2) * 8
            place[:, row + j, j * 16 + c] = 1
            place[0, row + 3 + j, 48 + j * 16 + c] = 1
            place[1, row + 3 + j, 48 + (2 - j) * 16 + c] = 1
    return place


def lane_orders():
    return np.stack([np.eye(128), np.eye(128)[::-1]]).astype(np.float32)


def tap_gather():
    gather = np.zeros((3, 64, 128), np.float32)
    for a in range(7):
        for b in range(7):
            gather[0, a * 7 + b, b * 16 + a + 12] = 1
            for h in range(2):
                lane = b * 16 + 8 * h + a + (15 if a < 3 else -1)
                if a != 3:
                    gather[1 + h, a * 7 + b, lane] = 1
    return gather


def valid_mask():
    mask = np.zeros((6, ROWS, 128), np.float32)
    for r in range(ROWS):
        for b in range(7):
            for i in range(16):
                if 0 <= i + 3 - r <= 6:
                    mask[0, r, b * 16 + i] = 1
            for h in range(2):
                for j in range(6):
                    p = j if j < 3 else 16 + j
                    if 0 <= p - r <= 6:
                        mask[1 + h, r, b * 16 + 8 * h + j] = 1
    mask[3:] = mask[:3, ::-1]
    return mask


def dot(a, b):
    return jnp.dot(a, b, preferred_element_type=F32)


def dot_lanes(a, b, precision=None):
    return lax.dot_general(a, b, (((1,), (1,)), ((), ())), preferred_element_type=F32, precision=precision)


def dot_first(a, b):
    return lax.dot_general(a, b, (((0,), (0,)), ((), ())), preferred_element_type=F32)


def shifted(tile, edge, lane):
    windows = []
    for b in range(7):
        if b == 3:
            windows.append(tile)
            continue
        mask = lane >= 125 + b if b < 3 else lane < b - 3
        windows.append(pltpu.roll(jnp.where(mask, edge, tile), (3 - b) % LANES, 1))
    return jnp.concatenate(windows, 0)


def gather_columns(g):
    source = lax.broadcasted_iota(jnp.int32, (LANES, LANES), 0)
    target = lax.broadcasted_iota(jnp.int32, (LANES, LANES), 1) - 8 * g
    first = (source < 3) & (target == source)
    last = (source >= 125) & (target == source - 122)
    return jnp.where(first | last, 1.0, 0.0).astype(BF16)


def spread_columns(g, turned):
    source = lax.broadcasted_iota(jnp.int32, (LANES, LANES), 0) - 8 * g
    target = lax.broadcasted_iota(jnp.int32, (LANES, LANES), 1)
    target = jnp.where(turned, LANES - 1 - target, target)
    first = (target < 3) & (source == target)
    last = (target >= 125) & (source == target - 122)
    return jnp.where(first | last, 1.0, 0.0).astype(BF16)


def join_columns(g):
    source = lax.broadcasted_iota(jnp.int32, (2 * LANES, LANES), 0) - 8 * g
    target = lax.broadcasted_iota(jnp.int32, (2 * LANES, LANES), 1)
    last = (target >= 125) & (source == target - 122)
    first = (target < 3) & (source == target + LANES)
    return jnp.where(first | last, 1.0, 0.0).astype(BF16)


def halves(hidden):
    bell = jnp.exp(hidden * hidden * -0.5)
    t = pl.reciprocal(1.0 + 0.23164190 * jnp.abs(hidden), approx=False)
    poly = t * (0.127414796 + t * (-0.142248368 + t * (0.7107068705 + t * (-0.7265760135 + t * 0.5307027145))))
    tail = poly * bell
    return jnp.where(hidden >= 0.0, 1.0 - tail, tail), bell


def device_at(core, y, x, z, ny):
    return {"lon": (x % 2) * (2 * ny) + y * 2 + core, "lat": z * 2 + x // 2}


def my_place(ny):
    lon, lat = lax.axis_index("lon"), lax.axis_index("lat")
    return lon % 2, (lon // 2) % ny, (lat % 2) * 2 + lon // (2 * ny), lat // 2


def group_size(sizes, axes):
    return int(np.prod([sizes[axis] for axis in axes]))


def neighbours_of(place, sizes, axes):
    out = []
    for steps in np.ndindex(*(sizes[axis] for axis in axes)):
        if any(steps):
            other = list(place)
            for axis, step in zip(axes, steps):
                other[axis] = (place[axis] + step) % sizes[axis]
            out.append(tuple(other))
    return out


class Halo:
    def __init__(self, field, rows_out, tables, rows_in, cols, cols_in, corner, corner_in, edge, halo, halo_edge, sems):
        self.field, self.rows_out, self.tables, self.rows_in = field, rows_out, tables, rows_in
        self.cols, self.cols_in, self.corner, self.corner_in = cols, cols_in, corner, corner_in
        self.edge, self.halo, self.halo_edge = edge, halo, halo_edge
        self.send, self.recv = sems
        lon, lat = lax.axis_index("lon"), lax.axis_index("lat")
        nlon, nlat = lax.axis_size("lon"), lax.axis_size("lat")
        self.at_top, self.lat = lat == nlat - 1, lat
        self.below = jnp.where(self.at_top, 1, 0)
        self.up = {"lon": jnp.where(self.at_top, nlon - 1 - lon, lon), "lat": jnp.minimum(lat + 1, nlat - 1)}
        self.down = {"lon": lon, "lat": jnp.maximum(lat - 1, 0)}
        self.left = {"lon": (lon + nlon - 1) % nlon, "lat": lat}
        self.right = {"lon": (lon + 1) % nlon, "lat": lat}

    def copy(self, src, dst, sem, to):
        return pltpu.make_async_remote_copy(
            src_ref=src, dst_ref=dst, send_sem=self.send.at[sem[0]], recv_sem=self.recv.at[sem[1]], device_id=to,
            device_id_type=MESH,
        )

    def row_copies(self):
        low, high = self.rows_out
        return (
            self.copy(high, self.rows_in.at[self.below], (0, self.below), self.up),
            self.copy(low, self.rows_in.at[1], (1, 1), self.down),
            self.copy(high, self.rows_in.at[0], (0, 0), self.up),
        )

    def corner_copies(self):
        return (
            self.copy(self.corner, self.corner_in.at[self.below], (4, 4 + self.below), self.up),
            self.copy(self.corner, self.corner_in.at[1], (5, 5), self.down),
            self.copy(self.corner, self.corner_in.at[0], (4, 4), self.up),
        )

    def column_copies(self):
        return (
            self.copy(self.cols, self.cols_in.at[1], (2, 2), self.left),
            self.copy(self.cols, self.cols_in.at[0], (3, 3), self.right),
        )

    def send_pair(self, copies):
        copies[0].start()

        @pl.when(self.lat > 0)
        def _():
            copies[1].start()

    def await_pair(self, copies):
        copies[0].wait_send()
        copies[1].wait_recv()

        @pl.when(self.lat > 0)
        def _():
            copies[1].wait_send()
            copies[2].wait_recv()

    def pack_rows(self):
        pick = self.tables["edge_picker"]
        low, high = self.rows_out

        def pack(i, carry):
            for u in range(8):
                g = i * 8 + u
                edges = dot(pick[...], self.field[pl.ds(g * 16, 16)].reshape(256, LANES)).astype(BF16)
                channels = pl.ds(pl.multiple_of(g * 16, 16), 16)
                for j in range(3):
                    low[j, channels, :] = edges[j * 16 : (j + 1) * 16]
                    high[j, channels, :] = edges[64 + j * 16 : 64 + (j + 1) * 16]
            return carry

        lax.fori_loop(0, GROUPS // 8, pack, 0)

    def pack_columns(self):
        def pack(i, total):
            for u in range(8):
                g = i * 8 + u
                total = total + dot(self.field[pl.ds(g * 16, 16)].reshape(256, LANES), gather_columns(g))
            return total

        self.cols[...] = lax.fori_loop(0, GROUPS // 8, pack, jnp.zeros((256, LANES), F32)).astype(BF16)

    def send_rows(self):
        self.send_pair(self.row_copies())

    def send_columns(self):
        for copy in self.column_copies():
            copy.start()

    def columns(self):
        for copy in self.column_copies():
            copy.wait()
        pick = self.tables["edge_picker"]

        def put(i, total):
            both = jnp.concatenate([self.cols_in[0], self.cols_in[1]], 1)
            for u in range(8):
                g = i * 8 + u
                tiles = dot(both, join_columns(g)).astype(BF16)
                self.edge[pl.ds(g * 16, 16)] = tiles.reshape(16, ROWS, LANES)
                total = total + dot(dot(pick[...], tiles).astype(BF16), gather_columns(g))
            return total

        self.corner[...] = lax.fori_loop(0, GROUPS // 8, put, jnp.zeros((LANES, LANES), F32)).astype(BF16)
        self.send_pair(self.corner_copies())

    def rows(self):
        self.await_pair(self.row_copies())
        self.await_pair(self.corner_copies())

        @pl.when(self.lat == 0)
        def _():
            self.rows_in[0] = jnp.zeros_like(self.rows_in[0])
            self.corner_in[0] = jnp.zeros_like(self.corner_in[0])

        @pl.when(self.at_top)
        def _():
            turned = dot(self.rows_in[1].reshape(3 * C, LANES), self.tables["lane_orders"][1])
            self.rows_in[1] = turned.astype(BF16).reshape(3, C, LANES)

        placer = self.tables["halo_placer"]

        def put(i, carry):
            place = placer[self.below]
            above = self.corner_in[0, 64:112, :]
            under = jnp.where(self.at_top, self.corner_in[1, 64:112, :], self.corner_in[1, :48, :])
            for u in range(8):
                g = i * 8 + u
                channels = pl.ds(pl.multiple_of(g * 16, 16), 16)
                both = jnp.concatenate([self.rows_in[h, j, channels, :] for h in range(2) for j in range(3)], 0)
                self.halo[pl.ds(g * 8, 8)] = dot(place, both).astype(BF16).reshape(8, ROWS, LANES)
                both = jnp.concatenate(
                    [dot(above, spread_columns(g, False)), dot(under, spread_columns(g, self.at_top))], 0
                ).astype(BF16)
                self.halo_edge[pl.ds(g * 8, 8)] = dot(place, both).astype(BF16).reshape(8, ROWS, LANES)
            return carry

        lax.fori_loop(0, GROUPS // 8, put, 0)


def halo_scratch():
    return [
        pltpu.VMEM((2, 3, C, LANES), BF16),
        pltpu.VMEM((256, LANES), BF16),
        pltpu.VMEM((2, 256, LANES), BF16),
        pltpu.VMEM((LANES, LANES), BF16),
        pltpu.VMEM((2, LANES, LANES), BF16),
        pltpu.VMEM((C, ROWS, LANES), BF16),
        pltpu.VMEM((C // 2, ROWS, LANES), BF16),
        pltpu.VMEM((C // 2, ROWS, LANES), BF16),
    ]


def build_row_matrices(variant, taps, spread, mask, lines, out):
    both = dot(taps[...].astype(BF16), spread[variant])
    lines[0] = both[:, :LANES]
    lines[1] = both[:, LANES:]

    def per_group(g, carry):
        for u in range(16):
            c = g * 16 + u
            for h in range(2):
                line = jnp.broadcast_to(lines[h, pl.ds(c, 1), :], (8, LANES))
                upper = pltpu.roll(line, 0, 1, stride=1, stride_axis=0)
                lower = pltpu.roll(line, 8, 1, stride=1, stride_axis=0)
                kept = jnp.where(mask[h * (1 + u % 2)] > 0.0, jnp.concatenate([upper, lower], 0), 0.0)
                out[c, :, h * LANES : (h + 1) * LANES] = kept.astype(BF16)
        return carry

    lax.fori_loop(0, GROUPS, per_group, 0)


def convolve_own(start, stop, field, edge, matrices, emit):
    lane = lax.broadcasted_iota(jnp.int32, (ROWS, LANES), 1)
    count = 2 * UNROLL_PAIRS

    def step(i, carry):
        for u in range(count):
            c = i * count + u
            emit(c, dot(matrices[c][:, :112], shifted(field[c], edge[c], lane)))
        return carry

    lax.fori_loop(start, stop, step, 0)


def convolve_beyond(halo, halo_edge, matrices, emit):
    lane = lax.broadcasted_iota(jnp.int32, (ROWS, LANES), 1)

    def step(i, carry):
        for u in range(UNROLL_PAIRS):
            q = i * UNROLL_PAIRS + u
            both = matrices[pl.ds(2 * q, 2)].reshape(2 * ROWS, 256)
            emit(q, dot(both[:, 128:240], shifted(halo[q], halo_edge[q], lane)))
        return carry

    lax.fori_loop(0, C // 2 // UNROLL_PAIRS, step, 0)


def kernel_sums(part, grad, field, edge, halo, halo_edge, mask, inner_sums, outer_sums):
    lane = lax.broadcasted_iota(jnp.int32, (ROWS, LANES), 1)
    pad = jnp.zeros((LANES - 112, LANES), BF16)

    def in_line(product, which):
        kept = jnp.where(mask[3 + which] > 0.0, product, 0.0)
        upper = pltpu.roll(kept[:8], 0, 1, stride=1, stride_axis=0)
        lower = pltpu.roll(kept[8:], 8, 1, stride=1, stride_axis=0)
        return jnp.sum(upper + lower, 0, keepdims=True)

    def step(i, carry):
        for u in range(UNROLL_PAIRS):
            q = i * UNROLL_PAIRS + u
            beyond = jnp.concatenate([shifted(halo[q], halo_edge[q], lane), pad], 0)
            both = grad[pl.ds(2 * q, 2)].reshape(2 * ROWS, LANES)
            outer = dot_lanes(both, beyond)
            for k in range(2):
                c = 2 * q + k
                own = jnp.concatenate([shifted(field[c], edge[c], lane), pad], 0)
                inner = dot_lanes(both[k * ROWS : (k + 1) * ROWS], own)
                inner_sums[pl.ds(c, 1), :] = in_line(inner, 0)
                outer_sums[k, pl.ds(q, 1), :] = in_line(outer[k * ROWS : (k + 1) * ROWS], 1 + k)
        return carry

    steps = C // 2 // UNROLL_PAIRS // 4
    lax.fori_loop(part * steps, (part + 1) * steps, step, 0)


class Sum:
    def __init__(self, sizes, stages, first, last, got, held, full, sems):
        self.sizes, self.ny, self.stages = sizes, sizes[1], stages
        self.place = my_place(self.ny)
        self.first, self.last, self.got, self.held, self.full = first, last, got, held, full
        self.send, self.recv, self.send_back, self.recv_back = sems
        self.base = [sum(group_size(sizes, axes) - 1 for axes, _ in stages[:i]) for i in range(len(stages))]
        self.backs = [i for i, (_, shared) in enumerate(stages) if shared]

    def others(self, axes):
        return enumerate(neighbours_of(self.place, self.sizes, axes))

    def index(self, place, axes):
        found = 0
        for axis in axes:
            found = found * self.sizes[axis] + place[axis]
        return found

    def source(self, stage):
        return self.first if stage == 0 else self.held[stage - 1]

    def start(self, stage):
        axes, shared = self.stages[stage]
        source = self.source(stage)
        tiles = self.held[stage].shape[0]
        self.copies = []
        for d, other in self.others(axes):
            self.copies.append(
                pltpu.make_async_remote_copy(
                    src_ref=source.at[pl.ds(self.index(other, axes) * tiles, tiles)] if shared else source,
                    dst_ref=self.got[stage].at[d],
                    send_sem=self.send.at[self.base[stage] + d],
                    recv_sem=self.recv.at[self.base[stage] + d],
                    device_id=device_at(*other, self.ny),
                    device_id_type=MESH,
                )
            )
        for copy in self.copies:
            copy.start()

    def finish(self, stage):
        for copy in self.copies:
            copy.wait()
        axes, shared = self.stages[stage]
        source, got, held = self.source(stage), self.got[stage], self.held[stage]
        tiles = held.shape[0]
        mine = self.index(self.place, axes) * tiles if shared else 0
        group = min(8, tiles)

        def add_up(i, carry):
            total = source[pl.ds(mine + i * group, group)].astype(F32)
            for d in range(group_size(self.sizes, axes) - 1):
                total = total + got[d, pl.ds(i * group, group)].astype(F32)
            held[pl.ds(i * group, group)] = total.astype(held.dtype)
            return carry

        lax.fori_loop(0, tiles // group, add_up, 0)

    def start_back(self, i):
        stage = self.backs[i]
        axes, _ = self.stages[stage]
        source = self.held[-1] if i == len(self.backs) - 1 else self.full[i]
        target = self.last if i == 0 else self.full[i - 1]
        tiles = source.shape[0]
        mine = self.index(self.place, axes) * tiles
        self.copies = []
        for d, other in self.others(axes):
            self.copies.append(
                pltpu.make_async_remote_copy(
                    src_ref=source,
                    dst_ref=target.at[pl.ds(mine, tiles)],
                    send_sem=self.send_back.at[self.base[stage] + d],
                    recv_sem=self.recv_back.at[self.base[stage] + d],
                    device_id=device_at(*other, self.ny),
                    device_id_type=MESH,
                )
            )
        for copy in self.copies:
            copy.start()
        group = min(8, tiles)

        def keep(i, carry):
            target[pl.ds(mine + i * group, group)] = source[pl.ds(i * group, group)]
            return carry

        lax.fori_loop(0, tiles // group, keep, 0)

    def finish_back(self, i):
        for copy in self.copies:
            copy.wait()


BIG_STAGES = (((0,), True), ((1, 2), True), ((3,), True))
SMALL_STAGES = (((0,), True), ((3,), True), ((1, 2), False))


def sum_scratch(sizes, stages, count, tile, dtype):
    got, held, full = [], [], []
    rest = count
    for axes, shared in stages:
        members = group_size(sizes, axes)
        rest = rest // members if shared else rest
        got.append(pltpu.VMEM((members - 1, rest) + tile, dtype))
        held.append(pltpu.VMEM((rest,) + tile, dtype))
        if shared:
            full.append(pltpu.VMEM((rest,) + tile, dtype))
    return [pltpu.VMEM((count,) + tile, dtype), pltpu.VMEM((count,) + tile, dtype)] + got + held + full[:-1]


def sum_sems(sizes):
    links = sum(group_size(sizes, axes) - 1 for axes, _ in BIG_STAGES)
    return [pltpu.SemaphoreType.DMA((links,)) for _ in range(4)]


TABLES = ("tap_spread", "edge_picker", "halo_placer", "lane_orders", "tap_gather", "valid_mask")


def make_tables():
    return (
        jnp.asarray(tap_spreads(), BF16),
        jnp.asarray(edge_picker(), BF16),
        jnp.asarray(halo_placer(), BF16),
        jnp.asarray(lane_orders(), BF16),
        jnp.asarray(tap_gather(), F32),
        jnp.asarray(valid_mask(), F32),
    )


def forward_block(rb, w1t, w2, s):
    first = rb * BLOCK_ROWS
    for j in range(BLOCK_ROWS):
        rows = pl.ds(first + j, C, stride=ROWS)
        sea = s["land"][pl.ds(first + j, 1), :]
        lanes = slice(j * LANES, (j + 1) * LANES)
        masked = sea * s["filt"][rows, :]
        average = jnp.sum(masked, 0, keepdims=True) * (1.0 / C)
        centred = masked - average
        inverse = lax.rsqrt(jnp.sum(centred * centred, 0, keepdims=True) * (1.0 / C) + epsilon)
        unit = centred * inverse
        s["inverse"][pl.ds(first + j, 1), :] = inverse
        s["unit"][first + j] = unit
        s["normed"][:, lanes] = (unit * s["gain"][...]).astype(BF16)
        s["scaled"][:, lanes] = (sea * s["scale"][...] * s["cot"][rows, :]).astype(BF16)
    for f in range(4):
        part = slice(f * 256, (f + 1) * 256)
        s["hidden"][f % 2] = dot(w1t[part, :], s["normed"][...])
        s["grad_act"][f % 2] = dot(w2[part, :], s["scaled"][...])
        for t in range(16):
            hidden = s["hidden"][f % 2, t * 16 : (t + 1) * 16, :]
            grad_act = s["grad_act"][f % 2, t * 16 : (t + 1) * 16, :]
            lower, bell = halves(hidden)
            rows = slice(f * 256 + t * 16, f * 256 + (t + 1) * 16)
            s["activated"][rb, rows, :] = (hidden * lower).astype(BF16)
            s["grad_hidden"][rb, rows, :] = (grad_act * (lower + hidden * bell * 0.3989422804014327)).astype(BF16)
    s["reduce_sum"][...] += dot_lanes(s["activated"][rb], s["scaled"][...])
    s["expand_sum"][...] += dot_lanes(s["normed"][...], s["grad_hidden"][rb])


def backward_block(rb, w1, w2t, s):
    first = rb * BLOCK_ROWS
    s["branch"][...] = dot(w2t[...], s["activated"][rb])
    s["grad_norm"][...] = dot(w1[...], s["grad_hidden"][rb])
    for j in range(BLOCK_ROWS):
        rows = pl.ds(first + j, C, stride=ROWS)
        sea = s["land"][pl.ds(first + j, 1), :]
        lanes = slice(j * LANES, (j + 1) * LANES)
        branch = sea * s["branch"][:, lanes]
        grad_norm = s["grad_norm"][:, lanes]
        unit = s["unit"][first + j]
        s["scale_sum"][...] += s["cot"][rows, :] * branch
        s["added"][rows, :] = s["scale"][...] * branch
        s["gain_sum"][...] += grad_norm * unit
        grad_hat = grad_norm * s["gain"][...]
        mean = jnp.sum(grad_hat, 0, keepdims=True) * (1.0 / C)
        mean_unit = jnp.sum(grad_hat * unit, 0, keepdims=True) * (1.0 / C)
        grad = (sea * s["inverse"][pl.ds(first + j, 1), :]) * (grad_hat - mean - unit * mean_unit)
        s["grad_wide"][0, rows, :] = grad
        s["grad_wide"][1, pl.ds(ROWS - 1 - first - j, C, stride=ROWS), :] = grad
        s["grad_rows"][first + j] = grad.astype(BF16)


COMPUTE = {
    "land": ((ROWS, LANES), F32),
    "gain": ((C, LANES), F32),
    "scale": ((C, LANES), F32),
    "taps": ((C, LANES), F32),
    "lines": ((2, C, LANES), F32),
    "tap_rows": ((LANES, C), F32),
    "w1t": ((FF, C), BF16),
    "w2t": ((C, FF), BF16),
    "matrices": ((C, ROWS, 256), BF16),
    "back_matrices": ((C, ROWS, 256), BF16),
    "filt": ((C * ROWS, LANES), F32),
    "cot": ((C * ROWS, LANES), F32),
    "inverse": ((ROWS, LANES), F32),
    "unit": ((ROWS, C, LANES), F32),
    "normed": ((C, BLOCK), BF16),
    "scaled": ((C, BLOCK), BF16),
    "hidden": ((2, 256, BLOCK), F32),
    "grad_act": ((2, 256, BLOCK), F32),
    "activated": ((ROWS // BLOCK_ROWS, FF, BLOCK), BF16),
    "grad_hidden": ((ROWS // BLOCK_ROWS, FF, BLOCK), BF16),
    "branch": ((C, BLOCK), F32),
    "grad_norm": ((C, BLOCK), F32),
    "reduce_sum": ((FF, C), F32),
    "expand_sum": ((C, FF), F32),
    "added": ((C * ROWS, LANES), F32),
    "grad_wide": ((2, C * ROWS, LANES), F32),
    "grad": ((C, ROWS, LANES), BF16),
    "grad_rows": ((ROWS, C, LANES), BF16),
    "edge_rows": ((2, 3, C, LANES), BF16),
    "turned_grad": ((C, ROWS, LANES), BF16),
    "scale_sum": ((C, LANES), F32),
    "gain_sum": ((C, LANES), F32),
    "inner_sums": ((C, LANES), F32),
    "outer_sums": ((2, C // 2, LANES), F32),
}


def prepare(land, depth_kernel, gain, scale, w1, w2, cotangent, s):
    s["land"][...] = land[...].astype(F32)
    for vector, name in ((gain, "gain"), (scale, "scale")):
        for h in range(2):
            row = vector[pl.ds(h, 1), :]
            s[name][h * LANES : (h + 1) * LANES, :] = jnp.broadcast_to(row, (LANES, LANES)).T
    for f in range(4):
        part = slice(f * 256, (f + 1) * 256)
        s["w1t"][part, :] = w1[:, part].T
        s["w2t"][:, part] = w2[part, :].T

    def widen(g, carry):
        rows = pl.ds(pl.multiple_of(g * 256, 256), 256)
        s["cot"][rows, :] = cotangent[pl.ds(g * 16, 16)].reshape(256, LANES).astype(F32)
        return carry

    lax.fori_loop(0, GROUPS, widen, 0)
    for name in ("reduce_sum", "expand_sum", "scale_sum", "gain_sum"):
        s[name][...] = jnp.zeros_like(s[name])


def place_taps(depth_kernel, s):
    taps = depth_kernel[...].astype(F32)
    even = lax.broadcasted_iota(jnp.int32, taps.shape, 1) % 2 == 0
    s["tap_rows"][...] = jnp.zeros_like(s["tap_rows"])
    s["tap_rows"][:49, :] = jnp.where(even, taps, 0.0)
    s["tap_rows"][64 : 64 + 49, :] = jnp.where(even, 0.0, taps)
    s["taps"][...] = s["tap_rows"][...].T


def block_kernel(sizes, state, land, depth_kernel, gain, scale, w1, w2, cotangent, *rest):
    tables = dict(zip(TABLES, rest[: len(TABLES)]))
    rest = list(rest[len(TABLES) :])
    updated, state_grad, big_last, small_out = rest[:4]
    rest = rest[4:]

    def take(n):
        out = rest[:n]
        del rest[:n]
        return out

    s = dict(zip(COMPUTE, take(len(COMPUTE))))
    ahead_refs = take(len(halo_scratch()))
    back_refs = take(len(halo_scratch()))
    edge_rows, grad_rows = s["edge_rows"], s["grad_rows"]
    ahead = Halo(state, (edge_rows.at[0], edge_rows.at[1]), tables, *ahead_refs, sems=take(2))
    back = Halo(
        s["grad"], (grad_rows.at[pl.ds(0, 3)], grad_rows.at[pl.ds(ROWS - 3, 3)]), tables, *back_refs, sems=take(2)
    )
    stages = len(BIG_STAGES)
    (big_first,) = take(1)
    big = Sum(sizes, BIG_STAGES, big_first, big_last, take(stages), take(stages), take(2), take(4))
    small_first, small_last = take(2)
    small = Sum(sizes, SMALL_STAGES, small_first, small_last, take(stages), take(stages), take(1), take(4))

    barrier = pltpu.get_barrier_semaphore()
    greeted = [ahead.up, ahead.left, ahead.right]
    for axes, _ in BIG_STAGES:
        greeted += [device_at(*other, sizes[1]) for _, other in big.others(axes)]
    for device in greeted:
        pl.semaphore_signal(barrier, inc=1, device_id=device, device_id_type=MESH)

    @pl.when(ahead.lat > 0)
    def _():
        pl.semaphore_signal(barrier, inc=1, device_id=ahead.down, device_id_type=MESH)

    ahead.pack_rows()
    pl.semaphore_wait(barrier, len(greeted) + jnp.where(ahead.lat > 0, 1, 0))
    ahead.send_rows()
    ahead.pack_columns()
    ahead.send_columns()
    place_taps(depth_kernel, s)
    build_row_matrices(0, s["taps"], tables["tap_spread"], tables["valid_mask"], s["lines"], s["matrices"])
    prepare(land, depth_kernel, gain, scale, w1, w2, cotangent, s)
    ahead.columns()

    def put_filtered(c, value):
        s["filt"][pl.ds(pl.multiple_of(c * ROWS, ROWS), ROWS), :] = value

    own_steps = C // 2 // UNROLL_PAIRS
    convolve_own(0, own_steps, state, ahead.edge, s["matrices"], put_filtered)

    def add_filtered(q, value):
        rows = pl.ds(pl.multiple_of(q * 2 * ROWS, 2 * ROWS), 2 * ROWS)
        s["filt"][rows, :] += value

    def ahead_step(step, carry):
        @pl.when(step == 1)
        def _():
            ahead.rows()
            convolve_beyond(ahead.halo, ahead.halo_edge, s["matrices"], add_filtered)

        forward_block(step + 1 - 2 * (step % 2), s["w1t"], w2, s)
        return carry

    lax.fori_loop(0, ROWS // BLOCK_ROWS, ahead_step, 0)

    def cut_expand(g, carry):
        rows = pl.ds(pl.multiple_of(g * 16, 16), 16)
        for h in range(8):
            big_first[g * 8 + h] = s["expand_sum"][rows, h * LANES : (h + 1) * LANES].astype(BF16)
        return carry

    lax.fori_loop(0, C // 16, cut_expand, 0)

    def cut_reduce(g, carry):
        rows = pl.ds(pl.multiple_of(g * 16, 16), 16)
        for h in range(2):
            big_first[128 + g * 2 + h] = s["reduce_sum"][rows, h * LANES : (h + 1) * LANES].astype(BF16)
        return carry

    lax.fori_loop(0, FF // 16, cut_reduce, 0)
    big.start(0)
    build_row_matrices(
        back.below + 1, s["taps"], tables["tap_spread"], tables["valid_mask"], s["lines"], s["back_matrices"]
    )
    big.finish(0)
    big.start(1)

    def back_step(step, carry):
        @pl.when(step == 2)
        def _():
            back.send_rows()

        backward_block(jnp.where(step < 2, 3 * step, step - 1), w1, s["w2t"], s)
        return carry

    lax.fori_loop(0, ROWS // BLOCK_ROWS, back_step, 0)

    def settle(g, carry):
        rows = pl.ds(pl.multiple_of(g * 128, 128), 128)
        channels = pl.ds(g * 8, 8)
        s["grad"][channels] = s["grad_wide"][0, rows, :].astype(BF16).reshape(8, ROWS, LANES)
        s["turned_grad"][channels] = s["grad_wide"][1, rows, :].astype(BF16).reshape(8, ROWS, LANES)
        updated[channels] = (
            (state[channels].reshape(128, LANES).astype(F32) + s["added"][rows, :]).astype(BF16).reshape(8, ROWS, LANES)
        )
        return carry

    lax.fori_loop(0, C // 8, settle, 0)
    back.pack_columns()
    back.send_columns()

    def sums(part):
        kernel_sums(
            part, s["turned_grad"], state, ahead.edge, ahead.halo, ahead.halo_edge, tables["valid_mask"],
            s["inner_sums"], s["outer_sums"],
        )

    sums(0)
    big.finish(1)
    big.start(2)
    sums(1)
    sums(2)
    big.finish(2)
    big.start_back(2)
    sums(3)

    exact = lax.Precision.HIGHEST
    gather = tables["tap_gather"]
    pair = lax.broadcasted_iota(jnp.int32, (C // 2, C), 0)
    channel = lax.broadcasted_iota(jnp.int32, (C // 2, C), 1)
    total = dot_lanes(gather[0], s["inner_sums"][...], exact)
    for h in range(2):
        part = dot_lanes(gather[1 + h], s["outer_sums"][h], exact)
        spread = jnp.where(channel == 2 * pair + h, 1.0, 0.0)
        total = total + jnp.dot(part, spread, preferred_element_type=F32, precision=exact)
    row = lax.broadcasted_iota(jnp.int32, (64, LANES), 0)
    total = total + dot_lanes(jnp.where(row == 49, 1.0, 0.0), s["gain_sum"][...], exact)
    total = total + dot_lanes(jnp.where(row == 50, 1.0, 0.0), s["scale_sum"][...], exact)
    for g in range(8):
        for h in range(2):
            small_first[g * 2 + h] = total[g * 8 : (g + 1) * 8, h * LANES : (h + 1) * LANES]
    small.start(0)
    back.columns()
    small.finish(0)
    small.start(1)
    big.finish_back(2)
    big.start_back(1)

    def put_part(c, value):
        s["added"][pl.ds(pl.multiple_of(c * ROWS, ROWS), ROWS), :] = value

    def put_grad(q, value):
        rows = pl.ds(pl.multiple_of(q * 2 * ROWS, 2 * ROWS), 2 * ROWS)
        total = s["cot"][rows, :] + s["added"][rows, :] + value
        state_grad[pl.ds(q * 2, 2)] = total.astype(BF16).reshape(2, ROWS, LANES)

    convolve_own(0, own_steps, s["grad"], back.edge, s["back_matrices"], put_part)
    small.finish(1)
    small.start(2)
    back.rows()
    small.finish(2)
    small.start_back(1)
    convolve_beyond(back.halo, back.halo_edge, s["back_matrices"], put_grad)
    big.finish_back(1)
    big.start_back(0)
    small.finish_back(1)
    small.start_back(0)
    small.finish_back(0)
    for g in range(8):
        for h in range(2):
            small_out[g * 8 : (g + 1) * 8, h * LANES : (h + 1) * LANES] = small_last[g * 2 + h]
    big.finish_back(0)


def hand_over(factor, big, small, *outs):
    kernel_out, gain_out, expand_out, reduce_out, scale_out = outs

    def paste_expand(g, carry):
        rows = pl.ds(pl.multiple_of(g * 16, 16), 16)
        for h in range(8):
            expand_out[rows, h * LANES : (h + 1) * LANES] = big[g * 8 + h].astype(F32) * factor
        return carry

    lax.fori_loop(0, C // 16, paste_expand, 0)

    def paste_reduce(g, carry):
        rows = pl.ds(pl.multiple_of(g * 16, 16), 16)
        for h in range(2):
            reduce_out[rows, h * LANES : (h + 1) * LANES] = big[128 + g * 2 + h].astype(F32) * factor
        return carry

    lax.fori_loop(0, FF // 16, paste_reduce, 0)
    kernel_out[...] = small[:49, :] * factor
    gain_out[...] = small[49:50, :] * factor
    scale_out[...] = small[50:51, :] * factor


def local(state, land, depth_kernel, norm_gain, expand_weight, reduce_weight, layer_scale, cotangent):
    ny, nz = lax.axis_size("lon") // 4, lax.axis_size("lat") // 2
    sizes = (2, ny, 4, nz)
    operands = (
        state, land, depth_kernel.T, norm_gain.reshape(2, LANES), layer_scale.reshape(2, LANES), expand_weight,
        reduce_weight, cotangent, *make_tables(),
    )
    vmem = pl.BlockSpec(memory_space=pltpu.VMEM)
    field = jax.ShapeDtypeStruct((C, ROWS, LANES), BF16)
    out_shape = (
        field,
        field,
        jax.ShapeDtypeStruct((256, 16, LANES), BF16),
        jax.ShapeDtypeStruct((64, C), F32),
    )
    halo_sems = [pltpu.SemaphoreType.DMA((6,)) for _ in range(4)]
    updated, state_grad, *parts = pl.pallas_call(
        functools.partial(block_kernel, sizes),
        out_shape=out_shape,
        in_specs=[vmem] * len(operands),
        out_specs=[vmem] * len(out_shape),
        scratch_shapes=[pltpu.VMEM(shape, dtype) for shape, dtype in COMPUTE.values()]
        + halo_scratch()
        + halo_scratch()
        + halo_sems
        + sum_scratch(sizes, BIG_STAGES, 256, (16, LANES), BF16)[1:]
        + sum_sems(sizes)
        + sum_scratch(sizes, SMALL_STAGES, 16, (8, LANES), F32)
        + sum_sems(sizes),
        compiler_params=pltpu.CompilerParams(
            collective_id=0, has_side_effects=True, vmem_limit_bytes=63 * 2**20
        ),
        name="convnext_block",
    )(*operands)
    factor = float(ROWS * lax.axis_size("lat") * LANES * lax.axis_size("lon")) ** (-0.5)
    vector = jax.ShapeDtypeStruct((1, C), F32)
    kernel_grad, gain_grad, expand_grad, reduce_grad, scale_grad = pl.pallas_call(
        functools.partial(hand_over, factor),
        out_shape=(
            jax.ShapeDtypeStruct((49, C), F32), vector, jax.ShapeDtypeStruct((C, FF), F32),
            jax.ShapeDtypeStruct((FF, C), F32), vector,
        ),
        in_specs=[vmem] * 2,
        out_specs=[vmem] * 5,
        compiler_params=pltpu.CompilerParams(vmem_limit_bytes=24 * 2**20),
        name="hand_over",
    )(*parts)
    return updated, state_grad, kernel_grad.T, gain_grad.reshape(C), expand_grad, reduce_grad, scale_grad.reshape(C)


def solution(mesh):
    grid = P(None, "lat", "lon")
    return jax.shard_map(
        local,
        mesh=mesh,
        in_specs=(grid, P("lat", "lon"), P(), P(), P(), P(), P(), grid),
        out_specs=(grid, grid, P(), P(), P(), P(), P()),
        check_vma=False,
    )
```
